256 devices in a mesh: layer: 32 (over y, z), xs: 8 (over x, core).
Axes of the slice: x: 4, y: 4, z: 8, core: 2. Of those that a mesh axis runs over, the one named last changes fastest.
Arguments:
- probes: float32 [64, 32, 16, 640], P('layer', None, 'xs'), may hold values from -6 to 6
- potential: float32 [64, 16, 640], P('layer', 'xs'), may hold values from -1 to 1
- projector: bfloat16 [64, 512, 1280], P('layer', 'xs'), may hold values from -0.15625 to 0.15625
- intersection_ids: int32 [64, 512], P('layer', 'xs'), may hold values from 0 to 255
- strength: float32 [64, 256], P('layer'), may hold values from -2 to 2
- decay_rates: float32 [64, 32], P('layer'), may hold values from 0.3 to 1
- contour_nodes: float32 [4], replicated, may hold values from -1 to 3
- node_weights: float32 [4], replicated, may hold values from 0.5 to 1.5
Outputs:
- moments: float32 [2, 64, 32, 16, 640], P(None, 'layer', None, 'xs')
The draws below stay inside these ranges and needn't reach their ends.
All inputs are finite; a program needn't handle non-finite values.
Results may differ from the reference program's by a relative error of at most 0.00059.
Values sent between devices are 32-bit elements; how exact they have to be, the bound alone decides.
A program may use at most 64 MiB of HBM per device.

```python
import jax
import jax.numpy as jnp
from jax import lax

PROBE_COLUMNS = 32
K = 4
PZ = 640
NPL = 64
NPROJ = 256
LAYER_TOTAL = 64
PX = 16
SLOTS = 512
PTS = 1280


def draw_decay_rates(key, part):
    random_keys = jax.random.split(key, 6)
    share = 0.5
    fast = jax.random.uniform(random_keys[0], (PROBE_COLUMNS,)) < share
    slow_rate = jnp.log(0.1) * jax.random.uniform(random_keys[1], (PROBE_COLUMNS,), minval=0.3, maxval=1.0) / LAYER_TOTAL
    fast_rate = -4.6 / jax.random.uniform(random_keys[2], (PROBE_COLUMNS,), minval=30.0, maxval=50.0)
    baseline_term = jnp.where(fast, fast_rate, slow_rate)
    roughness_term = jnp.exp(jax.random.uniform(random_keys[3], (LAYER_TOTAL, PROBE_COLUMNS), minval=-0.7, maxval=0.7))
    sudden_spike = jax.random.uniform(random_keys[4], (LAYER_TOTAL, PROBE_COLUMNS)) < 0.04
    falloff_term = jax.random.uniform(random_keys[5], (LAYER_TOTAL, PROBE_COLUMNS), minval=0.6, maxval=0.8)
    value_entries = jnp.exp(baseline_term[None, :] * roughness_term) * jnp.where(sudden_spike, falloff_term, 1.0)
    return jnp.clip(value_entries, 0.3, 1.0).astype(jnp.float32)


def plant(drawn, key, least, top_value):
    dims = drawn.shape
    spot = [jax.random.randint(jax.random.fold_in(key, axis), (), 0, dims[axis]) for axis in range(len(dims))]
    drawn = drawn.at[tuple(spot)].set(least)
    longest = dims.index(max(dims))
    spot[longest] = (spot[longest] + 1) % dims[longest]
    return drawn.at[tuple(spot)].set(top_value)


def shard_levels(rng, dims, pieces, low, largest):
    loudness, own = 1.0, jax.random.fold_in(rng, 6)
    for dim, blocks in pieces:
        steps = jnp.exp(jax.random.uniform(jax.random.fold_in(own, dim), (blocks,), jnp.float32, low / len(pieces), largest / len(pieces)))
        loudness = loudness * jnp.repeat(steps, dims[dim] // blocks).reshape([-1 if axis == dim else 1 for axis in range(len(dims))])
    return loudness


def normal_values(own_key, extent, width, most, pieces=(), held_as=jnp.bfloat16):
    entries = width * jax.random.normal(own_key, extent, jnp.float32)
    if pieces:
        entries = entries * shard_levels(own_key, extent, pieces, -0.22, 0.18)
    return jnp.clip(entries, -most, most).astype(held_as)


def setup_inputs(seed: int = 0) -> dict:
    seeds = jax.random.split(jax.random.key(seed), 9)
    return {
        "probes": normal_values(seeds[0], (LAYER_TOTAL, PROBE_COLUMNS, PX, PZ), 1.0, 6.0, ((0, 32), (2, 8)), jnp.float32),
        "potential": jnp.clip(jax.random.uniform(seeds[1], (LAYER_TOTAL, PX, PZ), jnp.float32, -1.0, 1.0) * shard_levels(seeds[1], (LAYER_TOTAL, PX, PZ), ((0, 32), (1, 8)), -0.4, 0.0), -1.0, 1.0),
        "projector": normal_values(seeds[2], (LAYER_TOTAL, SLOTS, PTS), PTS ** -0.5, 0.15625, ((0, 32), (1, 8))),
        "intersection_ids": plant(jax.random.randint(seeds[3], (LAYER_TOTAL, SLOTS), 0, NPROJ), jax.random.fold_in(seeds[3], 1), 0, NPROJ - 1).astype(jnp.int32),
        "strength": jnp.clip(jax.random.uniform(seeds[4], (LAYER_TOTAL, NPROJ), jnp.float32, -2.0, 2.0) * shard_levels(seeds[4], (LAYER_TOTAL, NPROJ), ((0, 32),), -0.4, 0.0), -2.0, 2.0),
        "decay_rates": draw_decay_rates(jax.random.fold_in(seeds[8], 71), 0),
        "contour_nodes": jnp.clip(jax.random.uniform(seeds[6], (K,), jnp.float32, -1.0, 3.0), -1.0, 3.0),
        "node_weights": jnp.clip(jax.random.uniform(seeds[7], (K,), jnp.float32, 0.5, 1.5), 0.5, 1.5),
    }


FAR = -1.0 / 12.0
NEAR = 4.0 / 3.0
CENTER = -2.5


def second_along(padded, axis, count):
    def piece(offset):
        return lax.slice_in_dim(padded, 2 + offset, 2 + offset + count, axis=axis)
    return FAR * (piece(-2) + piece(2)) + NEAR * (piece(-1) + piece(1)) + CENTER * piece(0)


def reference(probes, potential, projector, intersection_ids, strength, decay_rates, contour_nodes, node_weights):
    hi = lax.Precision.HIGHEST
    layers, columns, rows, depth = probes.shape
    padded = jnp.pad(probes, ((2, 2), (0, 0), (2, 2), (2, 2)))
    laplace = second_along(padded[:, :, 2:-2, 2:-2], 0, layers)
    laplace = laplace + second_along(padded[2:-2, :, :, 2:-2], 2, rows)
    laplace = laplace + second_along(padded[2:-2, :, 2:-2, :], 3, depth)
    tiles = SLOTS // NPL
    rounded = probes.astype(jnp.bfloat16).astype(jnp.float32).reshape(layers, columns, tiles, PTS)
    proj_f = projector.astype(jnp.float32).reshape(layers, tiles, NPL, PTS)
    slot_coef = jnp.einsum("ltsp,lctp->ltsc", proj_f, rounded, precision=hi)
    onehot = (intersection_ids.reshape(layers, tiles, NPL)[..., None] == jnp.arange(NPROJ, dtype=jnp.int32)).astype(jnp.float32)
    coef = jnp.einsum("ltsq,ltsc->lqc", onehot, slot_coef, precision=hi)
    scaled = (strength[:, :, None] * coef).astype(jnp.bfloat16).astype(jnp.float32)
    slot_back = jnp.einsum("ltsq,lqc->ltsc", onehot, scaled, precision=hi)
    projected = jnp.einsum("ltsp,ltsc->lctp", proj_f, slot_back, precision=hi).reshape(layers, columns, rows, depth)
    hamil = -0.5 * laplace + potential[:, None] * probes + projected

    def forward_step(state, inputs):
        rate, source = inputs
        rate = rate[:, None, None]
        state = rate * state + (1.0 - rate) * source
        return state, state

    zero = jnp.zeros((columns, rows, depth), jnp.float32)
    first = jnp.zeros_like(probes)
    second = jnp.zeros_like(probes)
    for node in range(K):
        forcing = hamil - contour_nodes[node] * probes
        _, ahead = lax.scan(forward_step, zero, (decay_rates, forcing))
        _, back = lax.scan(forward_step, zero, (decay_rates, ahead), reverse=True)
        first = first + node_weights[node] * back
        second = second + node_weights[node] * contour_nodes[node] * back
    return jnp.stack([first, second])
```

```python
import jax
import jax.numpy as jnp
from jax import lax
from jax.sharding import PartitionSpec as P

NPROJ = 256


FAR = -1.0 / 12.0
NEAR = 4.0 / 3.0
CENTER = -2.5


def with_halo(cells, sides, width):
    for axis, dim in sides:
        count = lax.axis_size(axis)
        ends = count - 1
        head = lax.slice_in_dim(cells, 0, width, axis=dim)
        tail = lax.slice_in_dim(cells, cells.shape[dim] - width, cells.shape[dim], axis=dim)
        cells = jnp.concatenate(
            [
                lax.ppermute(tail, axis, [(i, (i + 1) % count) for i in range(ends)]),
                cells,
                lax.ppermute(head, axis, [((i + 1) % count, i) for i in range(ends)]),
            ],
            axis=dim,
        )
    return cells


def second_along(padded, axis, count):

    def piece(offset):
        return lax.slice_in_dim(padded, 2 + offset, 2 + offset + count, axis=axis)

    return FAR * (piece(-2) + piece(2)) + NEAR * (piece(-1) + piece(1)) + CENTER * piece(0)


def shifted(tree, axis, step, reverse):
    count = lax.axis_size(axis)
    if reverse:
        pairs = [(i + step, i) for i in range(count - step)]
    else:
        pairs = [(i, i + step) for i in range(count - step)]
    return lax.ppermute(tree, axis, pairs)


def carried(through, end, axis, reverse):
    count = lax.axis_size(axis)
    span = 1
    t, a = through, end
    while 2 * span < count:
        tr, ar = shifted((t, a), axis, span, reverse)
        a = a + t[None, :, None, None] * ar
        t = t * tr
        span *= 2
    near_t, near_a = shifted((t, a), axis, 1, reverse)
    if span + 1 < count:
        far_a = shifted(a, axis, span + 1, reverse)
        return near_a + near_t[None, :, None, None] * far_a
    return near_a


def sweeps(forcing, decay_rates):
    count = forcing.shape[1]
    rates = decay_rates[None, :, :, None, None]
    keep = 1.0 - rates
    state = jnp.zeros_like(forcing[:, 0])
    ahead_list = []
    for index in range(count):
        state = rates[:, index] * state + keep[:, index] * forcing[:, index]
        ahead_list.append(state)
    through = jnp.prod(decay_rates, axis=0)
    entering = carried(through, state, "layer", False)
    lower = jnp.cumprod(decay_rates, axis=0)
    ahead = [ahead_list[i] + lower[i][None, :, None, None] * entering for i in range(count)]
    state = jnp.zeros_like(forcing[:, 0])
    back_list = [None] * count
    for index in reversed(range(count)):
        state = rates[:, index] * state + keep[:, index] * ahead[index]
        back_list[index] = state
    from_above = carried(through, state, "layer", True)
    upper = jnp.cumprod(decay_rates[::-1], axis=0)[::-1]
    return jnp.stack(
        [back_list[i] + upper[i][None, :, None, None] * from_above for i in range(count)], axis=1
    )


def plane_sum(x, axis):
    count = lax.axis_size(axis)
    step = 1
    while step < count:
        x = x + lax.ppermute(x, axis, [(i, i ^ step) for i in range(count)])
        step *= 2
    return x


def shards(
    probes,
    potential,
    projector,
    intersection_ids,
    strength,
    decay_rates,
    contour_nodes,
    node_weights,
):
    layers, columns, rows, depth = probes.shape
    padded = with_halo(probes, (("layer", 0), ("xs", 2)), 2)
    across = jnp.pad(probes, ((0, 0), (0, 0), (0, 0), (2, 2)))
    laplace = second_along(padded[:, :, 2:-2, :], 0, layers)
    laplace = laplace + second_along(padded[2:-2], 2, rows)
    laplace = laplace + second_along(across, 3, depth)
    rounded = probes.astype(jnp.bfloat16).reshape(layers, columns, rows * depth)
    slot_coef = jnp.einsum("lsp,lcp->lsc", projector, rounded, preferred_element_type=jnp.float32)
    onehot = (intersection_ids[:, :, None] == jnp.arange(NPROJ, dtype=jnp.int32)).astype(
        jnp.float32
    )
    partial_coef = jnp.einsum("lsq,lsc->lqc", onehot, slot_coef, precision=lax.Precision.HIGHEST)
    coef = plane_sum(partial_coef, "xs")
    scaled = (strength[:, :, None] * coef).astype(jnp.bfloat16)
    slot_back = jnp.einsum(
        "lsq,lqc->lsc", onehot.astype(jnp.bfloat16), scaled, preferred_element_type=jnp.float32
    ).astype(jnp.bfloat16)
    projected = jnp.einsum(
        "lsp,lsc->lcp", projector, slot_back, preferred_element_type=jnp.float32
    ).reshape(layers, columns, rows, depth)
    hamil = -0.5 * laplace + potential[:, None] * probes + projected
    w0 = jnp.sum(node_weights)
    w1 = jnp.sum(node_weights * contour_nodes)
    w2 = jnp.sum(node_weights * contour_nodes * contour_nodes)
    forcing = jnp.stack([w0 * hamil - w1 * probes, w1 * hamil - w2 * probes])
    return sweeps(forcing, decay_rates)


def solution(mesh):
    in_specs = (
        P("layer", None, "xs", None),
        P("layer", "xs", None),
        P("layer", "xs", None),
        P("layer", "xs"),
        P("layer", None),
        P("layer", None),
        P(),
        P(),
    )
    out_specs = P(None, "layer", None, "xs", None)
    return jax.shard_map(shards, mesh=mesh, in_specs=in_specs, out_specs=out_specs, check_vma=False)
```

```python
import functools

import jax
import jax.numpy as jnp
from jax import lax
from jax.experimental import pallas as pl
from jax.experimental.pallas import tpu as pltpu
from jax.sharding import PartitionSpec as P

NPROJ = 256


FAR = -1.0 / 12.0
NEAR = 4.0 / 3.0
CENTER = -2.5


def with_halo(cells, sides, width):
    for axis, dim in sides:
        count = lax.axis_size(axis)
        ends = count - 1
        head = lax.slice_in_dim(cells, 0, width, axis=dim)
        tail = lax.slice_in_dim(cells, cells.shape[dim] - width, cells.shape[dim], axis=dim)
        cells = jnp.concatenate(
            [
                lax.ppermute(tail, axis, [(i, (i + 1) % count) for i in range(ends)]),
                cells,
                lax.ppermute(head, axis, [((i + 1) % count, i) for i in range(ends)]),
            ],
            axis=dim,
        )
    return cells


def second_along(padded, axis, count):

    def piece(offset):
        return lax.slice_in_dim(padded, 2 + offset, 2 + offset + count, axis=axis)

    return FAR * (piece(-2) + piece(2)) + NEAR * (piece(-1) + piece(1)) + CENTER * piece(0)


MESH = pl.DeviceIdType.MESH


def spans_of(count):
    spans = []
    span = 1
    while 2 * span < count:
        spans.append(span)
        span *= 2
    return spans, span + 1


def sweep_kernel(count, f_ref, d_ref, o_ref, state, landed, send_sem, recv_sem):
    me = lax.axis_index("layer")
    row = lax.axis_index("xs")
    layers = f_ref.shape[1]
    width = f_ref.shape[3]
    spans, far = spans_of(count)
    hops = spans + [1, far]
    barrier = pltpu.get_barrier_semaphore()
    for hop in hops:
        for sign in (1, -1):
            pl.semaphore_signal(
                barrier, inc=1, device_id=(lax.rem(me + sign * hop + count, count), row),
                device_id_type=MESH,
            )
    pl.semaphore_wait(barrier, 2 * len(hops))

    rates = [d_ref[index] for index in range(layers)]
    through = rates[0]
    for index in range(1, layers):
        through = through * rates[index]

    def put(direction, slot, ends, keep):
        state[direction, slot, :, :, :width] = ends
        state[direction, slot, :, :, width:] = jnp.broadcast_to(keep[None], (2,) + keep.shape[:1] + (128,))

    def send(direction, slot, target_slot, hop, sign):
        copy = pltpu.make_async_remote_copy(
            src_ref=state.at[direction, slot],
            dst_ref=landed.at[direction, target_slot],
            send_sem=send_sem.at[direction, target_slot],
            recv_sem=recv_sem.at[direction, target_slot],
            device_id=(lax.rem(me + sign * hop + count, count), row),
            device_id_type=MESH,
        )
        copy.start()
        return copy

    def scan(direction, ends, sign):
        put(direction, 0, ends, through)
        for slot, hop in enumerate(spans):
            send(direction, slot, slot, hop, sign).wait()
            source = me - hop if sign == 1 else me + hop
            valid = ((source >= 0) & (source < count)).astype(jnp.float32)
            mine = state[direction, slot]
            got = landed[direction, slot]
            keep = mine[0, :, width:width + 1]
            put(
                direction, slot + 1,
                mine[:, :, :width] + (valid * keep)[None] * got[:, :, :width],
                keep * (valid * got[0, :, width:width + 1]),
            )
        last = len(spans)
        near = send(direction, last, last, 1, sign)
        distant = send(direction, last, last + 1, far, sign)
        near.wait()
        distant.wait()
        near_source = me - 1 if sign == 1 else me + 1
        far_source = me - far if sign == 1 else me + far
        near_valid = ((near_source >= 0) & (near_source < count)).astype(jnp.float32)
        far_valid = ((far_source >= 0) & (far_source < count)).astype(jnp.float32)
        got = landed[direction, last]
        result = got[:, :, :width]
        if far < count:
            result = result + (far_valid * got[0, :, width:width + 1])[None] * landed[direction, last + 1, :, :, :width]
        return near_valid * result

    state_now = None
    ahead = []
    for index in range(layers):
        source = f_ref[:, index]
        if state_now is None:
            state_now = (1.0 - rates[index])[None] * source
        else:
            state_now = rates[index][None] * state_now + (1.0 - rates[index])[None] * source
        ahead.append(state_now)
    entering = scan(0, state_now, 1)
    lower = rates[0]
    for index in range(layers):
        if index > 0:
            lower = lower * rates[index]
        ahead[index] = ahead[index] + lower[None] * entering
    state_now = None
    back = [None] * layers
    for index in reversed(range(layers)):
        if state_now is None:
            state_now = (1.0 - rates[index])[None] * ahead[index]
        else:
            state_now = rates[index][None] * state_now + (1.0 - rates[index])[None] * ahead[index]
        back[index] = state_now
    from_above = scan(1, state_now, -1)
    upper = rates[layers - 1]
    for index in reversed(range(layers)):
        if index < layers - 1:
            upper = upper * rates[index]
        o_ref[:, index] = back[index] + upper[None] * from_above


def sweeps(forcing, decay_rates):
    moments, layers, columns, rows, depth = forcing.shape
    width = rows * depth
    count = lax.axis_size("layer")
    spans, _ = spans_of(count)
    rounds = len(spans) + 2
    flat = forcing.reshape(moments, layers, columns, width)
    out = pl.pallas_call(
        functools.partial(sweep_kernel, count),
        out_shape=jax.ShapeDtypeStruct(flat.shape, jnp.float32),
        in_specs=[pl.BlockSpec(memory_space=pltpu.VMEM)] * 2,
        out_specs=pl.BlockSpec(memory_space=pltpu.VMEM),
        scratch_shapes=[
            pltpu.VMEM((2, rounds, moments, columns, width + 128), jnp.float32),
            pltpu.VMEM((2, rounds, moments, columns, width + 128), jnp.float32),
            pltpu.SemaphoreType.DMA((2, rounds)),
            pltpu.SemaphoreType.DMA((2, rounds)),
        ],
        compiler_params=pltpu.CompilerParams(collective_id=0, has_side_effects=True),
    )(flat, decay_rates[:, :, None])
    return out.reshape(forcing.shape)


def plane_sum(x, axis):
    count = lax.axis_size(axis)
    step = 1
    while step < count:
        x = x + lax.ppermute(x, axis, [(i, i ^ step) for i in range(count)])
        step *= 2
    return x


def shards(
    probes,
    potential,
    projector,
    intersection_ids,
    strength,
    decay_rates,
    contour_nodes,
    node_weights,
):
    layers, columns, rows, depth = probes.shape
    padded = with_halo(probes, (("layer", 0), ("xs", 2)), 2)
    across = jnp.pad(probes, ((0, 0), (0, 0), (0, 0), (2, 2)))
    laplace = second_along(padded[:, :, 2:-2, :], 0, layers)
    laplace = laplace + second_along(padded[2:-2], 2, rows)
    laplace = laplace + second_along(across, 3, depth)
    rounded = probes.astype(jnp.bfloat16).reshape(layers, columns, rows * depth)
    slot_coef = jnp.einsum("lsp,lcp->lsc", projector, rounded, preferred_element_type=jnp.float32)
    onehot = (intersection_ids[:, :, None] == jnp.arange(NPROJ, dtype=jnp.int32)).astype(
        jnp.float32
    )
    partial_coef = jnp.einsum("lsq,lsc->lqc", onehot, slot_coef, precision=lax.Precision.HIGHEST)
    coef = plane_sum(partial_coef, "xs")
    scaled = (strength[:, :, None] * coef).astype(jnp.bfloat16)
    slot_back = jnp.einsum(
        "lsq,lqc->lsc", onehot.astype(jnp.bfloat16), scaled, preferred_element_type=jnp.float32
    ).astype(jnp.bfloat16)
    projected = jnp.einsum(
        "lsp,lsc->lcp", projector, slot_back, preferred_element_type=jnp.float32
    ).reshape(layers, columns, rows, depth)
    hamil = -0.5 * laplace + potential[:, None] * probes + projected
    w0 = jnp.sum(node_weights)
    w1 = jnp.sum(node_weights * contour_nodes)
    w2 = jnp.sum(node_weights * contour_nodes * contour_nodes)
    forcing = jnp.stack([w0 * hamil - w1 * probes, w1 * hamil - w2 * probes])
    return sweeps(forcing, decay_rates)


def solution(mesh):
    in_specs = (
        P("layer", None, "xs", None),
        P("layer", "xs", None),
        P("layer", "xs", None),
        P("layer", "xs"),
        P("layer", None),
        P("layer", None),
        P(),
        P(),
    )
    out_specs = P(None, "layer", None, "xs", None)
    return jax.shard_map(shards, mesh=mesh, in_specs=in_specs, out_specs=out_specs, check_vma=False)
```

```python
import functools

import jax
import jax.numpy as jnp
from jax import lax
from jax.experimental import pallas as pl
from jax.experimental.pallas import tpu as pltpu
from jax.sharding import PartitionSpec as P

NPROJ = 256


FAR = -1.0 / 12.0
NEAR = 4.0 / 3.0
CENTER = -2.5


def with_halo(cells, sides, width):
    for axis, dim in sides:
        count = lax.axis_size(axis)
        ends = count - 1
        head = lax.slice_in_dim(cells, 0, width, axis=dim)
        tail = lax.slice_in_dim(cells, cells.shape[dim] - width, cells.shape[dim], axis=dim)
        cells = jnp.concatenate(
            [
                lax.ppermute(tail, axis, [(i, (i + 1) % count) for i in range(ends)]),
                cells,
                lax.ppermute(head, axis, [((i + 1) % count, i) for i in range(ends)]),
            ],
            axis=dim,
        )
    return cells


def second_along(padded, axis, count):

    def piece(offset):
        return lax.slice_in_dim(padded, 2 + offset, 2 + offset + count, axis=axis)

    return FAR * (piece(-2) + piece(2)) + NEAR * (piece(-1) + piece(1)) + CENTER * piece(0)


MESH = pl.DeviceIdType.MESH


def spans_of(count):
    spans = []
    span = 1
    while 2 * span < count:
        spans.append(span)
        span *= 2
    return spans, span + 1


def sweep_kernel(count, f_ref, d_ref, o_ref, state, landed, send_sem, recv_sem):
    me = lax.axis_index("layer")
    row = lax.axis_index("xs")
    layers = f_ref.shape[1]
    width = f_ref.shape[3]
    spans, far = spans_of(count)
    hops = spans + [1, far]
    barrier = pltpu.get_barrier_semaphore()
    for hop in hops:
        for sign in (1, -1):
            pl.semaphore_signal(
                barrier, inc=1, device_id=(lax.rem(me + sign * hop + count, count), row),
                device_id_type=MESH,
            )
    pl.semaphore_wait(barrier, 2 * len(hops))

    rates = [d_ref[index] for index in range(layers)]
    through = rates[0]
    for index in range(1, layers):
        through = through * rates[index]

    def put(direction, slot, ends, keep):
        state[direction, slot, :, :, :width] = ends
        state[direction, slot, :, :, width:] = jnp.broadcast_to(keep[None], (2,) + keep.shape[:1] + (128,))

    def send(direction, slot, target_slot, hop, sign):
        copy = pltpu.make_async_remote_copy(
            src_ref=state.at[direction, slot],
            dst_ref=landed.at[direction, target_slot],
            send_sem=send_sem.at[direction, target_slot],
            recv_sem=recv_sem.at[direction, target_slot],
            device_id=(lax.rem(me + sign * hop + count, count), row),
            device_id_type=MESH,
        )
        copy.start()
        return copy

    def scan(direction, ends, sign):
        put(direction, 0, ends, through)
        for slot, hop in enumerate(spans):
            send(direction, slot, slot, hop, sign).wait()
            source = me - hop if sign == 1 else me + hop
            valid = ((source >= 0) & (source < count)).astype(jnp.float32)
            mine = state[direction, slot]
            got = landed[direction, slot]
            keep = mine[0, :, width:width + 1]
            put(
                direction, slot + 1,
                mine[:, :, :width] + (valid * keep)[None] * got[:, :, :width],
                keep * (valid * got[0, :, width:width + 1]),
            )
        last = len(spans)
        near = send(direction, last, last, 1, sign)
        distant = send(direction, last, last + 1, far, sign)
        near.wait()
        distant.wait()
        near_source = me - 1 if sign == 1 else me + 1
        far_source = me - far if sign == 1 else me + far
        near_valid = ((near_source >= 0) & (near_source < count)).astype(jnp.float32)
        far_valid = ((far_source >= 0) & (far_source < count)).astype(jnp.float32)
        got = landed[direction, last]
        result = got[:, :, :width]
        if far < count:
            result = result + (far_valid * got[0, :, width:width + 1])[None] * landed[direction, last + 1, :, :, :width]
        return near_valid * result

    state_now = None
    ahead = []
    for index in range(layers):
        source = f_ref[:, index]
        if state_now is None:
            state_now = (1.0 - rates[index])[None] * source
        else:
            state_now = rates[index][None] * state_now + (1.0 - rates[index])[None] * source
        ahead.append(state_now)
    entering = scan(0, state_now, 1)
    lower = rates[0]
    for index in range(layers):
        if index > 0:
            lower = lower * rates[index]
        ahead[index] = ahead[index] + lower[None] * entering
    state_now = None
    back = [None] * layers
    for index in reversed(range(layers)):
        if state_now is None:
            state_now = (1.0 - rates[index])[None] * ahead[index]
        else:
            state_now = rates[index][None] * state_now + (1.0 - rates[index])[None] * ahead[index]
        back[index] = state_now
    from_above = scan(1, state_now, -1)
    upper = rates[layers - 1]
    for index in reversed(range(layers)):
        if index < layers - 1:
            upper = upper * rates[index]
        o_ref[:, index] = back[index] + upper[None] * from_above


def sweeps(forcing, decay_rates):
    moments, layers, columns, rows, depth = forcing.shape
    flat = forcing.reshape(moments, layers, columns, rows * depth)
    whole = lax.all_to_all(flat, "layer", 2, 1, tiled=True)
    rates = lax.all_to_all(decay_rates, "layer", 1, 0, tiled=True)
    total = whole.shape[1]
    rate = rates[:, None, :, None]
    keep = 1.0 - rate
    state = jnp.zeros_like(whole[:, 0])
    ahead = []
    for index in range(total):
        state = rate[index] * state + keep[index] * whole[:, index]
        ahead.append(state)
    state = jnp.zeros_like(whole[:, 0])
    back = [None] * total
    for index in reversed(range(total)):
        state = rate[index] * state + keep[index] * ahead[index]
        back[index] = state
    swept = jnp.stack(back, axis=1)
    return lax.all_to_all(swept, "layer", 1, 2, tiled=True).reshape(forcing.shape)


def plane_sum(x, axis):
    count = lax.axis_size(axis)
    step = 1
    while step < count:
        x = x + lax.ppermute(x, axis, [(i, i ^ step) for i in range(count)])
        step *= 2
    return x


def shards(
    probes,
    potential,
    projector,
    intersection_ids,
    strength,
    decay_rates,
    contour_nodes,
    node_weights,
):
    layers, columns, rows, depth = probes.shape
    padded = with_halo(probes, (("layer", 0), ("xs", 2)), 2)
    across = jnp.pad(probes, ((0, 0), (0, 0), (0, 0), (2, 2)))
    laplace = second_along(padded[:, :, 2:-2, :], 0, layers)
    laplace = laplace + second_along(padded[2:-2], 2, rows)
    laplace = laplace + second_along(across, 3, depth)
    rounded = probes.astype(jnp.bfloat16).reshape(layers, columns, rows * depth)
    slot_coef = jnp.einsum("lsp,lcp->lsc", projector, rounded, preferred_element_type=jnp.float32)
    onehot = (intersection_ids[:, :, None] == jnp.arange(NPROJ, dtype=jnp.int32)).astype(
        jnp.float32
    )
    partial_coef = jnp.einsum("lsq,lsc->lqc", onehot, slot_coef, precision=lax.Precision.HIGHEST)
    coef = plane_sum(partial_coef, "xs")
    scaled = (strength[:, :, None] * coef).astype(jnp.bfloat16)
    slot_back = jnp.einsum(
        "lsq,lqc->lsc", onehot.astype(jnp.bfloat16), scaled, preferred_element_type=jnp.float32
    ).astype(jnp.bfloat16)
    projected = jnp.einsum(
        "lsp,lsc->lcp", projector, slot_back, preferred_element_type=jnp.float32
    ).reshape(layers, columns, rows, depth)
    hamil = -0.5 * laplace + potential[:, None] * probes + projected
    w0 = jnp.sum(node_weights)
    w1 = jnp.sum(node_weights * contour_nodes)
    w2 = jnp.sum(node_weights * contour_nodes * contour_nodes)
    forcing = jnp.stack([w0 * hamil - w1 * probes, w1 * hamil - w2 * probes])
    return sweeps(forcing, decay_rates)


def solution(mesh):
    in_specs = (
        P("layer", None, "xs", None),
        P("layer", "xs", None),
        P("layer", "xs", None),
        P("layer", "xs"),
        P("layer", None),
        P("layer", None),
        P(),
        P(),
    )
    out_specs = P(None, "layer", None, "xs", None)
    return jax.shard_map(shards, mesh=mesh, in_specs=in_specs, out_specs=out_specs, check_vma=False)
```

```python
import functools

import jax
import jax.numpy as jnp
from jax import lax
from jax.experimental import pallas as pl
from jax.experimental.pallas import tpu as pltpu
from jax.sharding import PartitionSpec as P

NPROJ = 256


FAR = -1.0 / 12.0
NEAR = 4.0 / 3.0
CENTER = -2.5


def with_halo(cells, sides, width):
    for axis, dim in sides:
        count = lax.axis_size(axis)
        ends = count - 1
        head = lax.slice_in_dim(cells, 0, width, axis=dim)
        tail = lax.slice_in_dim(cells, cells.shape[dim] - width, cells.shape[dim], axis=dim)
        cells = jnp.concatenate(
            [
                lax.ppermute(tail, axis, [(i, (i + 1) % count) for i in range(ends)]),
                cells,
                lax.ppermute(head, axis, [((i + 1) % count, i) for i in range(ends)]),
            ],
            axis=dim,
        )
    return cells


def second_along(padded, axis, count):

    def piece(offset):
        return lax.slice_in_dim(padded, 2 + offset, 2 + offset + count, axis=axis)

    return FAR * (piece(-2) + piece(2)) + NEAR * (piece(-1) + piece(1)) + CENTER * piece(0)


MESH = pl.DeviceIdType.MESH


def spans_of(count):
    spans = []
    span = 1
    while 2 * span < count:
        spans.append(span)
        span *= 2
    return spans, span + 1


def sweep_kernel(count, f_ref, d_ref, o_ref, state, landed, send_sem, recv_sem):
    me = lax.axis_index("layer")
    row = lax.axis_index("xs")
    layers = f_ref.shape[1]
    width = f_ref.shape[3]
    spans, far = spans_of(count)
    hops = spans + [1, far]
    barrier = pltpu.get_barrier_semaphore()
    for hop in hops:
        for sign in (1, -1):
            pl.semaphore_signal(
                barrier, inc=1, device_id=(lax.rem(me + sign * hop + count, count), row),
                device_id_type=MESH,
            )
    pl.semaphore_wait(barrier, 2 * len(hops))

    rates = [d_ref[index] for index in range(layers)]
    through = rates[0]
    for index in range(1, layers):
        through = through * rates[index]

    def put(direction, slot, ends, keep):
        state[direction, slot, :, :, :width] = ends
        state[direction, slot, :, :, width:] = jnp.broadcast_to(keep[None], (2,) + keep.shape[:1] + (128,))

    def send(direction, slot, target_slot, hop, sign):
        copy = pltpu.make_async_remote_copy(
            src_ref=state.at[direction, slot],
            dst_ref=landed.at[direction, target_slot],
            send_sem=send_sem.at[direction, target_slot],
            recv_sem=recv_sem.at[direction, target_slot],
            device_id=(lax.rem(me + sign * hop + count, count), row),
            device_id_type=MESH,
        )
        copy.start()
        return copy

    def scan(direction, ends, sign):
        put(direction, 0, ends, through)
        for slot, hop in enumerate(spans):
            send(direction, slot, slot, hop, sign).wait()
            source = me - hop if sign == 1 else me + hop
            valid = ((source >= 0) & (source < count)).astype(jnp.float32)
            mine = state[direction, slot]
            got = landed[direction, slot]
            keep = mine[0, :, width:width + 1]
            put(
                direction, slot + 1,
                mine[:, :, :width] + (valid * keep)[None] * got[:, :, :width],
                keep * (valid * got[0, :, width:width + 1]),
            )
        last = len(spans)
        near = send(direction, last, last, 1, sign)
        distant = send(direction, last, last + 1, far, sign)
        near.wait()
        distant.wait()
        near_source = me - 1 if sign == 1 else me + 1
        far_source = me - far if sign == 1 else me + far
        near_valid = ((near_source >= 0) & (near_source < count)).astype(jnp.float32)
        far_valid = ((far_source >= 0) & (far_source < count)).astype(jnp.float32)
        got = landed[direction, last]
        result = got[:, :, :width]
        if far < count:
            result = result + (far_valid * got[0, :, width:width + 1])[None] * landed[direction, last + 1, :, :, :width]
        return near_valid * result

    state_now = None
    ahead = []
    for index in range(layers):
        source = f_ref[:, index]
        if state_now is None:
            state_now = (1.0 - rates[index])[None] * source
        else:
            state_now = rates[index][None] * state_now + (1.0 - rates[index])[None] * source
        ahead.append(state_now)
    entering = scan(0, state_now, 1)
    lower = rates[0]
    for index in range(layers):
        if index > 0:
            lower = lower * rates[index]
        ahead[index] = ahead[index] + lower[None] * entering
    state_now = None
    back = [None] * layers
    for index in reversed(range(layers)):
        if state_now is None:
            state_now = (1.0 - rates[index])[None] * ahead[index]
        else:
            state_now = rates[index][None] * state_now + (1.0 - rates[index])[None] * ahead[index]
        back[index] = state_now
    from_above = scan(1, state_now, -1)
    upper = rates[layers - 1]
    for index in reversed(range(layers)):
        if index < layers - 1:
            upper = upper * rates[index]
        o_ref[:, index] = back[index] + upper[None] * from_above


def local_sweep_kernel(r_ref, f_ref, o_ref):
    total = f_ref.shape[0]
    here = f_ref.shape[2]
    for column in range(here):

        def forward(index, state):
            rate = r_ref[index, column]
            state = rate * state + (1.0 - rate) * f_ref[index, :, column]
            o_ref[index, :, column] = state
            return state

        zero = jnp.zeros(f_ref.shape[1:2] + f_ref.shape[3:], jnp.float32)
        lax.fori_loop(0, total, forward, zero)

        def backward(step, state):
            index = total - 1 - step
            rate = r_ref[index, column]
            state = rate * state + (1.0 - rate) * o_ref[index, :, column]
            o_ref[index, :, column] = state
            return state

        lax.fori_loop(0, total, backward, zero)


def sweeps(forcing, decay_rates):
    layers, moments, columns, width = forcing.shape
    whole = lax.all_to_all(forcing, "layer", 2, 0, tiled=True)
    rates = lax.all_to_all(decay_rates, "layer", 1, 0, tiled=True)
    total, _, here, _ = whole.shape
    tiles = whole.reshape(total, moments, here, width // 128, 128)
    swept = pl.pallas_call(
        local_sweep_kernel,
        out_shape=jax.ShapeDtypeStruct(tiles.shape, jnp.float32),
        in_specs=[pl.BlockSpec(memory_space=pltpu.SMEM), pl.BlockSpec(memory_space=pltpu.VMEM)],
        out_specs=pl.BlockSpec(memory_space=pltpu.VMEM),
    )(rates, tiles)
    swept = swept.reshape(total, moments, here, width)
    return lax.all_to_all(swept, "layer", 0, 2, tiled=True)


def plane_sum(x, axis):
    count = lax.axis_size(axis)
    step = 1
    while step < count:
        x = x + lax.ppermute(x, axis, [(i, i ^ step) for i in range(count)])
        step *= 2
    return x


def shards(
    probes,
    potential,
    projector,
    intersection_ids,
    strength,
    decay_rates,
    contour_nodes,
    node_weights,
):
    layers, columns, rows, depth = probes.shape
    padded = with_halo(probes, (("layer", 0), ("xs", 2)), 2)
    across = jnp.pad(probes, ((0, 0), (0, 0), (0, 0), (2, 2)))
    laplace = second_along(padded[:, :, 2:-2, :], 0, layers)
    laplace = laplace + second_along(padded[2:-2], 2, rows)
    laplace = laplace + second_along(across, 3, depth)
    rounded = probes.astype(jnp.bfloat16).reshape(layers, columns, rows * depth)
    slot_coef = jnp.einsum("lsp,lcp->lsc", projector, rounded, preferred_element_type=jnp.float32)
    onehot = (intersection_ids[:, :, None] == jnp.arange(NPROJ, dtype=jnp.int32)).astype(
        jnp.float32
    )
    partial_coef = jnp.einsum("lsq,lsc->lqc", onehot, slot_coef, precision=lax.Precision.HIGHEST)
    coef = plane_sum(partial_coef, "xs")
    scaled = (strength[:, :, None] * coef).astype(jnp.bfloat16)
    slot_back = jnp.einsum(
        "lsq,lqc->lsc", onehot.astype(jnp.bfloat16), scaled, preferred_element_type=jnp.float32
    ).astype(jnp.bfloat16)
    projected = jnp.einsum(
        "lsp,lsc->lcp", projector, slot_back, preferred_element_type=jnp.float32
    ).reshape(layers, columns, rows, depth)
    hamil = -0.5 * laplace + potential[:, None] * probes + projected
    w0 = jnp.sum(node_weights)
    w1 = jnp.sum(node_weights * contour_nodes)
    w2 = jnp.sum(node_weights * contour_nodes * contour_nodes)
    forcing = jnp.stack([w0 * hamil - w1 * probes, w1 * hamil - w2 * probes], axis=1)
    swept = sweeps(forcing.reshape(layers, 2, columns, rows * depth), decay_rates)
    return jnp.swapaxes(swept, 0, 1).reshape(2, layers, columns, rows, depth)


def solution(mesh):
    in_specs = (
        P("layer", None, "xs", None),
        P("layer", "xs", None),
        P("layer", "xs", None),
        P("layer", "xs"),
        P("layer", None),
        P("layer", None),
        P(),
        P(),
    )
    out_specs = P(None, "layer", None, "xs", None)
    return jax.shard_map(shards, mesh=mesh, in_specs=in_specs, out_specs=out_specs, check_vma=False)
```

```python
import functools

import jax
import jax.numpy as jnp
from jax import lax
from jax.experimental import pallas as pl
from jax.experimental.pallas import tpu as pltpu
from jax.sharding import PartitionSpec as P

NPROJ = 256


FAR = -1.0 / 12.0
NEAR = 4.0 / 3.0
CENTER = -2.5


def with_halo(cells, sides, width):
    for axis, dim in sides:
        count = lax.axis_size(axis)
        ends = count - 1
        head = lax.slice_in_dim(cells, 0, width, axis=dim)
        tail = lax.slice_in_dim(cells, cells.shape[dim] - width, cells.shape[dim], axis=dim)
        cells = jnp.concatenate(
            [
                lax.ppermute(tail, axis, [(i, (i + 1) % count) for i in range(ends)]),
                cells,
                lax.ppermute(head, axis, [((i + 1) % count, i) for i in range(ends)]),
            ],
            axis=dim,
        )
    return cells


def second_along(padded, axis, count):

    def piece(offset):
        return lax.slice_in_dim(padded, 2 + offset, 2 + offset + count, axis=axis)

    return FAR * (piece(-2) + piece(2)) + NEAR * (piece(-1) + piece(1)) + CENTER * piece(0)


MESH = pl.DeviceIdType.MESH


def spans_of(count):
    spans = []
    span = 1
    while 2 * span < count:
        spans.append(span)
        span *= 2
    return spans, span + 1


def sweep_kernel(count, f_ref, d_ref, o_ref, state, landed, send_sem, recv_sem):
    me = lax.axis_index("layer")
    row = lax.axis_index("xs")
    layers = f_ref.shape[1]
    width = f_ref.shape[3]
    spans, far = spans_of(count)
    hops = spans + [1, far]
    barrier = pltpu.get_barrier_semaphore()
    for hop in hops:
        for sign in (1, -1):
            pl.semaphore_signal(
                barrier, inc=1, device_id=(lax.rem(me + sign * hop + count, count), row),
                device_id_type=MESH,
            )
    pl.semaphore_wait(barrier, 2 * len(hops))

    rates = [d_ref[index] for index in range(layers)]
    through = rates[0]
    for index in range(1, layers):
        through = through * rates[index]

    def put(direction, slot, ends, keep):
        state[direction, slot, :, :, :width] = ends
        state[direction, slot, :, :, width:] = jnp.broadcast_to(keep[None], (2,) + keep.shape[:1] + (128,))

    def send(direction, slot, target_slot, hop, sign):
        copy = pltpu.make_async_remote_copy(
            src_ref=state.at[direction, slot],
            dst_ref=landed.at[direction, target_slot],
            send_sem=send_sem.at[direction, target_slot],
            recv_sem=recv_sem.at[direction, target_slot],
            device_id=(lax.rem(me + sign * hop + count, count), row),
            device_id_type=MESH,
        )
        copy.start()
        return copy

    def scan(direction, ends, sign):
        put(direction, 0, ends, through)
        for slot, hop in enumerate(spans):
            send(direction, slot, slot, hop, sign).wait()
            source = me - hop if sign == 1 else me + hop
            valid = ((source >= 0) & (source < count)).astype(jnp.float32)
            mine = state[direction, slot]
            got = landed[direction, slot]
            keep = mine[0, :, width:width + 1]
            put(
                direction, slot + 1,
                mine[:, :, :width] + (valid * keep)[None] * got[:, :, :width],
                keep * (valid * got[0, :, width:width + 1]),
            )
        last = len(spans)
        near = send(direction, last, last, 1, sign)
        distant = send(direction, last, last + 1, far, sign)
        near.wait()
        distant.wait()
        near_source = me - 1 if sign == 1 else me + 1
        far_source = me - far if sign == 1 else me + far
        near_valid = ((near_source >= 0) & (near_source < count)).astype(jnp.float32)
        far_valid = ((far_source >= 0) & (far_source < count)).astype(jnp.float32)
        got = landed[direction, last]
        result = got[:, :, :width]
        if far < count:
            result = result + (far_valid * got[0, :, width:width + 1])[None] * landed[direction, last + 1, :, :, :width]
        return near_valid * result

    state_now = None
    ahead = []
    for index in range(layers):
        source = f_ref[:, index]
        if state_now is None:
            state_now = (1.0 - rates[index])[None] * source
        else:
            state_now = rates[index][None] * state_now + (1.0 - rates[index])[None] * source
        ahead.append(state_now)
    entering = scan(0, state_now, 1)
    lower = rates[0]
    for index in range(layers):
        if index > 0:
            lower = lower * rates[index]
        ahead[index] = ahead[index] + lower[None] * entering
    state_now = None
    back = [None] * layers
    for index in reversed(range(layers)):
        if state_now is None:
            state_now = (1.0 - rates[index])[None] * ahead[index]
        else:
            state_now = rates[index][None] * state_now + (1.0 - rates[index])[None] * ahead[index]
        back[index] = state_now
    from_above = scan(1, state_now, -1)
    upper = rates[layers - 1]
    for index in reversed(range(layers)):
        if index < layers - 1:
            upper = upper * rates[index]
        o_ref[:, index] = back[index] + upper[None] * from_above


def exchange_kernel(count, ext_ref, out_ref, gathered, swept, send_sem, recv_sem, back_send, back_recv):
    me = lax.axis_index("layer")
    row = lax.axis_index("xs")
    layers = ext_ref.shape[1]
    tiles = out_ref.shape[3]
    barrier = pltpu.get_barrier_semaphore()

    def greet(step, carry):
        pl.semaphore_signal(
            barrier, inc=1, device_id=(lax.rem(me + step, count), row), device_id_type=MESH
        )
        return carry

    lax.fori_loop(1, count, greet, 0)
    pl.semaphore_wait(barrier, count - 1)

    def outgoing(step, carry):
        target = lax.rem(me + step, count)
        pltpu.make_async_remote_copy(
            src_ref=ext_ref.at[target],
            dst_ref=gathered.at[me],
            send_sem=send_sem.at[step],
            recv_sem=recv_sem.at[step],
            device_id=(target, row),
            device_id_type=MESH,
        ).start()
        return carry

    lax.fori_loop(1, count, outgoing, 0)
    gathered[me] = ext_ref[me]

    def arrived(step, carry):
        copy = pltpu.make_async_remote_copy(
            src_ref=ext_ref.at[me],
            dst_ref=gathered.at[lax.rem(me + count - step, count)],
            send_sem=send_sem.at[step],
            recv_sem=recv_sem.at[step],
            device_id=(lax.rem(me + step, count), row),
            device_id_type=MESH,
        )
        copy.wait_send()
        copy.wait_recv()
        return carry

    lax.fori_loop(1, count, arrived, 0)

    zero = jnp.zeros(out_ref.shape[2:], jnp.float32)

    def forward(source, state):
        for layer in range(layers):
            slab = gathered[source, layer]
            rate = slab[0, tiles]
            state = rate * state + (1.0 - rate) * slab[:, :tiles]
            swept[source, layer] = state
        return state

    lax.fori_loop(0, count, forward, zero)

    def backward(step, state):
        source = count - 1 - step
        for layer in reversed(range(layers)):
            rate = gathered[source, layer, 0, tiles]
            state = rate * state + (1.0 - rate) * swept[source, layer]
            swept[source, layer] = state
        return state

    lax.fori_loop(0, count, backward, zero)

    def returning(step, carry):
        target = lax.rem(me + step, count)
        pltpu.make_async_remote_copy(
            src_ref=swept.at[target],
            dst_ref=out_ref.at[me],
            send_sem=back_send.at[step],
            recv_sem=back_recv.at[step],
            device_id=(target, row),
            device_id_type=MESH,
        ).start()
        return carry

    lax.fori_loop(1, count, returning, 0)
    out_ref[me] = swept[me]

    def returned(step, carry):
        copy = pltpu.make_async_remote_copy(
            src_ref=swept.at[me],
            dst_ref=out_ref.at[lax.rem(me + count - step, count)],
            send_sem=back_send.at[step],
            recv_sem=back_recv.at[step],
            device_id=(lax.rem(me + step, count), row),
            device_id_type=MESH,
        )
        copy.wait_send()
        copy.wait_recv()
        return carry

    lax.fori_loop(1, count, returned, 0)


def sweeps(forcing, decay_rates):
    layers, moments, columns, width = forcing.shape
    count = lax.axis_size("layer")
    if columns != count:
        raise ValueError("columns")
    tiles = width // 128
    lanes = jnp.broadcast_to(decay_rates[:, None, :, None], (layers, moments, columns, 128))
    ext = jnp.concatenate([forcing, lanes], axis=3).reshape(layers, moments, columns, tiles + 1, 128)
    ext = jnp.transpose(ext, (2, 0, 1, 3, 4))
    out = pl.pallas_call(
        functools.partial(exchange_kernel, count),
        out_shape=jax.ShapeDtypeStruct((columns, layers, moments, tiles, 128), jnp.float32),
        in_specs=[pl.BlockSpec(memory_space=pltpu.VMEM)],
        out_specs=pl.BlockSpec(memory_space=pltpu.VMEM),
        scratch_shapes=[
            pltpu.VMEM((count, layers, moments, tiles + 1, 128), jnp.float32),
            pltpu.VMEM((count, layers, moments, tiles, 128), jnp.float32),
            pltpu.SemaphoreType.DMA((count,)),
            pltpu.SemaphoreType.DMA((count,)),
            pltpu.SemaphoreType.DMA((count,)),
            pltpu.SemaphoreType.DMA((count,)),
        ],
        compiler_params=pltpu.CompilerParams(collective_id=0, has_side_effects=True),
    )(ext)
    return jnp.transpose(out, (1, 2, 0, 3, 4)).reshape(layers, moments, columns, width)


def plane_sum(x, axis):
    count = lax.axis_size(axis)
    step = 1
    while step < count:
        x = x + lax.ppermute(x, axis, [(i, i ^ step) for i in range(count)])
        step *= 2
    return x


def shards(
    probes,
    potential,
    projector,
    intersection_ids,
    strength,
    decay_rates,
    contour_nodes,
    node_weights,
):
    layers, columns, rows, depth = probes.shape
    stacked = with_halo(probes, (("layer", 0),), 2)
    beside = with_halo(probes, (("xs", 2),), 2)
    across = jnp.pad(probes, ((0, 0), (0, 0), (0, 0), (2, 2)))
    laplace = second_along(stacked, 0, layers)
    laplace = laplace + second_along(beside, 2, rows)
    laplace = laplace + second_along(across, 3, depth)
    rounded = probes.astype(jnp.bfloat16).reshape(layers, columns, rows * depth)
    slot_coef = jnp.einsum("lsp,lcp->lsc", projector, rounded, preferred_element_type=jnp.float32)
    onehot = (intersection_ids[:, :, None] == jnp.arange(NPROJ, dtype=jnp.int32)).astype(
        jnp.float32
    )
    partial_coef = jnp.einsum("lsq,lsc->lqc", onehot, slot_coef, precision=lax.Precision.HIGHEST)
    coef = plane_sum(partial_coef, "xs")
    scaled = (strength[:, :, None] * coef).astype(jnp.bfloat16)
    slot_back = jnp.einsum(
        "lsq,lqc->lsc", onehot.astype(jnp.bfloat16), scaled, preferred_element_type=jnp.float32
    ).astype(jnp.bfloat16)
    projected = jnp.einsum(
        "lsp,lsc->lcp", projector, slot_back, preferred_element_type=jnp.float32
    ).reshape(layers, columns, rows, depth)
    hamil = -0.5 * laplace + potential[:, None] * probes + projected
    w0 = jnp.sum(node_weights)
    w1 = jnp.sum(node_weights * contour_nodes)
    w2 = jnp.sum(node_weights * contour_nodes * contour_nodes)
    forcing = jnp.stack([w0 * hamil - w1 * probes, w1 * hamil - w2 * probes], axis=1)
    swept = sweeps(forcing.reshape(layers, 2, columns, rows * depth), decay_rates)
    return jnp.swapaxes(swept, 0, 1).reshape(2, layers, columns, rows, depth)


def solution(mesh):
    in_specs = (
        P("layer", None, "xs", None),
        P("layer", "xs", None),
        P("layer", "xs", None),
        P("layer", "xs"),
        P("layer", None),
        P("layer", None),
        P(),
        P(),
    )
    out_specs = P(None, "layer", None, "xs", None)
    return jax.shard_map(shards, mesh=mesh, in_specs=in_specs, out_specs=out_specs, check_vma=False)
```

```python
import functools

import jax
import jax.numpy as jnp
from jax import lax
from jax.experimental import pallas as pl
from jax.experimental.pallas import tpu as pltpu
from jax.sharding import PartitionSpec as P

NPROJ = 256


FAR = -1.0 / 12.0
NEAR = 4.0 / 3.0
CENTER = -2.5


def with_halo(cells, sides, width):
    for axis, dim in sides:
        count = lax.axis_size(axis)
        ends = count - 1
        head = lax.slice_in_dim(cells, 0, width, axis=dim)
        tail = lax.slice_in_dim(cells, cells.shape[dim] - width, cells.shape[dim], axis=dim)
        cells = jnp.concatenate(
            [
                lax.ppermute(tail, axis, [(i, (i + 1) % count) for i in range(ends)]),
                cells,
                lax.ppermute(head, axis, [((i + 1) % count, i) for i in range(ends)]),
            ],
            axis=dim,
        )
    return cells


def second_along(padded, axis, count):

    def piece(offset):
        return lax.slice_in_dim(padded, 2 + offset, 2 + offset + count, axis=axis)

    return FAR * (piece(-2) + piece(2)) + NEAR * (piece(-1) + piece(1)) + CENTER * piece(0)


MESH = pl.DeviceIdType.MESH


def spans_of(count):
    spans = []
    span = 1
    while 2 * span < count:
        spans.append(span)
        span *= 2
    return spans, span + 1


def sweep_kernel(count, f_ref, d_ref, o_ref, state, landed, send_sem, recv_sem):
    me = lax.axis_index("layer")
    row = lax.axis_index("xs")
    layers = f_ref.shape[1]
    width = f_ref.shape[3]
    spans, far = spans_of(count)
    hops = spans + [1, far]
    barrier = pltpu.get_barrier_semaphore()
    for hop in hops:
        for sign in (1, -1):
            pl.semaphore_signal(
                barrier, inc=1, device_id=(lax.rem(me + sign * hop + count, count), row),
                device_id_type=MESH,
            )
    pl.semaphore_wait(barrier, 2 * len(hops))

    rates = [d_ref[index] for index in range(layers)]
    through = rates[0]
    for index in range(1, layers):
        through = through * rates[index]

    def put(direction, slot, ends, keep):
        state[direction, slot, :, :, :width] = ends
        state[direction, slot, :, :, width:] = jnp.broadcast_to(keep[None], (2,) + keep.shape[:1] + (128,))

    def send(direction, slot, target_slot, hop, sign):
        copy = pltpu.make_async_remote_copy(
            src_ref=state.at[direction, slot],
            dst_ref=landed.at[direction, target_slot],
            send_sem=send_sem.at[direction, target_slot],
            recv_sem=recv_sem.at[direction, target_slot],
            device_id=(lax.rem(me + sign * hop + count, count), row),
            device_id_type=MESH,
        )
        copy.start()
        return copy

    def scan(direction, ends, sign):
        put(direction, 0, ends, through)
        for slot, hop in enumerate(spans):
            send(direction, slot, slot, hop, sign).wait()
            source = me - hop if sign == 1 else me + hop
            valid = ((source >= 0) & (source < count)).astype(jnp.float32)
            mine = state[direction, slot]
            got = landed[direction, slot]
            keep = mine[0, :, width:width + 1]
            put(
                direction, slot + 1,
                mine[:, :, :width] + (valid * keep)[None] * got[:, :, :width],
                keep * (valid * got[0, :, width:width + 1]),
            )
        last = len(spans)
        near = send(direction, last, last, 1, sign)
        distant = send(direction, last, last + 1, far, sign)
        near.wait()
        distant.wait()
        near_source = me - 1 if sign == 1 else me + 1
        far_source = me - far if sign == 1 else me + far
        near_valid = ((near_source >= 0) & (near_source < count)).astype(jnp.float32)
        far_valid = ((far_source >= 0) & (far_source < count)).astype(jnp.float32)
        got = landed[direction, last]
        result = got[:, :, :width]
        if far < count:
            result = result + (far_valid * got[0, :, width:width + 1])[None] * landed[direction, last + 1, :, :, :width]
        return near_valid * result

    state_now = None
    ahead = []
    for index in range(layers):
        source = f_ref[:, index]
        if state_now is None:
            state_now = (1.0 - rates[index])[None] * source
        else:
            state_now = rates[index][None] * state_now + (1.0 - rates[index])[None] * source
        ahead.append(state_now)
    entering = scan(0, state_now, 1)
    lower = rates[0]
    for index in range(layers):
        if index > 0:
            lower = lower * rates[index]
        ahead[index] = ahead[index] + lower[None] * entering
    state_now = None
    back = [None] * layers
    for index in reversed(range(layers)):
        if state_now is None:
            state_now = (1.0 - rates[index])[None] * ahead[index]
        else:
            state_now = rates[index][None] * state_now + (1.0 - rates[index])[None] * ahead[index]
        back[index] = state_now
    from_above = scan(1, state_now, -1)
    upper = rates[layers - 1]
    for index in reversed(range(layers)):
        if index < layers - 1:
            upper = upper * rates[index]
        o_ref[:, index] = back[index] + upper[None] * from_above


def exchange_kernel(count, ext_ref, out_ref, gathered, swept, send_sem, recv_sem, back_send, back_recv):
    me = lax.axis_index("layer")
    row = lax.axis_index("xs")
    layers = ext_ref.shape[1]
    tiles = out_ref.shape[3]
    barrier = pltpu.get_barrier_semaphore()

    def greet(step, carry):
        pl.semaphore_signal(
            barrier, inc=1, device_id=(lax.rem(me + step, count), row), device_id_type=MESH
        )
        return carry

    lax.fori_loop(1, count, greet, 0)
    pl.semaphore_wait(barrier, count - 1)

    def outgoing(step, carry):
        target = lax.rem(me + step, count)
        pltpu.make_async_remote_copy(
            src_ref=ext_ref.at[target],
            dst_ref=gathered.at[me],
            send_sem=send_sem.at[step],
            recv_sem=recv_sem.at[step],
            device_id=(target, row),
            device_id_type=MESH,
        ).start()
        return carry

    lax.fori_loop(1, count, outgoing, 0)
    gathered[me] = ext_ref[me]

    def arrived(step, carry):
        copy = pltpu.make_async_remote_copy(
            src_ref=ext_ref.at[me],
            dst_ref=gathered.at[lax.rem(me + count - step, count)],
            send_sem=send_sem.at[step],
            recv_sem=recv_sem.at[step],
            device_id=(lax.rem(me + step, count), row),
            device_id_type=MESH,
        )
        copy.wait_send()
        copy.wait_recv()
        return carry

    lax.fori_loop(1, count, arrived, 0)

    zero = jnp.zeros(out_ref.shape[2:], jnp.float32)

    def forward(source, state):
        for layer in range(layers):
            slab = gathered[source, layer]
            rate = slab[0, tiles]
            state = rate * state + (1.0 - rate) * slab[:, :tiles]
            swept[source, layer] = state
        return state

    lax.fori_loop(0, count, forward, zero)

    def backward(step, state):
        source = count - 1 - step
        for layer in reversed(range(layers)):
            rate = gathered[source, layer, 0, tiles]
            state = rate * state + (1.0 - rate) * swept[source, layer]
            swept[source, layer] = state
        return state

    lax.fori_loop(0, count, backward, zero)

    def returning(step, carry):
        target = lax.rem(me + step, count)
        pltpu.make_async_remote_copy(
            src_ref=swept.at[target],
            dst_ref=out_ref.at[me],
            send_sem=back_send.at[step],
            recv_sem=back_recv.at[step],
            device_id=(target, row),
            device_id_type=MESH,
        ).start()
        return carry

    lax.fori_loop(1, count, returning, 0)
    out_ref[me] = swept[me]

    def returned(step, carry):
        copy = pltpu.make_async_remote_copy(
            src_ref=swept.at[me],
            dst_ref=out_ref.at[lax.rem(me + count - step, count)],
            send_sem=back_send.at[step],
            recv_sem=back_recv.at[step],
            device_id=(lax.rem(me + step, count), row),
            device_id_type=MESH,
        )
        copy.wait_send()
        copy.wait_recv()
        return carry

    lax.fori_loop(1, count, returned, 0)


def sweeps(forcing, decay_rates):
    layers, moments, columns, width = forcing.shape
    count = lax.axis_size("layer")
    if columns != count:
        raise ValueError("columns")
    tiles = width // 128
    lanes = jnp.broadcast_to(decay_rates[:, None, :, None], (layers, moments, columns, 128))
    ext = jnp.concatenate([forcing, lanes], axis=3).reshape(layers, moments, columns, tiles + 1, 128)
    ext = jnp.transpose(ext, (2, 0, 1, 3, 4))
    out = pl.pallas_call(
        functools.partial(exchange_kernel, count),
        out_shape=jax.ShapeDtypeStruct((columns, layers, moments, tiles, 128), jnp.float32),
        in_specs=[pl.BlockSpec(memory_space=pltpu.VMEM)],
        out_specs=pl.BlockSpec(memory_space=pltpu.VMEM),
        scratch_shapes=[
            pltpu.VMEM((count, layers, moments, tiles + 1, 128), jnp.float32),
            pltpu.VMEM((count, layers, moments, tiles, 128), jnp.float32),
            pltpu.SemaphoreType.DMA((count,)),
            pltpu.SemaphoreType.DMA((count,)),
            pltpu.SemaphoreType.DMA((count,)),
            pltpu.SemaphoreType.DMA((count,)),
        ],
        compiler_params=pltpu.CompilerParams(collective_id=0, has_side_effects=True),
    )(ext)
    return jnp.transpose(out, (1, 2, 0, 3, 4)).reshape(layers, moments, columns, width)


def front_kernel(layer_count, row_count, block_ref, coef_ref, below, above, left, right, total,
                 gathered, send_sem, recv_sem):
    me = lax.axis_index("layer")
    row = lax.axis_index("xs")
    peers = row_count - 1
    barrier = pltpu.get_barrier_semaphore()
    for sign in (1, -1):
        pl.semaphore_signal(
            barrier, inc=1, device_id=(lax.rem(me + sign + layer_count, layer_count), row),
            device_id_type=MESH,
        )
    for step in range(1, row_count):
        pl.semaphore_signal(
            barrier, inc=1, device_id=(me, lax.rem(row + step, row_count)), device_id_type=MESH
        )
    pl.semaphore_wait(barrier, 2 + peers)
    copies = []
    targets = [
        (below, (lax.rem(me + 1, layer_count), row)),
        (above, (lax.rem(me + layer_count - 1, layer_count), row)),
        (left, (me, lax.rem(row + 1, row_count))),
        (right, (me, lax.rem(row + row_count - 1, row_count))),
    ]
    for slot, (dst, device) in enumerate(targets):
        copies.append(
            pltpu.make_async_remote_copy(
                src_ref=block_ref, dst_ref=dst, send_sem=send_sem.at[slot], recv_sem=recv_sem.at[slot],
                device_id=device, device_id_type=MESH,
            )
        )
    for step in range(1, row_count):
        copies.append(
            pltpu.make_async_remote_copy(
                src_ref=coef_ref, dst_ref=gathered.at[step - 1], send_sem=send_sem.at[3 + step],
                recv_sem=recv_sem.at[3 + step], device_id=(me, lax.rem(row + step, row_count)),
                device_id_type=MESH,
            )
        )
    for copy in copies:
        copy.start()
    for copy in copies[4:]:
        copy.wait()
    acc = coef_ref[...]
    for step in range(peers):
        acc = acc + gathered[step]
    total[...] = acc
    for copy in copies[:4]:
        copy.wait()


def front_exchange(block, coef):
    layer_count = lax.axis_size("layer")
    row_count = lax.axis_size("xs")
    spec = pl.BlockSpec(memory_space=pltpu.VMEM)
    return pl.pallas_call(
        functools.partial(front_kernel, layer_count, row_count),
        out_shape=[jax.ShapeDtypeStruct(block.shape, jnp.float32)] * 4
        + [jax.ShapeDtypeStruct(coef.shape, jnp.float32)],
        in_specs=[spec, spec],
        out_specs=[spec] * 5,
        scratch_shapes=[
            pltpu.VMEM((row_count - 1,) + coef.shape, jnp.float32),
            pltpu.SemaphoreType.DMA((3 + row_count,)),
            pltpu.SemaphoreType.DMA((3 + row_count,)),
        ],
        compiler_params=pltpu.CompilerParams(collective_id=1, has_side_effects=True),
    )(block, coef)


def shards(
    probes,
    potential,
    projector,
    intersection_ids,
    strength,
    decay_rates,
    contour_nodes,
    node_weights,
):
    layers, columns, rows, depth = probes.shape
    rounded = probes.astype(jnp.bfloat16).reshape(layers, columns, rows * depth)
    slot_coef = jnp.einsum("lsp,lcp->lsc", projector, rounded, preferred_element_type=jnp.float32)
    onehot = (intersection_ids[:, :, None] == jnp.arange(NPROJ, dtype=jnp.int32)).astype(
        jnp.float32
    )
    partial_coef = jnp.einsum("lsq,lsc->lcq", onehot, slot_coef, precision=lax.Precision.HIGHEST)
    below, above, left, right, coef = front_exchange(
        probes.reshape(layers, columns, rows * depth), partial_coef
    )
    me = lax.axis_index("layer")
    row = lax.axis_index("xs")
    below = jnp.where(me > 0, below, 0.0).reshape(probes.shape)
    above = jnp.where(me < lax.axis_size("layer") - 1, above, 0.0).reshape(probes.shape)
    left = jnp.where(row > 0, left, 0.0).reshape(probes.shape)
    right = jnp.where(row < lax.axis_size("xs") - 1, right, 0.0).reshape(probes.shape)
    stacked = jnp.concatenate([below, probes, above], axis=0)
    beside = jnp.concatenate([left, probes, right], axis=2)
    across = jnp.pad(probes, ((0, 0), (0, 0), (0, 0), (2, 2)))
    laplace = second_along(stacked, 0, layers)
    laplace = laplace + second_along(beside, 2, rows)
    laplace = laplace + second_along(across, 3, depth)
    coef = jnp.swapaxes(coef, 1, 2)
    scaled = (strength[:, :, None] * coef).astype(jnp.bfloat16)
    slot_back = jnp.einsum(
        "lsq,lqc->lsc", onehot.astype(jnp.bfloat16), scaled, preferred_element_type=jnp.float32
    ).astype(jnp.bfloat16)
    projected = jnp.einsum(
        "lsp,lsc->lcp", projector, slot_back, preferred_element_type=jnp.float32
    ).reshape(layers, columns, rows, depth)
    hamil = -0.5 * laplace + potential[:, None] * probes + projected
    w0 = jnp.sum(node_weights)
    w1 = jnp.sum(node_weights * contour_nodes)
    w2 = jnp.sum(node_weights * contour_nodes * contour_nodes)
    forcing = jnp.stack([w0 * hamil - w1 * probes, w1 * hamil - w2 * probes], axis=1)
    swept = sweeps(forcing.reshape(layers, 2, columns, rows * depth), decay_rates)
    return jnp.swapaxes(swept, 0, 1).reshape(2, layers, columns, rows, depth)


def solution(mesh):
    in_specs = (
        P("layer", None, "xs", None),
        P("layer", "xs", None),
        P("layer", "xs", None),
        P("layer", "xs"),
        P("layer", None),
        P("layer", None),
        P(),
        P(),
    )
    out_specs = P(None, "layer", None, "xs", None)
    return jax.shard_map(shards, mesh=mesh, in_specs=in_specs, out_specs=out_specs, check_vma=False)
```

```python
import functools

import jax
import jax.numpy as jnp
from jax import lax
from jax.experimental import pallas as pl
from jax.experimental.pallas import tpu as pltpu
from jax.sharding import PartitionSpec as P

NPROJ = 256


FAR = -1.0 / 12.0
NEAR = 4.0 / 3.0
CENTER = -2.5


def with_halo(cells, sides, width):
    for axis, dim in sides:
        count = lax.axis_size(axis)
        ends = count - 1
        head = lax.slice_in_dim(cells, 0, width, axis=dim)
        tail = lax.slice_in_dim(cells, cells.shape[dim] - width, cells.shape[dim], axis=dim)
        cells = jnp.concatenate(
            [
                lax.ppermute(tail, axis, [(i, (i + 1) % count) for i in range(ends)]),
                cells,
                lax.ppermute(head, axis, [((i + 1) % count, i) for i in range(ends)]),
            ],
            axis=dim,
        )
    return cells


def second_along(padded, axis, count):

    def piece(offset):
        return lax.slice_in_dim(padded, 2 + offset, 2 + offset + count, axis=axis)

    return FAR * (piece(-2) + piece(2)) + NEAR * (piece(-1) + piece(1)) + CENTER * piece(0)


MESH = pl.DeviceIdType.MESH


def spans_of(count):
    spans = []
    span = 1
    while 2 * span < count:
        spans.append(span)
        span *= 2
    return spans, span + 1


def sweep_kernel(count, f_ref, d_ref, o_ref, state, landed, send_sem, recv_sem):
    me = lax.axis_index("layer")
    row = lax.axis_index("xs")
    layers = f_ref.shape[1]
    width = f_ref.shape[3]
    spans, far = spans_of(count)
    hops = spans + [1, far]
    barrier = pltpu.get_barrier_semaphore()
    for hop in hops:
        for sign in (1, -1):
            pl.semaphore_signal(
                barrier, inc=1, device_id=(lax.rem(me + sign * hop + count, count), row),
                device_id_type=MESH,
            )
    pl.semaphore_wait(barrier, 2 * len(hops))

    rates = [d_ref[index] for index in range(layers)]
    through = rates[0]
    for index in range(1, layers):
        through = through * rates[index]

    def put(direction, slot, ends, keep):
        state[direction, slot, :, :, :width] = ends
        state[direction, slot, :, :, width:] = jnp.broadcast_to(keep[None], (2,) + keep.shape[:1] + (128,))

    def send(direction, slot, target_slot, hop, sign):
        copy = pltpu.make_async_remote_copy(
            src_ref=state.at[direction, slot],
            dst_ref=landed.at[direction, target_slot],
            send_sem=send_sem.at[direction, target_slot],
            recv_sem=recv_sem.at[direction, target_slot],
            device_id=(lax.rem(me + sign * hop + count, count), row),
            device_id_type=MESH,
        )
        copy.start()
        return copy

    def scan(direction, ends, sign):
        put(direction, 0, ends, through)
        for slot, hop in enumerate(spans):
            send(direction, slot, slot, hop, sign).wait()
            source = me - hop if sign == 1 else me + hop
            valid = ((source >= 0) & (source < count)).astype(jnp.float32)
            mine = state[direction, slot]
            got = landed[direction, slot]
            keep = mine[0, :, width:width + 1]
            put(
                direction, slot + 1,
                mine[:, :, :width] + (valid * keep)[None] * got[:, :, :width],
                keep * (valid * got[0, :, width:width + 1]),
            )
        last = len(spans)
        near = send(direction, last, last, 1, sign)
        distant = send(direction, last, last + 1, far, sign)
        near.wait()
        distant.wait()
        near_source = me - 1 if sign == 1 else me + 1
        far_source = me - far if sign == 1 else me + far
        near_valid = ((near_source >= 0) & (near_source < count)).astype(jnp.float32)
        far_valid = ((far_source >= 0) & (far_source < count)).astype(jnp.float32)
        got = landed[direction, last]
        result = got[:, :, :width]
        if far < count:
            result = result + (far_valid * got[0, :, width:width + 1])[None] * landed[direction, last + 1, :, :, :width]
        return near_valid * result

    state_now = None
    ahead = []
    for index in range(layers):
        source = f_ref[:, index]
        if state_now is None:
            state_now = (1.0 - rates[index])[None] * source
        else:
            state_now = rates[index][None] * state_now + (1.0 - rates[index])[None] * source
        ahead.append(state_now)
    entering = scan(0, state_now, 1)
    lower = rates[0]
    for index in range(layers):
        if index > 0:
            lower = lower * rates[index]
        ahead[index] = ahead[index] + lower[None] * entering
    state_now = None
    back = [None] * layers
    for index in reversed(range(layers)):
        if state_now is None:
            state_now = (1.0 - rates[index])[None] * ahead[index]
        else:
            state_now = rates[index][None] * state_now + (1.0 - rates[index])[None] * ahead[index]
        back[index] = state_now
    from_above = scan(1, state_now, -1)
    upper = rates[layers - 1]
    for index in reversed(range(layers)):
        if index < layers - 1:
            upper = upper * rates[index]
        o_ref[:, index] = back[index] + upper[None] * from_above


def exchange_kernel(count, layer_count, ext_ref, out_ref, gathered, swept, send_sem, recv_sem, back_send, back_recv):
    me = lax.axis_index("layer")
    row = lax.axis_index("xs")
    layers = layer_count
    barrier = pltpu.get_barrier_semaphore()

    def greet(step, carry):
        pl.semaphore_signal(
            barrier, inc=1, device_id=(lax.rem(me + step, count), row), device_id_type=MESH
        )
        return carry

    lax.fori_loop(1, count, greet, 0)
    pl.semaphore_wait(barrier, count - 1)

    def outgoing(step, carry):
        target = lax.rem(me + step, count)
        pltpu.make_async_remote_copy(
            src_ref=ext_ref.at[target],
            dst_ref=gathered.at[me],
            send_sem=send_sem.at[step],
            recv_sem=recv_sem.at[step],
            device_id=(target, row),
            device_id_type=MESH,
        ).start()
        return carry

    lax.fori_loop(1, count, outgoing, 0)
    gathered[me] = ext_ref[me]

    def arrived(step, carry):
        copy = pltpu.make_async_remote_copy(
            src_ref=ext_ref.at[me],
            dst_ref=gathered.at[lax.rem(me + count - step, count)],
            send_sem=send_sem.at[step],
            recv_sem=recv_sem.at[step],
            device_id=(lax.rem(me + step, count), row),
            device_id_type=MESH,
        )
        copy.wait_send()
        copy.wait_recv()
        return carry

    lax.fori_loop(1, count, arrived, 0)

    rows_per_layer = out_ref.shape[1] // layers
    zero = jnp.zeros((rows_per_layer, out_ref.shape[2]), jnp.float32)
    data_rows = out_ref.shape[1]

    def forward(source, state):
        for layer in range(layers):
            rate = gathered[source, pl.ds(data_rows + layer, 1), :]
            slab = gathered[source, pl.ds(layer * rows_per_layer, rows_per_layer), :]
            state = rate * state + (1.0 - rate) * slab
            swept[source, pl.ds(layer * rows_per_layer, rows_per_layer), :] = state
        return state

    lax.fori_loop(0, count, forward, zero)

    def backward(step, state):
        source = count - 1 - step
        for layer in reversed(range(layers)):
            rate = gathered[source, pl.ds(data_rows + layer, 1), :]
            piece = pl.ds(layer * rows_per_layer, rows_per_layer)
            state = rate * state + (1.0 - rate) * swept[source, piece, :]
            swept[source, piece, :] = state
        return state

    lax.fori_loop(0, count, backward, zero)

    def returning(step, carry):
        target = lax.rem(me + step, count)
        pltpu.make_async_remote_copy(
            src_ref=swept.at[target],
            dst_ref=out_ref.at[me],
            send_sem=back_send.at[step],
            recv_sem=back_recv.at[step],
            device_id=(target, row),
            device_id_type=MESH,
        ).start()
        return carry

    lax.fori_loop(1, count, returning, 0)
    out_ref[me] = swept[me]

    def returned(step, carry):
        copy = pltpu.make_async_remote_copy(
            src_ref=swept.at[me],
            dst_ref=out_ref.at[lax.rem(me + count - step, count)],
            send_sem=back_send.at[step],
            recv_sem=back_recv.at[step],
            device_id=(lax.rem(me + step, count), row),
            device_id_type=MESH,
        )
        copy.wait_send()
        copy.wait_recv()
        return carry

    lax.fori_loop(1, count, returned, 0)


def sweeps(forcing, decay_rates):
    layers, moments, columns, width = forcing.shape
    count = lax.axis_size("layer")
    if columns != count:
        raise ValueError("columns")
    tiles = width // 128
    data_rows = layers * moments * tiles
    padded_rows = -(-(data_rows + layers) // 8) * 8
    body = jnp.transpose(forcing, (2, 0, 1, 3)).reshape(columns, data_rows, 128)
    lanes = jnp.broadcast_to(jnp.transpose(decay_rates)[:, :, None], (columns, layers, 128))
    spare = jnp.zeros((columns, padded_rows - data_rows - layers, 128), jnp.float32)
    ext = jnp.concatenate([body, lanes, spare], axis=1)
    out = pl.pallas_call(
        functools.partial(exchange_kernel, count, layers),
        out_shape=jax.ShapeDtypeStruct((columns, data_rows, 128), jnp.float32),
        in_specs=[pl.BlockSpec(memory_space=pltpu.VMEM)],
        out_specs=pl.BlockSpec(memory_space=pltpu.VMEM),
        scratch_shapes=[
            pltpu.VMEM((count, padded_rows, 128), jnp.float32),
            pltpu.VMEM((count, data_rows, 128), jnp.float32),
            pltpu.SemaphoreType.DMA((count,)),
            pltpu.SemaphoreType.DMA((count,)),
            pltpu.SemaphoreType.DMA((count,)),
            pltpu.SemaphoreType.DMA((count,)),
        ],
        compiler_params=pltpu.CompilerParams(collective_id=0, has_side_effects=True),
    )(ext)
    return jnp.transpose(out.reshape(columns, layers, moments, width), (1, 2, 0, 3))


def front_kernel(layer_count, row_count, block_ref, coef_ref, below, above, left, right, total,
                 gathered, send_sem, recv_sem):
    me = lax.axis_index("layer")
    row = lax.axis_index("xs")
    peers = row_count - 1
    barrier = pltpu.get_barrier_semaphore()
    for sign in (1, -1):
        pl.semaphore_signal(
            barrier, inc=1, device_id=(lax.rem(me + sign + layer_count, layer_count), row),
            device_id_type=MESH,
        )
    for step in range(1, row_count):
        pl.semaphore_signal(
            barrier, inc=1, device_id=(me, lax.rem(row + step, row_count)), device_id_type=MESH
        )
    pl.semaphore_wait(barrier, 2 + peers)
    copies = []
    targets = [
        (below, (lax.rem(me + 1, layer_count), row)),
        (above, (lax.rem(me + layer_count - 1, layer_count), row)),
        (left, (me, lax.rem(row + 1, row_count))),
        (right, (me, lax.rem(row + row_count - 1, row_count))),
    ]
    for slot, (dst, device) in enumerate(targets):
        copies.append(
            pltpu.make_async_remote_copy(
                src_ref=block_ref, dst_ref=dst, send_sem=send_sem.at[slot], recv_sem=recv_sem.at[slot],
                device_id=device, device_id_type=MESH,
            )
        )
    for step in range(1, row_count):
        copies.append(
            pltpu.make_async_remote_copy(
                src_ref=coef_ref, dst_ref=gathered.at[step - 1], send_sem=send_sem.at[3 + step],
                recv_sem=recv_sem.at[3 + step], device_id=(me, lax.rem(row + step, row_count)),
                device_id_type=MESH,
            )
        )
    for copy in copies:
        copy.start()
    for copy in copies[4:]:
        copy.wait()
    acc = coef_ref[...]
    for step in range(peers):
        acc = acc + gathered[step]
    total[...] = acc
    for copy in copies[:4]:
        copy.wait()


def front_exchange(block, coef):
    layer_count = lax.axis_size("layer")
    row_count = lax.axis_size("xs")
    spec = pl.BlockSpec(memory_space=pltpu.VMEM)
    return pl.pallas_call(
        functools.partial(front_kernel, layer_count, row_count),
        out_shape=[jax.ShapeDtypeStruct(block.shape, jnp.float32)] * 4
        + [jax.ShapeDtypeStruct(coef.shape, jnp.float32)],
        in_specs=[spec, spec],
        out_specs=[spec] * 5,
        scratch_shapes=[
            pltpu.VMEM((row_count - 1,) + coef.shape, jnp.float32),
            pltpu.SemaphoreType.DMA((3 + row_count,)),
            pltpu.SemaphoreType.DMA((3 + row_count,)),
        ],
        compiler_params=pltpu.CompilerParams(collective_id=1, has_side_effects=True),
    )(block, coef)


def shards(
    probes,
    potential,
    projector,
    intersection_ids,
    strength,
    decay_rates,
    contour_nodes,
    node_weights,
):
    layers, columns, rows, depth = probes.shape
    rounded = probes.astype(jnp.bfloat16).reshape(layers, columns, rows * depth)
    slot_coef = jnp.einsum("lsp,lcp->lsc", projector, rounded, preferred_element_type=jnp.float32)
    onehot = (intersection_ids[:, :, None] == jnp.arange(NPROJ, dtype=jnp.int32)).astype(
        jnp.float32
    )
    partial_coef = jnp.einsum("lsq,lsc->lcq", onehot, slot_coef, precision=lax.Precision.HIGHEST)
    below, above, left, right, coef = front_exchange(
        probes.reshape(layers, columns, rows * depth), partial_coef
    )
    me = lax.axis_index("layer")
    row = lax.axis_index("xs")
    below = jnp.where(me > 0, below, 0.0).reshape(probes.shape)
    above = jnp.where(me < lax.axis_size("layer") - 1, above, 0.0).reshape(probes.shape)
    left = jnp.where(row > 0, left, 0.0).reshape(probes.shape)
    right = jnp.where(row < lax.axis_size("xs") - 1, right, 0.0).reshape(probes.shape)
    stacked = jnp.concatenate([below, probes, above], axis=0)
    beside = jnp.concatenate([left, probes, right], axis=2)
    across = jnp.pad(probes, ((0, 0), (0, 0), (0, 0), (2, 2)))
    laplace = second_along(stacked, 0, layers)
    laplace = laplace + second_along(beside, 2, rows)
    laplace = laplace + second_along(across, 3, depth)
    coef = jnp.swapaxes(coef, 1, 2)
    scaled = (strength[:, :, None] * coef).astype(jnp.bfloat16)
    slot_back = jnp.einsum(
        "lsq,lqc->lsc", onehot.astype(jnp.bfloat16), scaled, preferred_element_type=jnp.float32
    ).astype(jnp.bfloat16)
    projected = jnp.einsum(
        "lsp,lsc->lcp", projector, slot_back, preferred_element_type=jnp.float32
    ).reshape(layers, columns, rows, depth)
    hamil = -0.5 * laplace + potential[:, None] * probes + projected
    w0 = jnp.sum(node_weights)
    w1 = jnp.sum(node_weights * contour_nodes)
    w2 = jnp.sum(node_weights * contour_nodes * contour_nodes)
    forcing = jnp.stack([w0 * hamil - w1 * probes, w1 * hamil - w2 * probes], axis=1)
    swept = sweeps(forcing.reshape(layers, 2, columns, rows * depth), decay_rates)
    return jnp.swapaxes(swept, 0, 1).reshape(2, layers, columns, rows, depth)


def solution(mesh):
    in_specs = (
        P("layer", None, "xs", None),
        P("layer", "xs", None),
        P("layer", "xs", None),
        P("layer", "xs"),
        P("layer", None),
        P("layer", None),
        P(),
        P(),
    )
    out_specs = P(None, "layer", None, "xs", None)
    return jax.shard_map(shards, mesh=mesh, in_specs=in_specs, out_specs=out_specs, check_vma=False)
```

```python
import functools

import jax
import jax.numpy as jnp
from jax import lax
from jax.experimental import pallas as pl
from jax.experimental.pallas import tpu as pltpu
from jax.sharding import PartitionSpec as P

NPROJ = 256


FAR = -1.0 / 12.0
NEAR = 4.0 / 3.0
CENTER = -2.5


def with_halo(cells, sides, width):
    for axis, dim in sides:
        count = lax.axis_size(axis)
        ends = count - 1
        head = lax.slice_in_dim(cells, 0, width, axis=dim)
        tail = lax.slice_in_dim(cells, cells.shape[dim] - width, cells.shape[dim], axis=dim)
        cells = jnp.concatenate(
            [
                lax.ppermute(tail, axis, [(i, (i + 1) % count) for i in range(ends)]),
                cells,
                lax.ppermute(head, axis, [((i + 1) % count, i) for i in range(ends)]),
            ],
            axis=dim,
        )
    return cells


def second_along(padded, axis, count):

    def piece(offset):
        return lax.slice_in_dim(padded, 2 + offset, 2 + offset + count, axis=axis)

    return FAR * (piece(-2) + piece(2)) + NEAR * (piece(-1) + piece(1)) + CENTER * piece(0)


MESH = pl.DeviceIdType.MESH


def spans_of(count):
    spans = []
    span = 1
    while 2 * span < count:
        spans.append(span)
        span *= 2
    return spans, span + 1


def sweep_kernel(count, f_ref, d_ref, o_ref, state, landed, send_sem, recv_sem):
    me = lax.axis_index("layer")
    row = lax.axis_index("xs")
    layers = f_ref.shape[1]
    width = f_ref.shape[3]
    spans, far = spans_of(count)
    hops = spans + [1, far]
    barrier = pltpu.get_barrier_semaphore()
    for hop in hops:
        for sign in (1, -1):
            pl.semaphore_signal(
                barrier, inc=1, device_id=(lax.rem(me + sign * hop + count, count), row),
                device_id_type=MESH,
            )
    pl.semaphore_wait(barrier, 2 * len(hops))

    rates = [d_ref[index] for index in range(layers)]
    through = rates[0]
    for index in range(1, layers):
        through = through * rates[index]

    def put(direction, slot, ends, keep):
        state[direction, slot, :, :, :width] = ends
        state[direction, slot, :, :, width:] = jnp.broadcast_to(keep[None], (2,) + keep.shape[:1] + (128,))

    def send(direction, slot, target_slot, hop, sign):
        copy = pltpu.make_async_remote_copy(
            src_ref=state.at[direction, slot],
            dst_ref=landed.at[direction, target_slot],
            send_sem=send_sem.at[direction, target_slot],
            recv_sem=recv_sem.at[direction, target_slot],
            device_id=(lax.rem(me + sign * hop + count, count), row),
            device_id_type=MESH,
        )
        copy.start()
        return copy

    def scan(direction, ends, sign):
        put(direction, 0, ends, through)
        for slot, hop in enumerate(spans):
            send(direction, slot, slot, hop, sign).wait()
            source = me - hop if sign == 1 else me + hop
            valid = ((source >= 0) & (source < count)).astype(jnp.float32)
            mine = state[direction, slot]
            got = landed[direction, slot]
            keep = mine[0, :, width:width + 1]
            put(
                direction, slot + 1,
                mine[:, :, :width] + (valid * keep)[None] * got[:, :, :width],
                keep * (valid * got[0, :, width:width + 1]),
            )
        last = len(spans)
        near = send(direction, last, last, 1, sign)
        distant = send(direction, last, last + 1, far, sign)
        near.wait()
        distant.wait()
        near_source = me - 1 if sign == 1 else me + 1
        far_source = me - far if sign == 1 else me + far
        near_valid = ((near_source >= 0) & (near_source < count)).astype(jnp.float32)
        far_valid = ((far_source >= 0) & (far_source < count)).astype(jnp.float32)
        got = landed[direction, last]
        result = got[:, :, :width]
        if far < count:
            result = result + (far_valid * got[0, :, width:width + 1])[None] * landed[direction, last + 1, :, :, :width]
        return near_valid * result

    state_now = None
    ahead = []
    for index in range(layers):
        source = f_ref[:, index]
        if state_now is None:
            state_now = (1.0 - rates[index])[None] * source
        else:
            state_now = rates[index][None] * state_now + (1.0 - rates[index])[None] * source
        ahead.append(state_now)
    entering = scan(0, state_now, 1)
    lower = rates[0]
    for index in range(layers):
        if index > 0:
            lower = lower * rates[index]
        ahead[index] = ahead[index] + lower[None] * entering
    state_now = None
    back = [None] * layers
    for index in reversed(range(layers)):
        if state_now is None:
            state_now = (1.0 - rates[index])[None] * ahead[index]
        else:
            state_now = rates[index][None] * state_now + (1.0 - rates[index])[None] * ahead[index]
        back[index] = state_now
    from_above = scan(1, state_now, -1)
    upper = rates[layers - 1]
    for index in reversed(range(layers)):
        if index < layers - 1:
            upper = upper * rates[index]
        o_ref[:, index] = back[index] + upper[None] * from_above


def exchange_kernel(count, layer_count, w_ref, ext_ref, out_ref, gathered, swept, send_sem, recv_sem, back_send, back_recv):
    me = lax.axis_index("layer")
    row = lax.axis_index("xs")
    layers = layer_count
    barrier = pltpu.get_barrier_semaphore()

    def greet(step, carry):
        pl.semaphore_signal(
            barrier, inc=1, device_id=(lax.rem(me + step, count), row), device_id_type=MESH
        )
        return carry

    lax.fori_loop(1, count, greet, 0)
    pl.semaphore_wait(barrier, count - 1)

    def outgoing(step, carry):
        target = lax.rem(me + step, count)
        pltpu.make_async_remote_copy(
            src_ref=ext_ref.at[target],
            dst_ref=gathered.at[me],
            send_sem=send_sem.at[step],
            recv_sem=recv_sem.at[step],
            device_id=(target, row),
            device_id_type=MESH,
        ).start()
        return carry

    lax.fori_loop(1, count, outgoing, 0)
    gathered[me] = ext_ref[me]

    def arrived(step, carry):
        copy = pltpu.make_async_remote_copy(
            src_ref=ext_ref.at[me],
            dst_ref=gathered.at[lax.rem(me + count - step, count)],
            send_sem=send_sem.at[step],
            recv_sem=recv_sem.at[step],
            device_id=(lax.rem(me + step, count), row),
            device_id_type=MESH,
        )
        copy.wait_send()
        copy.wait_recv()
        return carry

    lax.fori_loop(1, count, arrived, 0)

    rows_per_layer = out_ref.shape[1] // layers
    half = rows_per_layer // 2
    zero = jnp.zeros((rows_per_layer, out_ref.shape[2]), jnp.float32)
    data_rows = out_ref.shape[1]
    total = count * layers
    w0, w1, w2 = w_ref[0], w_ref[1], w_ref[2]

    def probe_at(place):
        inside = ((place >= 0) & (place < total)).astype(jnp.float32)
        place = jnp.clip(place, 0, total - 1)
        source = place // layers
        layer = place - source * layers
        return inside * gathered[source, pl.ds(layer * rows_per_layer + half, half), :]

    def prepare(source, carry):
        for layer in range(layers):
            place = source * layers + layer
            here = gathered[source, pl.ds(layer * rows_per_layer + half, half), :]
            partial = gathered[source, pl.ds(layer * rows_per_layer, half), :]
            second = (
                FAR * (probe_at(place - 2) + probe_at(place + 2))
                + NEAR * (probe_at(place - 1) + probe_at(place + 1))
                + CENTER * here
            )
            hamil = partial - 0.5 * second
            swept[source, pl.ds(layer * rows_per_layer, half), :] = w0 * hamil - w1 * here
            swept[source, pl.ds(layer * rows_per_layer + half, half), :] = w1 * hamil - w2 * here
        return carry

    lax.fori_loop(0, count, prepare, 0)

    def forward(source, state):
        for layer in range(layers):
            rate = gathered[source, pl.ds(data_rows + layer, 1), :]
            slab = swept[source, pl.ds(layer * rows_per_layer, rows_per_layer), :]
            state = rate * state + (1.0 - rate) * slab
            swept[source, pl.ds(layer * rows_per_layer, rows_per_layer), :] = state
        return state

    lax.fori_loop(0, count, forward, zero)

    def backward(step, state):
        source = count - 1 - step
        for layer in reversed(range(layers)):
            rate = gathered[source, pl.ds(data_rows + layer, 1), :]
            piece = pl.ds(layer * rows_per_layer, rows_per_layer)
            state = rate * state + (1.0 - rate) * swept[source, piece, :]
            swept[source, piece, :] = state
        return state

    lax.fori_loop(0, count, backward, zero)

    def returning(step, carry):
        target = lax.rem(me + step, count)
        pltpu.make_async_remote_copy(
            src_ref=swept.at[target],
            dst_ref=out_ref.at[me],
            send_sem=back_send.at[step],
            recv_sem=back_recv.at[step],
            device_id=(target, row),
            device_id_type=MESH,
        ).start()
        return carry

    lax.fori_loop(1, count, returning, 0)
    out_ref[me] = swept[me]

    def returned(step, carry):
        copy = pltpu.make_async_remote_copy(
            src_ref=swept.at[me],
            dst_ref=out_ref.at[lax.rem(me + count - step, count)],
            send_sem=back_send.at[step],
            recv_sem=back_recv.at[step],
            device_id=(lax.rem(me + step, count), row),
            device_id_type=MESH,
        )
        copy.wait_send()
        copy.wait_recv()
        return carry

    lax.fori_loop(1, count, returned, 0)


def sweeps(forcing, decay_rates, weights):
    layers, moments, columns, width = forcing.shape
    count = lax.axis_size("layer")
    if columns != count:
        raise ValueError("columns")
    tiles = width // 128
    data_rows = layers * moments * tiles
    padded_rows = -(-(data_rows + layers) // 8) * 8
    body = jnp.transpose(forcing, (2, 0, 1, 3)).reshape(columns, data_rows, 128)
    lanes = jnp.broadcast_to(jnp.transpose(decay_rates)[:, :, None], (columns, layers, 128))
    spare = jnp.zeros((columns, padded_rows - data_rows - layers, 128), jnp.float32)
    ext = jnp.concatenate([body, lanes, spare], axis=1)
    out = pl.pallas_call(
        functools.partial(exchange_kernel, count, layers),
        out_shape=jax.ShapeDtypeStruct((columns, data_rows, 128), jnp.float32),
        in_specs=[pl.BlockSpec(memory_space=pltpu.SMEM), pl.BlockSpec(memory_space=pltpu.VMEM)],
        out_specs=pl.BlockSpec(memory_space=pltpu.VMEM),
        scratch_shapes=[
            pltpu.VMEM((count, padded_rows, 128), jnp.float32),
            pltpu.VMEM((count, data_rows, 128), jnp.float32),
            pltpu.SemaphoreType.DMA((count,)),
            pltpu.SemaphoreType.DMA((count,)),
            pltpu.SemaphoreType.DMA((count,)),
            pltpu.SemaphoreType.DMA((count,)),
        ],
        compiler_params=pltpu.CompilerParams(collective_id=0, has_side_effects=True),
    )(weights, ext)
    return jnp.transpose(out.reshape(columns, layers, moments, width), (1, 2, 0, 3))


def front_kernel(row_count, block_ref, coef_ref, left, right, total, gathered, send_sem, recv_sem):
    me = lax.axis_index("layer")
    row = lax.axis_index("xs")
    peers = row_count - 1
    barrier = pltpu.get_barrier_semaphore()
    for step in range(1, row_count):
        pl.semaphore_signal(
            barrier, inc=1, device_id=(me, lax.rem(row + step, row_count)), device_id_type=MESH
        )
    pl.semaphore_wait(barrier, peers)
    copies = []
    targets = [
        (left, (me, lax.rem(row + 1, row_count))),
        (right, (me, lax.rem(row + row_count - 1, row_count))),
    ]
    for slot, (dst, device) in enumerate(targets):
        copies.append(
            pltpu.make_async_remote_copy(
                src_ref=block_ref, dst_ref=dst, send_sem=send_sem.at[slot], recv_sem=recv_sem.at[slot],
                device_id=device, device_id_type=MESH,
            )
        )
    for step in range(1, row_count):
        copies.append(
            pltpu.make_async_remote_copy(
                src_ref=coef_ref, dst_ref=gathered.at[step - 1], send_sem=send_sem.at[1 + step],
                recv_sem=recv_sem.at[1 + step], device_id=(me, lax.rem(row + step, row_count)),
                device_id_type=MESH,
            )
        )
    for copy in copies:
        copy.start()
    for copy in copies[2:]:
        copy.wait()
    acc = coef_ref[...]
    for step in range(peers):
        acc = acc + gathered[step]
    total[...] = acc
    for copy in copies[:2]:
        copy.wait()


def front_exchange(block, coef):
    row_count = lax.axis_size("xs")
    spec = pl.BlockSpec(memory_space=pltpu.VMEM)
    return pl.pallas_call(
        functools.partial(front_kernel, row_count),
        out_shape=[jax.ShapeDtypeStruct(block.shape, jnp.float32)] * 2
        + [jax.ShapeDtypeStruct(coef.shape, jnp.float32)],
        in_specs=[spec, spec],
        out_specs=[spec] * 3,
        scratch_shapes=[
            pltpu.VMEM((row_count - 1,) + coef.shape, jnp.float32),
            pltpu.SemaphoreType.DMA((1 + row_count,)),
            pltpu.SemaphoreType.DMA((1 + row_count,)),
        ],
        compiler_params=pltpu.CompilerParams(collective_id=1, has_side_effects=True),
    )(block, coef)


def shards(
    probes,
    potential,
    projector,
    intersection_ids,
    strength,
    decay_rates,
    contour_nodes,
    node_weights,
):
    layers, columns, rows, depth = probes.shape
    rounded = probes.astype(jnp.bfloat16).reshape(layers, columns, rows * depth)
    slot_coef = jnp.einsum("lsp,lcp->lsc", projector, rounded, preferred_element_type=jnp.float32)
    onehot = (intersection_ids[:, :, None] == jnp.arange(NPROJ, dtype=jnp.int32)).astype(
        jnp.float32
    )
    partial_coef = jnp.einsum("lsq,lsc->lcq", onehot, slot_coef, precision=lax.Precision.HIGHEST)
    left, right, coef = front_exchange(probes.reshape(layers, columns, rows * depth), partial_coef)
    row = lax.axis_index("xs")
    left = jnp.where(row > 0, left, 0.0).reshape(probes.shape)
    right = jnp.where(row < lax.axis_size("xs") - 1, right, 0.0).reshape(probes.shape)
    beside = jnp.concatenate([left, probes, right], axis=2)
    across = jnp.pad(probes, ((0, 0), (0, 0), (0, 0), (2, 2)))
    laplace = second_along(beside, 2, rows)
    laplace = laplace + second_along(across, 3, depth)
    coef = jnp.swapaxes(coef, 1, 2)
    scaled = (strength[:, :, None] * coef).astype(jnp.bfloat16)
    slot_back = jnp.einsum(
        "lsq,lqc->lsc", onehot.astype(jnp.bfloat16), scaled, preferred_element_type=jnp.float32
    ).astype(jnp.bfloat16)
    projected = jnp.einsum(
        "lsp,lsc->lcp", projector, slot_back, preferred_element_type=jnp.float32
    ).reshape(layers, columns, rows, depth)
    partial = -0.5 * laplace + potential[:, None] * probes + projected
    weights = jnp.stack(
        [
            jnp.sum(node_weights),
            jnp.sum(node_weights * contour_nodes),
            jnp.sum(node_weights * contour_nodes * contour_nodes),
        ]
    )
    fields = jnp.stack([partial, probes], axis=1)
    swept = sweeps(fields.reshape(layers, 2, columns, rows * depth), decay_rates, weights)
    return jnp.swapaxes(swept, 0, 1).reshape(2, layers, columns, rows, depth)


def solution(mesh):
    in_specs = (
        P("layer", None, "xs", None),
        P("layer", "xs", None),
        P("layer", "xs", None),
        P("layer", "xs"),
        P("layer", None),
        P("layer", None),
        P(),
        P(),
    )
    out_specs = P(None, "layer", None, "xs", None)
    return jax.shard_map(shards, mesh=mesh, in_specs=in_specs, out_specs=out_specs, check_vma=False)
```

```python
import functools

import jax
import jax.numpy as jnp
from jax import lax
from jax.experimental import pallas as pl
from jax.experimental.pallas import tpu as pltpu
from jax.sharding import PartitionSpec as P

NPROJ = 256


FAR = -1.0 / 12.0
NEAR = 4.0 / 3.0
CENTER = -2.5


def with_halo(cells, sides, width):
    for axis, dim in sides:
        count = lax.axis_size(axis)
        ends = count - 1
        head = lax.slice_in_dim(cells, 0, width, axis=dim)
        tail = lax.slice_in_dim(cells, cells.shape[dim] - width, cells.shape[dim], axis=dim)
        cells = jnp.concatenate(
            [
                lax.ppermute(tail, axis, [(i, (i + 1) % count) for i in range(ends)]),
                cells,
                lax.ppermute(head, axis, [((i + 1) % count, i) for i in range(ends)]),
            ],
            axis=dim,
        )
    return cells


def second_along(padded, axis, count):

    def piece(offset):
        return lax.slice_in_dim(padded, 2 + offset, 2 + offset + count, axis=axis)

    return FAR * (piece(-2) + piece(2)) + NEAR * (piece(-1) + piece(1)) + CENTER * piece(0)


MESH = pl.DeviceIdType.MESH


def spans_of(count):
    spans = []
    span = 1
    while 2 * span < count:
        spans.append(span)
        span *= 2
    return spans, span + 1


def sweep_kernel(count, f_ref, d_ref, o_ref, state, landed, send_sem, recv_sem):
    me = lax.axis_index("layer")
    row = lax.axis_index("xs")
    layers = f_ref.shape[1]
    width = f_ref.shape[3]
    spans, far = spans_of(count)
    hops = spans + [1, far]
    barrier = pltpu.get_barrier_semaphore()
    for hop in hops:
        for sign in (1, -1):
            pl.semaphore_signal(
                barrier, inc=1, device_id=(lax.rem(me + sign * hop + count, count), row),
                device_id_type=MESH,
            )
    pl.semaphore_wait(barrier, 2 * len(hops))

    rates = [d_ref[index] for index in range(layers)]
    through = rates[0]
    for index in range(1, layers):
        through = through * rates[index]

    def put(direction, slot, ends, keep):
        state[direction, slot, :, :, :width] = ends
        state[direction, slot, :, :, width:] = jnp.broadcast_to(keep[None], (2,) + keep.shape[:1] + (128,))

    def send(direction, slot, target_slot, hop, sign):
        copy = pltpu.make_async_remote_copy(
            src_ref=state.at[direction, slot],
            dst_ref=landed.at[direction, target_slot],
            send_sem=send_sem.at[direction, target_slot],
            recv_sem=recv_sem.at[direction, target_slot],
            device_id=(lax.rem(me + sign * hop + count, count), row),
            device_id_type=MESH,
        )
        copy.start()
        return copy

    def scan(direction, ends, sign):
        put(direction, 0, ends, through)
        for slot, hop in enumerate(spans):
            send(direction, slot, slot, hop, sign).wait()
            source = me - hop if sign == 1 else me + hop
            valid = ((source >= 0) & (source < count)).astype(jnp.float32)
            mine = state[direction, slot]
            got = landed[direction, slot]
            keep = mine[0, :, width:width + 1]
            put(
                direction, slot + 1,
                mine[:, :, :width] + (valid * keep)[None] * got[:, :, :width],
                keep * (valid * got[0, :, width:width + 1]),
            )
        last = len(spans)
        near = send(direction, last, last, 1, sign)
        distant = send(direction, last, last + 1, far, sign)
        near.wait()
        distant.wait()
        near_source = me - 1 if sign == 1 else me + 1
        far_source = me - far if sign == 1 else me + far
        near_valid = ((near_source >= 0) & (near_source < count)).astype(jnp.float32)
        far_valid = ((far_source >= 0) & (far_source < count)).astype(jnp.float32)
        got = landed[direction, last]
        result = got[:, :, :width]
        if far < count:
            result = result + (far_valid * got[0, :, width:width + 1])[None] * landed[direction, last + 1, :, :, :width]
        return near_valid * result

    state_now = None
    ahead = []
    for index in range(layers):
        source = f_ref[:, index]
        if state_now is None:
            state_now = (1.0 - rates[index])[None] * source
        else:
            state_now = rates[index][None] * state_now + (1.0 - rates[index])[None] * source
        ahead.append(state_now)
    entering = scan(0, state_now, 1)
    lower = rates[0]
    for index in range(layers):
        if index > 0:
            lower = lower * rates[index]
        ahead[index] = ahead[index] + lower[None] * entering
    state_now = None
    back = [None] * layers
    for index in reversed(range(layers)):
        if state_now is None:
            state_now = (1.0 - rates[index])[None] * ahead[index]
        else:
            state_now = rates[index][None] * state_now + (1.0 - rates[index])[None] * ahead[index]
        back[index] = state_now
    from_above = scan(1, state_now, -1)
    upper = rates[layers - 1]
    for index in reversed(range(layers)):
        if index < layers - 1:
            upper = upper * rates[index]
        o_ref[:, index] = back[index] + upper[None] * from_above


def exchange_kernel(count, layer_count, w_ref, ext_ref, probe_ref, out_ref, gathered, swept, send_sem, recv_sem, back_send, back_recv):
    me = lax.axis_index("layer")
    row = lax.axis_index("xs")
    layers = layer_count
    barrier = pltpu.get_barrier_semaphore()

    def greet(step, carry):
        pl.semaphore_signal(
            barrier, inc=1, device_id=(lax.rem(me + step, count), row), device_id_type=MESH
        )
        return carry

    lax.fori_loop(1, count, greet, 0)
    pl.semaphore_wait(barrier, count - 1)

    def outgoing(step, carry):
        target = lax.rem(me + step, count)
        pltpu.make_async_remote_copy(
            src_ref=ext_ref.at[target],
            dst_ref=gathered.at[me],
            send_sem=send_sem.at[step],
            recv_sem=recv_sem.at[step],
            device_id=(target, row),
            device_id_type=MESH,
        ).start()
        return carry

    lax.fori_loop(1, count, outgoing, 0)
    gathered[me] = ext_ref[me]

    def arrived(step, carry):
        copy = pltpu.make_async_remote_copy(
            src_ref=ext_ref.at[me],
            dst_ref=gathered.at[lax.rem(me + count - step, count)],
            send_sem=send_sem.at[step],
            recv_sem=recv_sem.at[step],
            device_id=(lax.rem(me + step, count), row),
            device_id_type=MESH,
        )
        copy.wait_send()
        copy.wait_recv()
        return carry

    lax.fori_loop(1, count, arrived, 0)

    rows_per_layer = out_ref.shape[1] // layers
    half = rows_per_layer // 2
    zero = jnp.zeros((rows_per_layer, out_ref.shape[2]), jnp.float32)
    data_rows = layers * half
    total = count * layers
    w0, w1, w2 = w_ref[0], w_ref[1], w_ref[2]

    def probe_at(place):
        inside = ((place >= 0) & (place < total)).astype(jnp.float32)
        place = jnp.clip(place, 0, total - 1)
        source = place // layers
        layer = place - source * layers
        return inside * probe_ref[source, pl.ds(layer * half, half), :]

    def prepare(source, carry):
        for layer in range(layers):
            place = source * layers + layer
            here = probe_ref[source, pl.ds(layer * half, half), :]
            partial = gathered[source, pl.ds(layer * half, half), :]
            second = (
                FAR * (probe_at(place - 2) + probe_at(place + 2))
                + NEAR * (probe_at(place - 1) + probe_at(place + 1))
                + CENTER * here
            )
            hamil = partial - 0.5 * second
            swept[source, pl.ds(layer * rows_per_layer, half), :] = w0 * hamil - w1 * here
            swept[source, pl.ds(layer * rows_per_layer + half, half), :] = w1 * hamil - w2 * here
        return carry

    lax.fori_loop(0, count, prepare, 0)

    def forward(source, state):
        for layer in range(layers):
            rate = gathered[source, pl.ds(data_rows + layer, 1), :]
            slab = swept[source, pl.ds(layer * rows_per_layer, rows_per_layer), :]
            state = rate * state + (1.0 - rate) * slab
            swept[source, pl.ds(layer * rows_per_layer, rows_per_layer), :] = state
        return state

    lax.fori_loop(0, count, forward, zero)

    def backward(step, state):
        source = count - 1 - step
        for layer in reversed(range(layers)):
            rate = gathered[source, pl.ds(data_rows + layer, 1), :]
            piece = pl.ds(layer * rows_per_layer, rows_per_layer)
            state = rate * state + (1.0 - rate) * swept[source, piece, :]
            swept[source, piece, :] = state
        return state

    lax.fori_loop(0, count, backward, zero)

    def returning(step, carry):
        target = lax.rem(me + step, count)
        pltpu.make_async_remote_copy(
            src_ref=swept.at[target],
            dst_ref=out_ref.at[me],
            send_sem=back_send.at[step],
            recv_sem=back_recv.at[step],
            device_id=(target, row),
            device_id_type=MESH,
        ).start()
        return carry

    lax.fori_loop(1, count, returning, 0)
    out_ref[me] = swept[me]

    def returned(step, carry):
        copy = pltpu.make_async_remote_copy(
            src_ref=swept.at[me],
            dst_ref=out_ref.at[lax.rem(me + count - step, count)],
            send_sem=back_send.at[step],
            recv_sem=back_recv.at[step],
            device_id=(lax.rem(me + step, count), row),
            device_id_type=MESH,
        )
        copy.wait_send()
        copy.wait_recv()
        return carry

    lax.fori_loop(1, count, returned, 0)


def sweeps(partial, gathered_probes, decay_rates, weights):
    layers, columns, width = partial.shape
    moments = 2
    count = lax.axis_size("layer")
    if columns != count:
        raise ValueError("columns")
    tiles = width // 128
    data_rows = layers * tiles
    padded_rows = -(-(data_rows + layers) // 8) * 8
    body = jnp.transpose(partial, (1, 0, 2)).reshape(columns, data_rows, 128)
    lanes = jnp.broadcast_to(jnp.transpose(decay_rates)[:, :, None], (columns, layers, 128))
    spare = jnp.zeros((columns, padded_rows - data_rows - layers, 128), jnp.float32)
    ext = jnp.concatenate([body, lanes, spare], axis=1)
    vmem = pl.BlockSpec(memory_space=pltpu.VMEM)
    out = pl.pallas_call(
        functools.partial(exchange_kernel, count, layers),
        out_shape=jax.ShapeDtypeStruct((columns, moments * data_rows, 128), jnp.float32),
        in_specs=[pl.BlockSpec(memory_space=pltpu.SMEM), vmem, vmem],
        out_specs=vmem,
        scratch_shapes=[
            pltpu.VMEM((count, padded_rows, 128), jnp.float32),
            pltpu.VMEM((count, moments * data_rows, 128), jnp.float32),
            pltpu.SemaphoreType.DMA((count,)),
            pltpu.SemaphoreType.DMA((count,)),
            pltpu.SemaphoreType.DMA((count,)),
            pltpu.SemaphoreType.DMA((count,)),
        ],
        compiler_params=pltpu.CompilerParams(collective_id=0, has_side_effects=True),
    )(weights, ext, gathered_probes)
    return jnp.transpose(out.reshape(columns, layers, moments, width), (1, 2, 0, 3))


def front_kernel(row_count, layer_count, block_ref, coef_ref, pieces_ref, left, right, total, regrouped,
                 gathered, send_sem, recv_sem, piece_send, piece_recv):
    me = lax.axis_index("layer")
    row = lax.axis_index("xs")
    peers = row_count - 1
    barrier = pltpu.get_barrier_semaphore()
    for step in range(1, row_count):
        pl.semaphore_signal(
            barrier, inc=1, device_id=(me, lax.rem(row + step, row_count)), device_id_type=MESH
        )

    def greet(step, carry):
        pl.semaphore_signal(
            barrier, inc=1, device_id=(lax.rem(me + step, layer_count), row), device_id_type=MESH
        )
        return carry

    lax.fori_loop(1, layer_count, greet, 0)
    pl.semaphore_wait(barrier, peers + layer_count - 1)

    def outgoing(step, carry):
        target = lax.rem(me + step, layer_count)
        pltpu.make_async_remote_copy(
            src_ref=pieces_ref.at[target],
            dst_ref=regrouped.at[me],
            send_sem=piece_send.at[step],
            recv_sem=piece_recv.at[step],
            device_id=(target, row),
            device_id_type=MESH,
        ).start()
        return carry

    copies = []
    targets = [
        (left, (me, lax.rem(row + 1, row_count))),
        (right, (me, lax.rem(row + row_count - 1, row_count))),
    ]
    for slot, (dst, device) in enumerate(targets):
        copies.append(
            pltpu.make_async_remote_copy(
                src_ref=block_ref, dst_ref=dst, send_sem=send_sem.at[slot], recv_sem=recv_sem.at[slot],
                device_id=device, device_id_type=MESH,
            )
        )
    for step in range(1, row_count):
        copies.append(
            pltpu.make_async_remote_copy(
                src_ref=coef_ref, dst_ref=gathered.at[step - 1], send_sem=send_sem.at[1 + step],
                recv_sem=recv_sem.at[1 + step], device_id=(me, lax.rem(row + step, row_count)),
                device_id_type=MESH,
            )
        )
    for copy in copies:
        copy.start()
    lax.fori_loop(1, layer_count, outgoing, 0)
    regrouped[me] = pieces_ref[me]
    for copy in copies[2:]:
        copy.wait()
    acc = coef_ref[...]
    for step in range(peers):
        acc = acc + gathered[step]
    total[...] = acc
    for copy in copies[:2]:
        copy.wait()

    def arrived(step, carry):
        copy = pltpu.make_async_remote_copy(
            src_ref=pieces_ref.at[me],
            dst_ref=regrouped.at[lax.rem(me + layer_count - step, layer_count)],
            send_sem=piece_send.at[step],
            recv_sem=piece_recv.at[step],
            device_id=(lax.rem(me + step, layer_count), row),
            device_id_type=MESH,
        )
        copy.wait_send()
        copy.wait_recv()
        return carry

    lax.fori_loop(1, layer_count, arrived, 0)


def front_exchange(block, coef):
    row_count = lax.axis_size("xs")
    layer_count = lax.axis_size("layer")
    layers, columns, width = block.shape
    pieces = jnp.transpose(block, (1, 0, 2)).reshape(columns, layers * width // 128, 128)
    spec = pl.BlockSpec(memory_space=pltpu.VMEM)
    return pl.pallas_call(
        functools.partial(front_kernel, row_count, layer_count),
        out_shape=[jax.ShapeDtypeStruct(block.shape, jnp.float32)] * 2
        + [jax.ShapeDtypeStruct(coef.shape, jnp.float32),
           jax.ShapeDtypeStruct((layer_count,) + pieces.shape[1:], jnp.float32)],
        in_specs=[spec, spec, spec],
        out_specs=[spec] * 4,
        scratch_shapes=[
            pltpu.VMEM((row_count - 1,) + coef.shape, jnp.float32),
            pltpu.SemaphoreType.DMA((1 + row_count,)),
            pltpu.SemaphoreType.DMA((1 + row_count,)),
            pltpu.SemaphoreType.DMA((layer_count,)),
            pltpu.SemaphoreType.DMA((layer_count,)),
        ],
        compiler_params=pltpu.CompilerParams(collective_id=1, has_side_effects=True),
    )(block, coef, pieces)


def shards(
    probes,
    potential,
    projector,
    intersection_ids,
    strength,
    decay_rates,
    contour_nodes,
    node_weights,
):
    layers, columns, rows, depth = probes.shape
    rounded = probes.astype(jnp.bfloat16).reshape(layers, columns, rows * depth)
    slot_coef = jnp.einsum("lsp,lcp->lsc", projector, rounded, preferred_element_type=jnp.float32)
    onehot = (intersection_ids[:, :, None] == jnp.arange(NPROJ, dtype=jnp.int32)).astype(
        jnp.float32
    )
    partial_coef = jnp.einsum("lsq,lsc->lcq", onehot, slot_coef, precision=lax.Precision.HIGHEST)
    left, right, coef, regrouped = front_exchange(
        probes.reshape(layers, columns, rows * depth), partial_coef
    )
    row = lax.axis_index("xs")
    left = jnp.where(row > 0, left, 0.0).reshape(probes.shape)
    right = jnp.where(row < lax.axis_size("xs") - 1, right, 0.0).reshape(probes.shape)
    beside = jnp.concatenate([left, probes, right], axis=2)
    across = jnp.pad(probes, ((0, 0), (0, 0), (0, 0), (2, 2)))
    laplace = second_along(beside, 2, rows)
    laplace = laplace + second_along(across, 3, depth)
    coef = jnp.swapaxes(coef, 1, 2)
    scaled = (strength[:, :, None] * coef).astype(jnp.bfloat16)
    slot_back = jnp.einsum(
        "lsq,lqc->lsc", onehot.astype(jnp.bfloat16), scaled, preferred_element_type=jnp.float32
    ).astype(jnp.bfloat16)
    projected = jnp.einsum(
        "lsp,lsc->lcp", projector, slot_back, preferred_element_type=jnp.float32
    ).reshape(layers, columns, rows, depth)
    partial = -0.5 * laplace + potential[:, None] * probes + projected
    weights = jnp.stack(
        [
            jnp.sum(node_weights),
            jnp.sum(node_weights * contour_nodes),
            jnp.sum(node_weights * contour_nodes * contour_nodes),
        ]
    )
    swept = sweeps(partial.reshape(layers, columns, rows * depth), regrouped, decay_rates, weights)
    return jnp.swapaxes(swept, 0, 1).reshape(2, layers, columns, rows, depth)


def solution(mesh):
    in_specs = (
        P("layer", None, "xs", None),
        P("layer", "xs", None),
        P("layer", "xs", None),
        P("layer", "xs"),
        P("layer", None),
        P("layer", None),
        P(),
        P(),
    )
    out_specs = P(None, "layer", None, "xs", None)
    return jax.shard_map(shards, mesh=mesh, in_specs=in_specs, out_specs=out_specs, check_vma=False)
```

```python
import functools

import jax
import jax.numpy as jnp
from jax import lax
from jax.experimental import pallas as pl
from jax.experimental.pallas import tpu as pltpu
from jax.sharding import PartitionSpec as P

NPROJ = 256


FAR = -1.0 / 12.0
NEAR = 4.0 / 3.0
CENTER = -2.5


def with_halo(cells, sides, width):
    for axis, dim in sides:
        count = lax.axis_size(axis)
        ends = count - 1
        head = lax.slice_in_dim(cells, 0, width, axis=dim)
        tail = lax.slice_in_dim(cells, cells.shape[dim] - width, cells.shape[dim], axis=dim)
        cells = jnp.concatenate(
            [
                lax.ppermute(tail, axis, [(i, (i + 1) % count) for i in range(ends)]),
                cells,
                lax.ppermute(head, axis, [((i + 1) % count, i) for i in range(ends)]),
            ],
            axis=dim,
        )
    return cells


def second_along(padded, axis, count):

    def piece(offset):
        return lax.slice_in_dim(padded, 2 + offset, 2 + offset + count, axis=axis)

    return FAR * (piece(-2) + piece(2)) + NEAR * (piece(-1) + piece(1)) + CENTER * piece(0)


MESH = pl.DeviceIdType.MESH


def spans_of(count):
    spans = []
    span = 1
    while 2 * span < count:
        spans.append(span)
        span *= 2
    return spans, span + 1


def sweep_kernel(count, f_ref, d_ref, o_ref, state, landed, send_sem, recv_sem):
    me = lax.axis_index("layer")
    row = lax.axis_index("xs")
    layers = f_ref.shape[1]
    width = f_ref.shape[3]
    spans, far = spans_of(count)
    hops = spans + [1, far]
    barrier = pltpu.get_barrier_semaphore()
    for hop in hops:
        for sign in (1, -1):
            pl.semaphore_signal(
                barrier, inc=1, device_id=(lax.rem(me + sign * hop + count, count), row),
                device_id_type=MESH,
            )
    pl.semaphore_wait(barrier, 2 * len(hops))

    rates = [d_ref[index] for index in range(layers)]
    through = rates[0]
    for index in range(1, layers):
        through = through * rates[index]

    def put(direction, slot, ends, keep):
        state[direction, slot, :, :, :width] = ends
        state[direction, slot, :, :, width:] = jnp.broadcast_to(keep[None], (2,) + keep.shape[:1] + (128,))

    def send(direction, slot, target_slot, hop, sign):
        copy = pltpu.make_async_remote_copy(
            src_ref=state.at[direction, slot],
            dst_ref=landed.at[direction, target_slot],
            send_sem=send_sem.at[direction, target_slot],
            recv_sem=recv_sem.at[direction, target_slot],
            device_id=(lax.rem(me + sign * hop + count, count), row),
            device_id_type=MESH,
        )
        copy.start()
        return copy

    def scan(direction, ends, sign):
        put(direction, 0, ends, through)
        for slot, hop in enumerate(spans):
            send(direction, slot, slot, hop, sign).wait()
            source = me - hop if sign == 1 else me + hop
            valid = ((source >= 0) & (source < count)).astype(jnp.float32)
            mine = state[direction, slot]
            got = landed[direction, slot]
            keep = mine[0, :, width:width + 1]
            put(
                direction, slot + 1,
                mine[:, :, :width] + (valid * keep)[None] * got[:, :, :width],
                keep * (valid * got[0, :, width:width + 1]),
            )
        last = len(spans)
        near = send(direction, last, last, 1, sign)
        distant = send(direction, last, last + 1, far, sign)
        near.wait()
        distant.wait()
        near_source = me - 1 if sign == 1 else me + 1
        far_source = me - far if sign == 1 else me + far
        near_valid = ((near_source >= 0) & (near_source < count)).astype(jnp.float32)
        far_valid = ((far_source >= 0) & (far_source < count)).astype(jnp.float32)
        got = landed[direction, last]
        result = got[:, :, :width]
        if far < count:
            result = result + (far_valid * got[0, :, width:width + 1])[None] * landed[direction, last + 1, :, :, :width]
        return near_valid * result

    state_now = None
    ahead = []
    for index in range(layers):
        source = f_ref[:, index]
        if state_now is None:
            state_now = (1.0 - rates[index])[None] * source
        else:
            state_now = rates[index][None] * state_now + (1.0 - rates[index])[None] * source
        ahead.append(state_now)
    entering = scan(0, state_now, 1)
    lower = rates[0]
    for index in range(layers):
        if index > 0:
            lower = lower * rates[index]
        ahead[index] = ahead[index] + lower[None] * entering
    state_now = None
    back = [None] * layers
    for index in reversed(range(layers)):
        if state_now is None:
            state_now = (1.0 - rates[index])[None] * ahead[index]
        else:
            state_now = rates[index][None] * state_now + (1.0 - rates[index])[None] * ahead[index]
        back[index] = state_now
    from_above = scan(1, state_now, -1)
    upper = rates[layers - 1]
    for index in reversed(range(layers)):
        if index < layers - 1:
            upper = upper * rates[index]
        o_ref[:, index] = back[index] + upper[None] * from_above


def exchange_kernel(count, layer_count, w_ref, ext_ref, probe_ref, out_ref, gathered, swept, send_sem, recv_sem, back_send, back_recv):
    me = lax.axis_index("layer")
    row = lax.axis_index("xs")
    layers = layer_count
    barrier = pltpu.get_barrier_semaphore()

    def greet(step, carry):
        pl.semaphore_signal(
            barrier, inc=1, device_id=(lax.rem(me + step, count), row), device_id_type=MESH
        )
        return carry

    lax.fori_loop(1, count, greet, 0)
    pl.semaphore_wait(barrier, count - 1)

    def outgoing(step, carry):
        target = lax.rem(me + step, count)
        pltpu.make_async_remote_copy(
            src_ref=ext_ref.at[target],
            dst_ref=gathered.at[me],
            send_sem=send_sem.at[step],
            recv_sem=recv_sem.at[step],
            device_id=(target, row),
            device_id_type=MESH,
        ).start()
        return carry

    lax.fori_loop(1, count, outgoing, 0)
    gathered[me] = ext_ref[me]

    def arrived(step, carry):
        copy = pltpu.make_async_remote_copy(
            src_ref=ext_ref.at[me],
            dst_ref=gathered.at[lax.rem(me + count - step, count)],
            send_sem=send_sem.at[step],
            recv_sem=recv_sem.at[step],
            device_id=(lax.rem(me + step, count), row),
            device_id_type=MESH,
        )
        copy.wait_send()
        copy.wait_recv()
        return carry

    lax.fori_loop(1, count, arrived, 0)

    half = out_ref.shape[3]
    rows_per_layer = 2 * half
    zero = jnp.zeros((half, out_ref.shape[4]), jnp.float32)
    data_rows = layers * half
    total = count * layers
    w0, w1, w2 = w_ref[0], w_ref[1], w_ref[2]

    def probe_at(place):
        inside = ((place >= 0) & (place < total)).astype(jnp.float32)
        place = jnp.clip(place, 0, total - 1)
        source = place // layers
        layer = place - source * layers
        return inside * probe_ref[source, pl.ds(layer * half, half), :]

    def prepare(source, carry):
        for layer in range(layers):
            place = source * layers + layer
            here = probe_ref[source, pl.ds(layer * half, half), :]
            partial = gathered[source, pl.ds(layer * half, half), :]
            second = (
                FAR * (probe_at(place - 2) + probe_at(place + 2))
                + NEAR * (probe_at(place - 1) + probe_at(place + 1))
                + CENTER * here
            )
            hamil = partial - 0.5 * second
            swept[source, 0, layer] = w0 * hamil - w1 * here
            swept[source, 1, layer] = w1 * hamil - w2 * here
        return carry

    lax.fori_loop(0, count, prepare, 0)

    def forward(source, state):
        for layer in range(layers):
            rate = gathered[source, pl.ds(data_rows + layer, 1), :]
            state = tuple(
                rate * state[m] + (1.0 - rate) * swept[source, m, layer] for m in range(2)
            )
            for m in range(2):
                swept[source, m, layer] = state[m]
        return state

    lax.fori_loop(0, count, forward, (zero, zero))

    def backward(step, state):
        source = count - 1 - step
        for layer in reversed(range(layers)):
            rate = gathered[source, pl.ds(data_rows + layer, 1), :]
            state = tuple(
                rate * state[m] + (1.0 - rate) * swept[source, m, layer] for m in range(2)
            )
            for m in range(2):
                swept[source, m, layer] = state[m]
        return state

    lax.fori_loop(0, count, backward, (zero, zero))

    def returning(step, carry):
        target = lax.rem(me + step, count)
        pltpu.make_async_remote_copy(
            src_ref=swept.at[target],
            dst_ref=out_ref.at[:, :, me],
            send_sem=back_send.at[step],
            recv_sem=back_recv.at[step],
            device_id=(target, row),
            device_id_type=MESH,
        ).start()
        return carry

    lax.fori_loop(1, count, returning, 0)
    out_ref[:, :, me] = swept[me]

    def returned(step, carry):
        copy = pltpu.make_async_remote_copy(
            src_ref=swept.at[me],
            dst_ref=out_ref.at[:, :, lax.rem(me + count - step, count)],
            send_sem=back_send.at[step],
            recv_sem=back_recv.at[step],
            device_id=(lax.rem(me + step, count), row),
            device_id_type=MESH,
        )
        copy.wait_send()
        copy.wait_recv()
        return carry

    lax.fori_loop(1, count, returned, 0)


def sweeps(partial, gathered_probes, decay_rates, weights):
    layers, columns, width = partial.shape
    moments = 2
    count = lax.axis_size("layer")
    if columns != count:
        raise ValueError("columns")
    tiles = width // 128
    data_rows = layers * tiles
    padded_rows = -(-(data_rows + layers) // 8) * 8
    body = jnp.transpose(partial, (1, 0, 2)).reshape(columns, data_rows, 128)
    lanes = jnp.broadcast_to(jnp.transpose(decay_rates)[:, :, None], (columns, layers, 128))
    spare = jnp.zeros((columns, padded_rows - data_rows - layers, 128), jnp.float32)
    ext = jnp.concatenate([body, lanes, spare], axis=1)
    vmem = pl.BlockSpec(memory_space=pltpu.VMEM)
    out = pl.pallas_call(
        functools.partial(exchange_kernel, count, layers),
        out_shape=jax.ShapeDtypeStruct((moments, layers, columns, tiles, 128), jnp.float32),
        in_specs=[pl.BlockSpec(memory_space=pltpu.SMEM), vmem, vmem],
        out_specs=vmem,
        scratch_shapes=[
            pltpu.VMEM((count, padded_rows, 128), jnp.float32),
            pltpu.VMEM((count, moments, layers, tiles, 128), jnp.float32),
            pltpu.SemaphoreType.DMA((count,)),
            pltpu.SemaphoreType.DMA((count,)),
            pltpu.SemaphoreType.DMA((count,)),
            pltpu.SemaphoreType.DMA((count,)),
        ],
        compiler_params=pltpu.CompilerParams(collective_id=0, has_side_effects=True),
    )(weights, ext, gathered_probes)
    return out.reshape(moments, layers, columns, width)


def front_kernel(row_count, layer_count, block_ref, coef_ref, pieces_ref, left, right, total, regrouped,
                 gathered, send_sem, recv_sem, piece_send, piece_recv):
    me = lax.axis_index("layer")
    row = lax.axis_index("xs")
    peers = row_count - 1
    barrier = pltpu.get_barrier_semaphore()
    for step in range(1, row_count):
        pl.semaphore_signal(
            barrier, inc=1, device_id=(me, lax.rem(row + step, row_count)), device_id_type=MESH
        )

    def greet(step, carry):
        pl.semaphore_signal(
            barrier, inc=1, device_id=(lax.rem(me + step, layer_count), row), device_id_type=MESH
        )
        return carry

    lax.fori_loop(1, layer_count, greet, 0)
    pl.semaphore_wait(barrier, peers + layer_count - 1)

    def outgoing(step, carry):
        target = lax.rem(me + step, layer_count)
        pltpu.make_async_remote_copy(
            src_ref=pieces_ref.at[target],
            dst_ref=regrouped.at[me],
            send_sem=piece_send.at[step],
            recv_sem=piece_recv.at[step],
            device_id=(target, row),
            device_id_type=MESH,
        ).start()
        return carry

    copies = []
    targets = [
        (left, (me, lax.rem(row + 1, row_count))),
        (right, (me, lax.rem(row + row_count - 1, row_count))),
    ]
    for slot, (dst, device) in enumerate(targets):
        copies.append(
            pltpu.make_async_remote_copy(
                src_ref=block_ref, dst_ref=dst, send_sem=send_sem.at[slot], recv_sem=recv_sem.at[slot],
                device_id=device, device_id_type=MESH,
            )
        )
    for step in range(1, row_count):
        copies.append(
            pltpu.make_async_remote_copy(
                src_ref=coef_ref, dst_ref=gathered.at[step - 1], send_sem=send_sem.at[1 + step],
                recv_sem=recv_sem.at[1 + step], device_id=(me, lax.rem(row + step, row_count)),
                device_id_type=MESH,
            )
        )
    for copy in copies:
        copy.start()
    lax.fori_loop(1, layer_count, outgoing, 0)
    regrouped[me] = pieces_ref[me]
    for copy in copies[2:]:
        copy.wait()
    acc = coef_ref[...]
    for step in range(peers):
        acc = acc + gathered[step]
    total[...] = acc
    for copy in copies[:2]:
        copy.wait()

    def arrived(step, carry):
        copy = pltpu.make_async_remote_copy(
            src_ref=pieces_ref.at[me],
            dst_ref=regrouped.at[lax.rem(me + layer_count - step, layer_count)],
            send_sem=piece_send.at[step],
            recv_sem=piece_recv.at[step],
            device_id=(lax.rem(me + step, layer_count), row),
            device_id_type=MESH,
        )
        copy.wait_send()
        copy.wait_recv()
        return carry

    lax.fori_loop(1, layer_count, arrived, 0)


def front_exchange(block, coef):
    row_count = lax.axis_size("xs")
    layer_count = lax.axis_size("layer")
    layers, columns, width = block.shape
    pieces = jnp.transpose(block, (1, 0, 2)).reshape(columns, layers * width // 128, 128)
    spec = pl.BlockSpec(memory_space=pltpu.VMEM)
    return pl.pallas_call(
        functools.partial(front_kernel, row_count, layer_count),
        out_shape=[jax.ShapeDtypeStruct(block.shape, jnp.float32)] * 2
        + [jax.ShapeDtypeStruct(coef.shape, jnp.float32),
           jax.ShapeDtypeStruct((layer_count,) + pieces.shape[1:], jnp.float32)],
        in_specs=[spec, spec, spec],
        out_specs=[spec] * 4,
        scratch_shapes=[
            pltpu.VMEM((row_count - 1,) + coef.shape, jnp.float32),
            pltpu.SemaphoreType.DMA((1 + row_count,)),
            pltpu.SemaphoreType.DMA((1 + row_count,)),
            pltpu.SemaphoreType.DMA((layer_count,)),
            pltpu.SemaphoreType.DMA((layer_count,)),
        ],
        compiler_params=pltpu.CompilerParams(collective_id=1, has_side_effects=True),
    )(block, coef, pieces)


def shards(
    probes,
    potential,
    projector,
    intersection_ids,
    strength,
    decay_rates,
    contour_nodes,
    node_weights,
):
    layers, columns, rows, depth = probes.shape
    rounded = probes.astype(jnp.bfloat16).reshape(layers, columns, rows * depth)
    slot_coef = jnp.einsum("lsp,lcp->lsc", projector, rounded, preferred_element_type=jnp.float32)
    onehot = (intersection_ids[:, :, None] == jnp.arange(NPROJ, dtype=jnp.int32)).astype(
        jnp.float32
    )
    partial_coef = jnp.einsum("lsq,lsc->lcq", onehot, slot_coef, precision=lax.Precision.HIGHEST)
    left, right, coef, regrouped = front_exchange(
        probes.reshape(layers, columns, rows * depth), partial_coef
    )
    row = lax.axis_index("xs")
    left = jnp.where(row > 0, left, 0.0).reshape(probes.shape)
    right = jnp.where(row < lax.axis_size("xs") - 1, right, 0.0).reshape(probes.shape)
    beside = jnp.concatenate([left, probes, right], axis=2)
    across = jnp.pad(probes, ((0, 0), (0, 0), (0, 0), (2, 2)))
    laplace = second_along(beside, 2, rows)
    laplace = laplace + second_along(across, 3, depth)
    coef = jnp.swapaxes(coef, 1, 2)
    scaled = (strength[:, :, None] * coef).astype(jnp.bfloat16)
    slot_back = jnp.einsum(
        "lsq,lqc->lsc", onehot.astype(jnp.bfloat16), scaled, preferred_element_type=jnp.float32
    ).astype(jnp.bfloat16)
    projected = jnp.einsum(
        "lsp,lsc->lcp", projector, slot_back, preferred_element_type=jnp.float32
    ).reshape(layers, columns, rows, depth)
    partial = -0.5 * laplace + potential[:, None] * probes + projected
    weights = jnp.stack(
        [
            jnp.sum(node_weights),
            jnp.sum(node_weights * contour_nodes),
            jnp.sum(node_weights * contour_nodes * contour_nodes),
        ]
    )
    swept = sweeps(partial.reshape(layers, columns, rows * depth), regrouped, decay_rates, weights)
    return swept.reshape(2, layers, columns, rows, depth)


def solution(mesh):
    in_specs = (
        P("layer", None, "xs", None),
        P("layer", "xs", None),
        P("layer", "xs", None),
        P("layer", "xs"),
        P("layer", None),
        P("layer", None),
        P(),
        P(),
    )
    out_specs = P(None, "layer", None, "xs", None)
    return jax.shard_map(shards, mesh=mesh, in_specs=in_specs, out_specs=out_specs, check_vma=False)
```

```python
import functools

import jax
import jax.numpy as jnp
from jax import lax
from jax.experimental import pallas as pl
from jax.experimental.pallas import tpu as pltpu
from jax.sharding import PartitionSpec as P

NPROJ = 256


FAR = -1.0 / 12.0
NEAR = 4.0 / 3.0
CENTER = -2.5


def with_halo(cells, sides, width):
    for axis, dim in sides:
        count = lax.axis_size(axis)
        ends = count - 1
        head = lax.slice_in_dim(cells, 0, width, axis=dim)
        tail = lax.slice_in_dim(cells, cells.shape[dim] - width, cells.shape[dim], axis=dim)
        cells = jnp.concatenate(
            [
                lax.ppermute(tail, axis, [(i, (i + 1) % count) for i in range(ends)]),
                cells,
                lax.ppermute(head, axis, [((i + 1) % count, i) for i in range(ends)]),
            ],
            axis=dim,
        )
    return cells


def second_along(padded, axis, count):

    def piece(offset):
        return lax.slice_in_dim(padded, 2 + offset, 2 + offset + count, axis=axis)

    return FAR * (piece(-2) + piece(2)) + NEAR * (piece(-1) + piece(1)) + CENTER * piece(0)


MESH = pl.DeviceIdType.MESH


def spans_of(count):
    spans = []
    span = 1
    while 2 * span < count:
        spans.append(span)
        span *= 2
    return spans, span + 1


def sweep_kernel(count, f_ref, d_ref, o_ref, state, landed, send_sem, recv_sem):
    me = lax.axis_index("layer")
    row = lax.axis_index("xs")
    layers = f_ref.shape[1]
    width = f_ref.shape[3]
    spans, far = spans_of(count)
    hops = spans + [1, far]
    barrier = pltpu.get_barrier_semaphore()
    for hop in hops:
        for sign in (1, -1):
            pl.semaphore_signal(
                barrier, inc=1, device_id=(lax.rem(me + sign * hop + count, count), row),
                device_id_type=MESH,
            )
    pl.semaphore_wait(barrier, 2 * len(hops))

    rates = [d_ref[index] for index in range(layers)]
    through = rates[0]
    for index in range(1, layers):
        through = through * rates[index]

    def put(direction, slot, ends, keep):
        state[direction, slot, :, :, :width] = ends
        state[direction, slot, :, :, width:] = jnp.broadcast_to(keep[None], (2,) + keep.shape[:1] + (128,))

    def send(direction, slot, target_slot, hop, sign):
        copy = pltpu.make_async_remote_copy(
            src_ref=state.at[direction, slot],
            dst_ref=landed.at[direction, target_slot],
            send_sem=send_sem.at[direction, target_slot],
            recv_sem=recv_sem.at[direction, target_slot],
            device_id=(lax.rem(me + sign * hop + count, count), row),
            device_id_type=MESH,
        )
        copy.start()
        return copy

    def scan(direction, ends, sign):
        put(direction, 0, ends, through)
        for slot, hop in enumerate(spans):
            send(direction, slot, slot, hop, sign).wait()
            source = me - hop if sign == 1 else me + hop
            valid = ((source >= 0) & (source < count)).astype(jnp.float32)
            mine = state[direction, slot]
            got = landed[direction, slot]
            keep = mine[0, :, width:width + 1]
            put(
                direction, slot + 1,
                mine[:, :, :width] + (valid * keep)[None] * got[:, :, :width],
                keep * (valid * got[0, :, width:width + 1]),
            )
        last = len(spans)
        near = send(direction, last, last, 1, sign)
        distant = send(direction, last, last + 1, far, sign)
        near.wait()
        distant.wait()
        near_source = me - 1 if sign == 1 else me + 1
        far_source = me - far if sign == 1 else me + far
        near_valid = ((near_source >= 0) & (near_source < count)).astype(jnp.float32)
        far_valid = ((far_source >= 0) & (far_source < count)).astype(jnp.float32)
        got = landed[direction, last]
        result = got[:, :, :width]
        if far < count:
            result = result + (far_valid * got[0, :, width:width + 1])[None] * landed[direction, last + 1, :, :, :width]
        return near_valid * result

    state_now = None
    ahead = []
    for index in range(layers):
        source = f_ref[:, index]
        if state_now is None:
            state_now = (1.0 - rates[index])[None] * source
        else:
            state_now = rates[index][None] * state_now + (1.0 - rates[index])[None] * source
        ahead.append(state_now)
    entering = scan(0, state_now, 1)
    lower = rates[0]
    for index in range(layers):
        if index > 0:
            lower = lower * rates[index]
        ahead[index] = ahead[index] + lower[None] * entering
    state_now = None
    back = [None] * layers
    for index in reversed(range(layers)):
        if state_now is None:
            state_now = (1.0 - rates[index])[None] * ahead[index]
        else:
            state_now = rates[index][None] * state_now + (1.0 - rates[index])[None] * ahead[index]
        back[index] = state_now
    from_above = scan(1, state_now, -1)
    upper = rates[layers - 1]
    for index in reversed(range(layers)):
        if index < layers - 1:
            upper = upper * rates[index]
        o_ref[:, index] = back[index] + upper[None] * from_above


def exchange_kernel(count, layer_count, nodes_ref, weights_ref, ext_ref, probe_ref, out_ref, gathered, swept, send_sem, recv_sem, back_send, back_recv):
    me = lax.axis_index("layer")
    row = lax.axis_index("xs")
    layers = layer_count
    barrier = pltpu.get_barrier_semaphore()

    def greet(step, carry):
        pl.semaphore_signal(
            barrier, inc=1, device_id=(lax.rem(me + step, count), row), device_id_type=MESH
        )
        return carry

    lax.fori_loop(1, count, greet, 0)
    pl.semaphore_wait(barrier, count - 1)

    def outgoing(step, carry):
        target = lax.rem(me + step, count)
        pltpu.make_async_remote_copy(
            src_ref=ext_ref.at[target],
            dst_ref=gathered.at[me],
            send_sem=send_sem.at[step],
            recv_sem=recv_sem.at[step],
            device_id=(target, row),
            device_id_type=MESH,
        ).start()
        return carry

    lax.fori_loop(1, count, outgoing, 0)
    gathered[me] = ext_ref[me]

    def arrived(step, carry):
        copy = pltpu.make_async_remote_copy(
            src_ref=ext_ref.at[me],
            dst_ref=gathered.at[lax.rem(me + count - step, count)],
            send_sem=send_sem.at[step],
            recv_sem=recv_sem.at[step],
            device_id=(lax.rem(me + step, count), row),
            device_id_type=MESH,
        )
        copy.wait_send()
        copy.wait_recv()
        return carry

    lax.fori_loop(1, count, arrived, 0)

    half = out_ref.shape[3]
    rows_per_layer = 2 * half
    zero = jnp.zeros((half, out_ref.shape[4]), jnp.float32)
    data_rows = layers * half
    total = count * layers
    w0 = w1 = w2 = None
    for node in range(nodes_ref.shape[0]):
        weight = weights_ref[node]
        scaled = weight * nodes_ref[node]
        if w0 is None:
            w0, w1, w2 = weight, scaled, scaled * nodes_ref[node]
        else:
            w0, w1, w2 = w0 + weight, w1 + scaled, w2 + scaled * nodes_ref[node]

    def probe_at(place):
        inside = ((place >= 0) & (place < total)).astype(jnp.float32)
        place = jnp.clip(place, 0, total - 1)
        source = place // layers
        layer = place - source * layers
        return inside * probe_ref[source, pl.ds(layer * half, half), :]

    def prepare(source, carry):
        for layer in range(layers):
            place = source * layers + layer
            here = probe_ref[source, pl.ds(layer * half, half), :]
            partial = gathered[source, pl.ds(layer * half, half), :]
            second = (
                FAR * (probe_at(place - 2) + probe_at(place + 2))
                + NEAR * (probe_at(place - 1) + probe_at(place + 1))
                + CENTER * here
            )
            hamil = partial - 0.5 * second
            swept[source, 0, layer] = w0 * hamil - w1 * here
            swept[source, 1, layer] = w1 * hamil - w2 * here
        return carry

    lax.fori_loop(0, count, prepare, 0)

    def forward(source, state):
        for layer in range(layers):
            rate = gathered[source, pl.ds(data_rows + layer, 1), :]
            state = tuple(
                rate * state[m] + (1.0 - rate) * swept[source, m, layer] for m in range(2)
            )
            for m in range(2):
                swept[source, m, layer] = state[m]
        return state

    lax.fori_loop(0, count, forward, (zero, zero))

    def backward(step, state):
        source = count - 1 - step
        for layer in reversed(range(layers)):
            rate = gathered[source, pl.ds(data_rows + layer, 1), :]
            state = tuple(
                rate * state[m] + (1.0 - rate) * swept[source, m, layer] for m in range(2)
            )
            for m in range(2):
                swept[source, m, layer] = state[m]
        return state

    lax.fori_loop(0, count, backward, (zero, zero))

    def returning(step, carry):
        target = lax.rem(me + step, count)
        pltpu.make_async_remote_copy(
            src_ref=swept.at[target],
            dst_ref=out_ref.at[:, :, me],
            send_sem=back_send.at[step],
            recv_sem=back_recv.at[step],
            device_id=(target, row),
            device_id_type=MESH,
        ).start()
        return carry

    lax.fori_loop(1, count, returning, 0)
    out_ref[:, :, me] = swept[me]

    def returned(step, carry):
        copy = pltpu.make_async_remote_copy(
            src_ref=swept.at[me],
            dst_ref=out_ref.at[:, :, lax.rem(me + count - step, count)],
            send_sem=back_send.at[step],
            recv_sem=back_recv.at[step],
            device_id=(lax.rem(me + step, count), row),
            device_id_type=MESH,
        )
        copy.wait_send()
        copy.wait_recv()
        return carry

    lax.fori_loop(1, count, returned, 0)


def sweeps(partial, gathered_probes, decay_rates, nodes, weights):
    layers, columns, width = partial.shape
    moments = 2
    count = lax.axis_size("layer")
    if columns != count:
        raise ValueError("columns")
    tiles = width // 128
    data_rows = layers * tiles
    padded_rows = -(-(data_rows + layers) // 8) * 8
    body = jnp.transpose(partial, (1, 0, 2)).reshape(columns, data_rows, 128)
    lanes = jnp.broadcast_to(jnp.transpose(decay_rates)[:, :, None], (columns, layers, 128))
    spare = jnp.zeros((columns, padded_rows - data_rows - layers, 128), jnp.float32)
    ext = jnp.concatenate([body, lanes, spare], axis=1)
    vmem = pl.BlockSpec(memory_space=pltpu.VMEM)
    out = pl.pallas_call(
        functools.partial(exchange_kernel, count, layers),
        out_shape=jax.ShapeDtypeStruct((moments, layers, columns, tiles, 128), jnp.float32),
        in_specs=[pl.BlockSpec(memory_space=pltpu.SMEM)] * 2 + [vmem, vmem],
        out_specs=vmem,
        scratch_shapes=[
            pltpu.VMEM((count, padded_rows, 128), jnp.float32),
            pltpu.VMEM((count, moments, layers, tiles, 128), jnp.float32),
            pltpu.SemaphoreType.DMA((count,)),
            pltpu.SemaphoreType.DMA((count,)),
            pltpu.SemaphoreType.DMA((count,)),
            pltpu.SemaphoreType.DMA((count,)),
        ],
        compiler_params=pltpu.CompilerParams(collective_id=0, has_side_effects=True),
    )(nodes, weights, ext, gathered_probes)
    return out.reshape(moments, layers, columns, width)


def front_kernel(row_count, layer_count, block_ref, coef_ref, pieces_ref, left, right, total, regrouped,
                 gathered, send_sem, recv_sem, piece_send, piece_recv):
    me = lax.axis_index("layer")
    row = lax.axis_index("xs")
    peers = row_count - 1
    barrier = pltpu.get_barrier_semaphore()
    for step in range(1, row_count):
        pl.semaphore_signal(
            barrier, inc=1, device_id=(me, lax.rem(row + step, row_count)), device_id_type=MESH
        )

    def greet(step, carry):
        pl.semaphore_signal(
            barrier, inc=1, device_id=(lax.rem(me + step, layer_count), row), device_id_type=MESH
        )
        return carry

    lax.fori_loop(1, layer_count, greet, 0)
    pl.semaphore_wait(barrier, peers + layer_count - 1)

    def outgoing(step, carry):
        target = lax.rem(me + step, layer_count)
        pltpu.make_async_remote_copy(
            src_ref=pieces_ref.at[target],
            dst_ref=regrouped.at[me],
            send_sem=piece_send.at[step],
            recv_sem=piece_recv.at[step],
            device_id=(target, row),
            device_id_type=MESH,
        ).start()
        return carry

    copies = []
    targets = [
        (left, (me, lax.rem(row + 1, row_count))),
        (right, (me, lax.rem(row + row_count - 1, row_count))),
    ]
    for slot, (dst, device) in enumerate(targets):
        copies.append(
            pltpu.make_async_remote_copy(
                src_ref=block_ref, dst_ref=dst, send_sem=send_sem.at[slot], recv_sem=recv_sem.at[slot],
                device_id=device, device_id_type=MESH,
            )
        )
    for step in range(1, row_count):
        copies.append(
            pltpu.make_async_remote_copy(
                src_ref=coef_ref, dst_ref=gathered.at[step - 1], send_sem=send_sem.at[1 + step],
                recv_sem=recv_sem.at[1 + step], device_id=(me, lax.rem(row + step, row_count)),
                device_id_type=MESH,
            )
        )
    for copy in copies:
        copy.start()
    lax.fori_loop(1, layer_count, outgoing, 0)
    regrouped[me] = pieces_ref[me]
    for copy in copies[2:]:
        copy.wait()
    acc = coef_ref[...]
    for step in range(peers):
        acc = acc + gathered[step]
    total[...] = acc
    for copy in copies[:2]:
        copy.wait()
    left[...] = left[...] * (row > 0).astype(jnp.float32)
    right[...] = right[...] * (row < row_count - 1).astype(jnp.float32)

    def arrived(step, carry):
        copy = pltpu.make_async_remote_copy(
            src_ref=pieces_ref.at[me],
            dst_ref=regrouped.at[lax.rem(me + layer_count - step, layer_count)],
            send_sem=piece_send.at[step],
            recv_sem=piece_recv.at[step],
            device_id=(lax.rem(me + step, layer_count), row),
            device_id_type=MESH,
        )
        copy.wait_send()
        copy.wait_recv()
        return carry

    lax.fori_loop(1, layer_count, arrived, 0)


def front_exchange(block, coef):
    row_count = lax.axis_size("xs")
    layer_count = lax.axis_size("layer")
    layers, columns, width = block.shape
    pieces = jnp.transpose(block, (1, 0, 2)).reshape(columns, layers * width // 128, 128)
    spec = pl.BlockSpec(memory_space=pltpu.VMEM)
    return pl.pallas_call(
        functools.partial(front_kernel, row_count, layer_count),
        out_shape=[jax.ShapeDtypeStruct(block.shape, jnp.float32)] * 2
        + [jax.ShapeDtypeStruct(coef.shape, jnp.float32),
           jax.ShapeDtypeStruct((layer_count,) + pieces.shape[1:], jnp.float32)],
        in_specs=[spec, spec, spec],
        out_specs=[spec] * 4,
        scratch_shapes=[
            pltpu.VMEM((row_count - 1,) + coef.shape, jnp.float32),
            pltpu.SemaphoreType.DMA((1 + row_count,)),
            pltpu.SemaphoreType.DMA((1 + row_count,)),
            pltpu.SemaphoreType.DMA((layer_count,)),
            pltpu.SemaphoreType.DMA((layer_count,)),
        ],
        compiler_params=pltpu.CompilerParams(collective_id=1, has_side_effects=True),
    )(block, coef, pieces)


def shards(
    probes,
    potential,
    projector,
    intersection_ids,
    strength,
    decay_rates,
    contour_nodes,
    node_weights,
):
    layers, columns, rows, depth = probes.shape
    rounded = probes.astype(jnp.bfloat16).reshape(layers, columns, rows * depth)
    slot_coef = jnp.einsum("lsp,lcp->lsc", projector, rounded, preferred_element_type=jnp.float32)
    onehot = (intersection_ids[:, :, None] == jnp.arange(NPROJ, dtype=jnp.int32)).astype(
        jnp.float32
    )
    partial_coef = jnp.einsum("lsq,lsc->lcq", onehot, slot_coef, precision=lax.Precision.HIGHEST)
    left, right, coef, regrouped = front_exchange(
        probes.reshape(layers, columns, rows * depth), partial_coef
    )
    left = left.reshape(probes.shape)
    right = right.reshape(probes.shape)
    beside = jnp.concatenate([left, probes, right], axis=2)
    across = jnp.pad(probes, ((0, 0), (0, 0), (0, 0), (2, 2)))
    laplace = second_along(beside, 2, rows)
    laplace = laplace + second_along(across, 3, depth)
    coef = jnp.swapaxes(coef, 1, 2)
    scaled = (strength[:, :, None] * coef).astype(jnp.bfloat16)
    slot_back = jnp.einsum(
        "lsq,lqc->lsc", onehot.astype(jnp.bfloat16), scaled, preferred_element_type=jnp.float32
    ).astype(jnp.bfloat16)
    projected = jnp.einsum(
        "lsp,lsc->lcp", projector, slot_back, preferred_element_type=jnp.float32
    ).reshape(layers, columns, rows, depth)
    partial = -0.5 * laplace + potential[:, None] * probes + projected
    swept = sweeps(
        partial.reshape(layers, columns, rows * depth), regrouped, decay_rates, contour_nodes,
        node_weights,
    )
    return swept.reshape(2, layers, columns, rows, depth)


def solution(mesh):
    in_specs = (
        P("layer", None, "xs", None),
        P("layer", "xs", None),
        P("layer", "xs", None),
        P("layer", "xs"),
        P("layer", None),
        P("layer", None),
        P(),
        P(),
    )
    out_specs = P(None, "layer", None, "xs", None)
    return jax.shard_map(shards, mesh=mesh, in_specs=in_specs, out_specs=out_specs, check_vma=False)
```

```python
import functools

import jax
import jax.numpy as jnp
from jax import lax
from jax.experimental import pallas as pl
from jax.experimental.pallas import tpu as pltpu
from jax.sharding import PartitionSpec as P

NPROJ = 256


FAR = -1.0 / 12.0
NEAR = 4.0 / 3.0
CENTER = -2.5


def with_halo(cells, sides, width):
    for axis, dim in sides:
        count = lax.axis_size(axis)
        ends = count - 1
        head = lax.slice_in_dim(cells, 0, width, axis=dim)
        tail = lax.slice_in_dim(cells, cells.shape[dim] - width, cells.shape[dim], axis=dim)
        cells = jnp.concatenate(
            [
                lax.ppermute(tail, axis, [(i, (i + 1) % count) for i in range(ends)]),
                cells,
                lax.ppermute(head, axis, [((i + 1) % count, i) for i in range(ends)]),
            ],
            axis=dim,
        )
    return cells


def second_along(padded, axis, count):

    def piece(offset):
        return lax.slice_in_dim(padded, 2 + offset, 2 + offset + count, axis=axis)

    return FAR * (piece(-2) + piece(2)) + NEAR * (piece(-1) + piece(1)) + CENTER * piece(0)


MESH = pl.DeviceIdType.MESH


def spans_of(count):
    spans = []
    span = 1
    while 2 * span < count:
        spans.append(span)
        span *= 2
    return spans, span + 1


def sweep_kernel(count, f_ref, d_ref, o_ref, state, landed, send_sem, recv_sem):
    me = lax.axis_index("layer")
    row = lax.axis_index("xs")
    layers = f_ref.shape[1]
    width = f_ref.shape[3]
    spans, far = spans_of(count)
    hops = spans + [1, far]
    barrier = pltpu.get_barrier_semaphore()
    for hop in hops:
        for sign in (1, -1):
            pl.semaphore_signal(
                barrier, inc=1, device_id=(lax.rem(me + sign * hop + count, count), row),
                device_id_type=MESH,
            )
    pl.semaphore_wait(barrier, 2 * len(hops))

    rates = [d_ref[index] for index in range(layers)]
    through = rates[0]
    for index in range(1, layers):
        through = through * rates[index]

    def put(direction, slot, ends, keep):
        state[direction, slot, :, :, :width] = ends
        state[direction, slot, :, :, width:] = jnp.broadcast_to(keep[None], (2,) + keep.shape[:1] + (128,))

    def send(direction, slot, target_slot, hop, sign):
        copy = pltpu.make_async_remote_copy(
            src_ref=state.at[direction, slot],
            dst_ref=landed.at[direction, target_slot],
            send_sem=send_sem.at[direction, target_slot],
            recv_sem=recv_sem.at[direction, target_slot],
            device_id=(lax.rem(me + sign * hop + count, count), row),
            device_id_type=MESH,
        )
        copy.start()
        return copy

    def scan(direction, ends, sign):
        put(direction, 0, ends, through)
        for slot, hop in enumerate(spans):
            send(direction, slot, slot, hop, sign).wait()
            source = me - hop if sign == 1 else me + hop
            valid = ((source >= 0) & (source < count)).astype(jnp.float32)
            mine = state[direction, slot]
            got = landed[direction, slot]
            keep = mine[0, :, width:width + 1]
            put(
                direction, slot + 1,
                mine[:, :, :width] + (valid * keep)[None] * got[:, :, :width],
                keep * (valid * got[0, :, width:width + 1]),
            )
        last = len(spans)
        near = send(direction, last, last, 1, sign)
        distant = send(direction, last, last + 1, far, sign)
        near.wait()
        distant.wait()
        near_source = me - 1 if sign == 1 else me + 1
        far_source = me - far if sign == 1 else me + far
        near_valid = ((near_source >= 0) & (near_source < count)).astype(jnp.float32)
        far_valid = ((far_source >= 0) & (far_source < count)).astype(jnp.float32)
        got = landed[direction, last]
        result = got[:, :, :width]
        if far < count:
            result = result + (far_valid * got[0, :, width:width + 1])[None] * landed[direction, last + 1, :, :, :width]
        return near_valid * result

    state_now = None
    ahead = []
    for index in range(layers):
        source = f_ref[:, index]
        if state_now is None:
            state_now = (1.0 - rates[index])[None] * source
        else:
            state_now = rates[index][None] * state_now + (1.0 - rates[index])[None] * source
        ahead.append(state_now)
    entering = scan(0, state_now, 1)
    lower = rates[0]
    for index in range(layers):
        if index > 0:
            lower = lower * rates[index]
        ahead[index] = ahead[index] + lower[None] * entering
    state_now = None
    back = [None] * layers
    for index in reversed(range(layers)):
        if state_now is None:
            state_now = (1.0 - rates[index])[None] * ahead[index]
        else:
            state_now = rates[index][None] * state_now + (1.0 - rates[index])[None] * ahead[index]
        back[index] = state_now
    from_above = scan(1, state_now, -1)
    upper = rates[layers - 1]
    for index in reversed(range(layers)):
        if index < layers - 1:
            upper = upper * rates[index]
        o_ref[:, index] = back[index] + upper[None] * from_above


def exchange_kernel(count, layer_count, nodes_ref, weights_ref, ext_ref, probe_ref, out_ref, gathered, swept, send_sem, recv_sem, back_send, back_recv):
    me = lax.axis_index("layer")
    row = lax.axis_index("xs")
    layers = layer_count
    barrier = pltpu.get_barrier_semaphore()

    def greet(step, carry):
        pl.semaphore_signal(
            barrier, inc=1, device_id=(lax.rem(me + step, count), row), device_id_type=MESH
        )
        return carry

    lax.fori_loop(1, count, greet, 0)
    pl.semaphore_wait(barrier, count - 1)

    def outgoing(step, carry):
        target = lax.rem(me + step, count)
        pltpu.make_async_remote_copy(
            src_ref=ext_ref.at[target],
            dst_ref=gathered.at[me],
            send_sem=send_sem.at[step],
            recv_sem=recv_sem.at[step],
            device_id=(target, row),
            device_id_type=MESH,
        ).start()
        return carry

    lax.fori_loop(1, count, outgoing, 0)
    gathered[me] = ext_ref[me]

    def arrived(step, carry):
        copy = pltpu.make_async_remote_copy(
            src_ref=ext_ref.at[me],
            dst_ref=gathered.at[lax.rem(me + count - step, count)],
            send_sem=send_sem.at[step],
            recv_sem=recv_sem.at[step],
            device_id=(lax.rem(me + step, count), row),
            device_id_type=MESH,
        )
        copy.wait_send()
        copy.wait_recv()
        return carry

    lax.fori_loop(1, count, arrived, 0)

    half = out_ref.shape[3]
    rows_per_layer = 2 * half
    zero = jnp.zeros((half, out_ref.shape[4]), jnp.float32)
    data_rows = layers * half
    total = count * layers
    w0 = w1 = w2 = None
    for node in range(nodes_ref.shape[0]):
        weight = weights_ref[node]
        scaled = weight * nodes_ref[node]
        if w0 is None:
            w0, w1, w2 = weight, scaled, scaled * nodes_ref[node]
        else:
            w0, w1, w2 = w0 + weight, w1 + scaled, w2 + scaled * nodes_ref[node]

    def probe_at(place):
        inside = ((place >= 0) & (place < total)).astype(jnp.float32)
        place = jnp.clip(place, 0, total - 1)
        source = place // layers
        layer = place - source * layers
        return inside * probe_ref[source, pl.ds(layer * half, half), :]

    def prepare(source, carry):
        for layer in range(layers):
            place = source * layers + layer
            here = probe_ref[source, pl.ds(layer * half, half), :]
            partial = gathered[source, pl.ds(layer * half, half), :]
            second = (
                FAR * (probe_at(place - 2) + probe_at(place + 2))
                + NEAR * (probe_at(place - 1) + probe_at(place + 1))
                + CENTER * here
            )
            hamil = partial - 0.5 * second
            swept[source, 0, layer] = w0 * hamil - w1 * here
            swept[source, 1, layer] = w1 * hamil - w2 * here
        return carry

    lax.fori_loop(0, count, prepare, 0)

    def forward(source, state):
        for layer in range(layers):
            rate = gathered[source, pl.ds(data_rows + layer, 1), :]
            state = tuple(
                rate * state[m] + (1.0 - rate) * swept[source, m, layer] for m in range(2)
            )
            for m in range(2):
                swept[source, m, layer] = state[m]
        return state

    lax.fori_loop(0, count, forward, (zero, zero))

    def backward(step, state):
        source = count - 1 - step
        for layer in reversed(range(layers)):
            rate = gathered[source, pl.ds(data_rows + layer, 1), :]
            state = tuple(
                rate * state[m] + (1.0 - rate) * swept[source, m, layer] for m in range(2)
            )
            for m in range(2):
                swept[source, m, layer] = state[m]
        return state

    lax.fori_loop(0, count, backward, (zero, zero))

    def returning(step, carry):
        target = lax.rem(me + step, count)
        pltpu.make_async_remote_copy(
            src_ref=swept.at[target],
            dst_ref=out_ref.at[:, :, me],
            send_sem=back_send.at[step],
            recv_sem=back_recv.at[step],
            device_id=(target, row),
            device_id_type=MESH,
        ).start()
        return carry

    lax.fori_loop(1, count, returning, 0)
    out_ref[:, :, me] = swept[me]

    def returned(step, carry):
        copy = pltpu.make_async_remote_copy(
            src_ref=swept.at[me],
            dst_ref=out_ref.at[:, :, lax.rem(me + count - step, count)],
            send_sem=back_send.at[step],
            recv_sem=back_recv.at[step],
            device_id=(lax.rem(me + step, count), row),
            device_id_type=MESH,
        )
        copy.wait_send()
        copy.wait_recv()
        return carry

    lax.fori_loop(1, count, returned, 0)


def sweeps(partial, gathered_probes, decay_rates, nodes, weights):
    layers, columns, width = partial.shape
    moments = 2
    count = lax.axis_size("layer")
    if columns != count:
        raise ValueError("columns")
    tiles = width // 128
    data_rows = layers * tiles
    padded_rows = -(-(data_rows + layers) // 8) * 8
    body = jnp.transpose(partial, (1, 0, 2)).reshape(columns, data_rows, 128)
    lanes = jnp.broadcast_to(jnp.transpose(decay_rates)[:, :, None], (columns, layers, 128))
    spare = jnp.zeros((columns, padded_rows - data_rows - layers, 128), jnp.float32)
    ext = jnp.concatenate([body, lanes, spare], axis=1)
    vmem = pl.BlockSpec(memory_space=pltpu.VMEM)
    out = pl.pallas_call(
        functools.partial(exchange_kernel, count, layers),
        out_shape=jax.ShapeDtypeStruct((moments, layers, columns, tiles, 128), jnp.float32),
        in_specs=[pl.BlockSpec(memory_space=pltpu.SMEM)] * 2 + [vmem, vmem],
        out_specs=vmem,
        scratch_shapes=[
            pltpu.VMEM((count, padded_rows, 128), jnp.float32),
            pltpu.VMEM((count, moments, layers, tiles, 128), jnp.float32),
            pltpu.SemaphoreType.DMA((count,)),
            pltpu.SemaphoreType.DMA((count,)),
            pltpu.SemaphoreType.DMA((count,)),
            pltpu.SemaphoreType.DMA((count,)),
        ],
        compiler_params=pltpu.CompilerParams(collective_id=0, has_side_effects=True),
    )(nodes, weights, ext, gathered_probes)
    return out.reshape(moments, layers, columns, width)


def front_kernel(row_count, layer_count, depth, block_ref, coef_ref, pieces_ref, across, total, regrouped,
                 left, right, gathered, send_sem, recv_sem, piece_send, piece_recv):
    me = lax.axis_index("layer")
    row = lax.axis_index("xs")
    peers = row_count - 1
    barrier = pltpu.get_barrier_semaphore()
    for step in range(1, row_count):
        pl.semaphore_signal(
            barrier, inc=1, device_id=(me, lax.rem(row + step, row_count)), device_id_type=MESH
        )

    def greet(step, carry):
        pl.semaphore_signal(
            barrier, inc=1, device_id=(lax.rem(me + step, layer_count), row), device_id_type=MESH
        )
        return carry

    lax.fori_loop(1, layer_count, greet, 0)
    pl.semaphore_wait(barrier, peers + layer_count - 1)

    def outgoing(step, carry):
        target = lax.rem(me + step, layer_count)
        pltpu.make_async_remote_copy(
            src_ref=pieces_ref.at[target],
            dst_ref=regrouped.at[me],
            send_sem=piece_send.at[step],
            recv_sem=piece_recv.at[step],
            device_id=(target, row),
            device_id_type=MESH,
        ).start()
        return carry

    copies = []
    targets = [
        (left, (me, lax.rem(row + 1, row_count))),
        (right, (me, lax.rem(row + row_count - 1, row_count))),
    ]
    for slot, (dst, device) in enumerate(targets):
        copies.append(
            pltpu.make_async_remote_copy(
                src_ref=block_ref, dst_ref=dst, send_sem=send_sem.at[slot], recv_sem=recv_sem.at[slot],
                device_id=device, device_id_type=MESH,
            )
        )
    for step in range(1, row_count):
        copies.append(
            pltpu.make_async_remote_copy(
                src_ref=coef_ref, dst_ref=gathered.at[step - 1], send_sem=send_sem.at[1 + step],
                recv_sem=recv_sem.at[1 + step], device_id=(me, lax.rem(row + step, row_count)),
                device_id_type=MESH,
            )
        )
    for copy in copies:
        copy.start()
    lax.fori_loop(1, layer_count, outgoing, 0)
    regrouped[me] = pieces_ref[me]
    for copy in copies[2:]:
        copy.wait()
    acc = coef_ref[...]
    for step in range(peers):
        acc = acc + gathered[step]
    total[...] = acc
    for copy in copies[:2]:
        copy.wait()
    before = left[...] * (row > 0).astype(jnp.float32)
    after = right[...] * (row < row_count - 1).astype(jnp.float32)
    mine = block_ref[...]
    first, second = slice(0, depth), slice(depth, 2 * depth)
    across[:, :, first] = (
        FAR * (before[:, :, first] + after[:, :, first])
        + NEAR * (before[:, :, second] + mine[:, :, second])
        + CENTER * mine[:, :, first]
    )
    across[:, :, second] = (
        FAR * (before[:, :, second] + after[:, :, second])
        + NEAR * (mine[:, :, first] + after[:, :, first])
        + CENTER * mine[:, :, second]
    )

    def arrived(step, carry):
        copy = pltpu.make_async_remote_copy(
            src_ref=pieces_ref.at[me],
            dst_ref=regrouped.at[lax.rem(me + layer_count - step, layer_count)],
            send_sem=piece_send.at[step],
            recv_sem=piece_recv.at[step],
            device_id=(lax.rem(me + step, layer_count), row),
            device_id_type=MESH,
        )
        copy.wait_send()
        copy.wait_recv()
        return carry

    lax.fori_loop(1, layer_count, arrived, 0)


def front_exchange(block, coef, depth):
    row_count = lax.axis_size("xs")
    layer_count = lax.axis_size("layer")
    layers, columns, width = block.shape
    pieces = jnp.transpose(block, (1, 0, 2)).reshape(columns, layers * width // 128, 128)
    spec = pl.BlockSpec(memory_space=pltpu.VMEM)
    return pl.pallas_call(
        functools.partial(front_kernel, row_count, layer_count, depth),
        out_shape=[jax.ShapeDtypeStruct(block.shape, jnp.float32)]
        + [jax.ShapeDtypeStruct(coef.shape, jnp.float32),
           jax.ShapeDtypeStruct((layer_count,) + pieces.shape[1:], jnp.float32)],
        in_specs=[spec, spec, spec],
        out_specs=[spec] * 3,
        scratch_shapes=[
            pltpu.VMEM(block.shape, jnp.float32),
            pltpu.VMEM(block.shape, jnp.float32),
            pltpu.VMEM((row_count - 1,) + coef.shape, jnp.float32),
            pltpu.SemaphoreType.DMA((1 + row_count,)),
            pltpu.SemaphoreType.DMA((1 + row_count,)),
            pltpu.SemaphoreType.DMA((layer_count,)),
            pltpu.SemaphoreType.DMA((layer_count,)),
        ],
        compiler_params=pltpu.CompilerParams(collective_id=1, has_side_effects=True),
    )(block, coef, pieces)


def shards(
    probes,
    potential,
    projector,
    intersection_ids,
    strength,
    decay_rates,
    contour_nodes,
    node_weights,
):
    layers, columns, rows, depth = probes.shape
    rounded = probes.astype(jnp.bfloat16).reshape(layers, columns, rows * depth)
    slot_coef = jnp.einsum("lsp,lcp->lsc", projector, rounded, preferred_element_type=jnp.float32)
    onehot = (intersection_ids[:, :, None] == jnp.arange(NPROJ, dtype=jnp.int32)).astype(
        jnp.float32
    )
    partial_coef = jnp.einsum("lsq,lsc->lcq", onehot, slot_coef, precision=lax.Precision.HIGHEST)
    if rows != 2:
        raise ValueError("rows")
    along_rows, coef, regrouped = front_exchange(
        probes.reshape(layers, columns, rows * depth), partial_coef, depth
    )
    across = jnp.pad(probes, ((0, 0), (0, 0), (0, 0), (2, 2)))
    laplace = along_rows.reshape(probes.shape) + second_along(across, 3, depth)
    coef = jnp.swapaxes(coef, 1, 2)
    scaled = (strength[:, :, None] * coef).astype(jnp.bfloat16)
    slot_back = jnp.einsum(
        "lsq,lqc->lsc", onehot.astype(jnp.bfloat16), scaled, preferred_element_type=jnp.float32
    ).astype(jnp.bfloat16)
    projected = jnp.einsum(
        "lsp,lsc->lcp", projector, slot_back, preferred_element_type=jnp.float32
    ).reshape(layers, columns, rows, depth)
    partial = -0.5 * laplace + potential[:, None] * probes + projected
    swept = sweeps(
        partial.reshape(layers, columns, rows * depth), regrouped, decay_rates, contour_nodes,
        node_weights,
    )
    return swept.reshape(2, layers, columns, rows, depth)


def solution(mesh):
    in_specs = (
        P("layer", None, "xs", None),
        P("layer", "xs", None),
        P("layer", "xs", None),
        P("layer", "xs"),
        P("layer", None),
        P("layer", None),
        P(),
        P(),
    )
    out_specs = P(None, "layer", None, "xs", None)
    return jax.shard_map(shards, mesh=mesh, in_specs=in_specs, out_specs=out_specs, check_vma=False)
```

```python
import functools

import jax
import jax.numpy as jnp
from jax import lax
from jax.experimental import pallas as pl
from jax.experimental.pallas import tpu as pltpu
from jax.sharding import PartitionSpec as P

NPROJ = 256


FAR = -1.0 / 12.0
NEAR = 4.0 / 3.0
CENTER = -2.5


def with_halo(cells, sides, width):
    for axis, dim in sides:
        count = lax.axis_size(axis)
        ends = count - 1
        head = lax.slice_in_dim(cells, 0, width, axis=dim)
        tail = lax.slice_in_dim(cells, cells.shape[dim] - width, cells.shape[dim], axis=dim)
        cells = jnp.concatenate(
            [
                lax.ppermute(tail, axis, [(i, (i + 1) % count) for i in range(ends)]),
                cells,
                lax.ppermute(head, axis, [((i + 1) % count, i) for i in range(ends)]),
            ],
            axis=dim,
        )
    return cells


def second_along_flat(flat, depth):
    width = flat.shape[-1]
    padded = jnp.pad(flat, [(0, 0)] * (flat.ndim - 1) + [(2, 2)])
    spot = lax.broadcasted_iota(jnp.int32, (width,), 0) % depth

    def piece(offset):
        shifted = lax.slice_in_dim(padded, 2 + offset, 2 + offset + width, axis=flat.ndim - 1)
        if offset == 0:
            return shifted
        inside = (spot + offset >= 0) & (spot + offset < depth)
        return jnp.where(inside, shifted, 0.0)

    return FAR * (piece(-2) + piece(2)) + NEAR * (piece(-1) + piece(1)) + CENTER * piece(0)


def second_along(padded, axis, count):

    def piece(offset):
        return lax.slice_in_dim(padded, 2 + offset, 2 + offset + count, axis=axis)

    return FAR * (piece(-2) + piece(2)) + NEAR * (piece(-1) + piece(1)) + CENTER * piece(0)


MESH = pl.DeviceIdType.MESH


def spans_of(count):
    spans = []
    span = 1
    while 2 * span < count:
        spans.append(span)
        span *= 2
    return spans, span + 1


def sweep_kernel(count, f_ref, d_ref, o_ref, state, landed, send_sem, recv_sem):
    me = lax.axis_index("layer")
    row = lax.axis_index("xs")
    layers = f_ref.shape[1]
    width = f_ref.shape[3]
    spans, far = spans_of(count)
    hops = spans + [1, far]
    barrier = pltpu.get_barrier_semaphore()
    for hop in hops:
        for sign in (1, -1):
            pl.semaphore_signal(
                barrier, inc=1, device_id=(lax.rem(me + sign * hop + count, count), row),
                device_id_type=MESH,
            )
    pl.semaphore_wait(barrier, 2 * len(hops))

    rates = [d_ref[index] for index in range(layers)]
    through = rates[0]
    for index in range(1, layers):
        through = through * rates[index]

    def put(direction, slot, ends, keep):
        state[direction, slot, :, :, :width] = ends
        state[direction, slot, :, :, width:] = jnp.broadcast_to(keep[None], (2,) + keep.shape[:1] + (128,))

    def send(direction, slot, target_slot, hop, sign):
        copy = pltpu.make_async_remote_copy(
            src_ref=state.at[direction, slot],
            dst_ref=landed.at[direction, target_slot],
            send_sem=send_sem.at[direction, target_slot],
            recv_sem=recv_sem.at[direction, target_slot],
            device_id=(lax.rem(me + sign * hop + count, count), row),
            device_id_type=MESH,
        )
        copy.start()
        return copy

    def scan(direction, ends, sign):
        put(direction, 0, ends, through)
        for slot, hop in enumerate(spans):
            send(direction, slot, slot, hop, sign).wait()
            source = me - hop if sign == 1 else me + hop
            valid = ((source >= 0) & (source < count)).astype(jnp.float32)
            mine = state[direction, slot]
            got = landed[direction, slot]
            keep = mine[0, :, width:width + 1]
            put(
                direction, slot + 1,
                mine[:, :, :width] + (valid * keep)[None] * got[:, :, :width],
                keep * (valid * got[0, :, width:width + 1]),
            )
        last = len(spans)
        near = send(direction, last, last, 1, sign)
        distant = send(direction, last, last + 1, far, sign)
        near.wait()
        distant.wait()
        near_source = me - 1 if sign == 1 else me + 1
        far_source = me - far if sign == 1 else me + far
        near_valid = ((near_source >= 0) & (near_source < count)).astype(jnp.float32)
        far_valid = ((far_source >= 0) & (far_source < count)).astype(jnp.float32)
        got = landed[direction, last]
        result = got[:, :, :width]
        if far < count:
            result = result + (far_valid * got[0, :, width:width + 1])[None] * landed[direction, last + 1, :, :, :width]
        return near_valid * result

    state_now = None
    ahead = []
    for index in range(layers):
        source = f_ref[:, index]
        if state_now is None:
            state_now = (1.0 - rates[index])[None] * source
        else:
            state_now = rates[index][None] * state_now + (1.0 - rates[index])[None] * source
        ahead.append(state_now)
    entering = scan(0, state_now, 1)
    lower = rates[0]
    for index in range(layers):
        if index > 0:
            lower = lower * rates[index]
        ahead[index] = ahead[index] + lower[None] * entering
    state_now = None
    back = [None] * layers
    for index in reversed(range(layers)):
        if state_now is None:
            state_now = (1.0 - rates[index])[None] * ahead[index]
        else:
            state_now = rates[index][None] * state_now + (1.0 - rates[index])[None] * ahead[index]
        back[index] = state_now
    from_above = scan(1, state_now, -1)
    upper = rates[layers - 1]
    for index in reversed(range(layers)):
        if index < layers - 1:
            upper = upper * rates[index]
        o_ref[:, index] = back[index] + upper[None] * from_above


def exchange_kernel(count, layer_count, nodes_ref, weights_ref, ext_ref, probe_ref, out_ref, gathered, swept, send_sem, recv_sem, back_send, back_recv):
    me = lax.axis_index("layer")
    row = lax.axis_index("xs")
    layers = layer_count
    barrier = pltpu.get_barrier_semaphore()

    def greet(step, carry):
        pl.semaphore_signal(
            barrier, inc=1, device_id=(lax.rem(me + step, count), row), device_id_type=MESH
        )
        return carry

    lax.fori_loop(1, count, greet, 0)
    pl.semaphore_wait(barrier, count - 1)

    def outgoing(step, carry):
        target = lax.rem(me + step, count)
        pltpu.make_async_remote_copy(
            src_ref=ext_ref.at[target],
            dst_ref=gathered.at[me],
            send_sem=send_sem.at[step],
            recv_sem=recv_sem.at[step],
            device_id=(target, row),
            device_id_type=MESH,
        ).start()
        return carry

    lax.fori_loop(1, count, outgoing, 0)
    gathered[me] = ext_ref[me]

    def arrived(step, carry):
        copy = pltpu.make_async_remote_copy(
            src_ref=ext_ref.at[me],
            dst_ref=gathered.at[lax.rem(me + count - step, count)],
            send_sem=send_sem.at[step],
            recv_sem=recv_sem.at[step],
            device_id=(lax.rem(me + step, count), row),
            device_id_type=MESH,
        )
        copy.wait_send()
        copy.wait_recv()
        return carry

    lax.fori_loop(1, count, arrived, 0)

    half = out_ref.shape[3]
    rows_per_layer = 2 * half
    zero = jnp.zeros((half, out_ref.shape[4]), jnp.float32)
    data_rows = layers * half
    total = count * layers
    w0 = w1 = w2 = None
    for node in range(nodes_ref.shape[0]):
        weight = weights_ref[node]
        scaled = weight * nodes_ref[node]
        if w0 is None:
            w0, w1, w2 = weight, scaled, scaled * nodes_ref[node]
        else:
            w0, w1, w2 = w0 + weight, w1 + scaled, w2 + scaled * nodes_ref[node]

    def probe_at(place):
        inside = ((place >= 0) & (place < total)).astype(jnp.float32)
        place = jnp.clip(place, 0, total - 1)
        source = place // layers
        layer = place - source * layers
        return inside * probe_ref[source, pl.ds(layer * half, half), :]

    def prepare(source, carry):
        for layer in range(layers):
            place = source * layers + layer
            here = probe_ref[source, pl.ds(layer * half, half), :]
            partial = gathered[source, pl.ds(layer * half, half), :]
            second = (
                FAR * (probe_at(place - 2) + probe_at(place + 2))
                + NEAR * (probe_at(place - 1) + probe_at(place + 1))
                + CENTER * here
            )
            hamil = partial - 0.5 * second
            swept[source, 0, layer] = w0 * hamil - w1 * here
            swept[source, 1, layer] = w1 * hamil - w2 * here
        return carry

    lax.fori_loop(0, count, prepare, 0)

    def forward(source, state):
        for layer in range(layers):
            rate = gathered[source, pl.ds(data_rows + layer, 1), :]
            state = tuple(
                rate * state[m] + (1.0 - rate) * swept[source, m, layer] for m in range(2)
            )
            for m in range(2):
                swept[source, m, layer] = state[m]
        return state

    lax.fori_loop(0, count, forward, (zero, zero))

    def backward(step, state):
        source = count - 1 - step
        for layer in reversed(range(layers)):
            rate = gathered[source, pl.ds(data_rows + layer, 1), :]
            state = tuple(
                rate * state[m] + (1.0 - rate) * swept[source, m, layer] for m in range(2)
            )
            for m in range(2):
                swept[source, m, layer] = state[m]
        return state

    lax.fori_loop(0, count, backward, (zero, zero))

    def returning(step, carry):
        target = lax.rem(me + step, count)
        pltpu.make_async_remote_copy(
            src_ref=swept.at[target],
            dst_ref=out_ref.at[:, :, me],
            send_sem=back_send.at[step],
            recv_sem=back_recv.at[step],
            device_id=(target, row),
            device_id_type=MESH,
        ).start()
        return carry

    lax.fori_loop(1, count, returning, 0)
    out_ref[:, :, me] = swept[me]

    def returned(step, carry):
        copy = pltpu.make_async_remote_copy(
            src_ref=swept.at[me],
            dst_ref=out_ref.at[:, :, lax.rem(me + count - step, count)],
            send_sem=back_send.at[step],
            recv_sem=back_recv.at[step],
            device_id=(lax.rem(me + step, count), row),
            device_id_type=MESH,
        )
        copy.wait_send()
        copy.wait_recv()
        return carry

    lax.fori_loop(1, count, returned, 0)


def sweeps(partial, gathered_probes, decay_rates, nodes, weights):
    layers, columns, width = partial.shape
    moments = 2
    count = lax.axis_size("layer")
    if columns != count:
        raise ValueError("columns")
    tiles = width // 128
    data_rows = layers * tiles
    padded_rows = -(-(data_rows + layers) // 8) * 8
    body = jnp.transpose(partial, (1, 0, 2)).reshape(columns, data_rows, 128)
    lanes = jnp.broadcast_to(jnp.transpose(decay_rates)[:, :, None], (columns, layers, 128))
    spare = jnp.zeros((columns, padded_rows - data_rows - layers, 128), jnp.float32)
    ext = jnp.concatenate([body, lanes, spare], axis=1)
    vmem = pl.BlockSpec(memory_space=pltpu.VMEM)
    out = pl.pallas_call(
        functools.partial(exchange_kernel, count, layers),
        out_shape=jax.ShapeDtypeStruct((moments, layers, columns, tiles, 128), jnp.float32),
        in_specs=[pl.BlockSpec(memory_space=pltpu.SMEM)] * 2 + [vmem, vmem],
        out_specs=vmem,
        scratch_shapes=[
            pltpu.VMEM((count, padded_rows, 128), jnp.float32),
            pltpu.VMEM((count, moments, layers, tiles, 128), jnp.float32),
            pltpu.SemaphoreType.DMA((count,)),
            pltpu.SemaphoreType.DMA((count,)),
            pltpu.SemaphoreType.DMA((count,)),
            pltpu.SemaphoreType.DMA((count,)),
        ],
        compiler_params=pltpu.CompilerParams(collective_id=0, has_side_effects=True),
    )(nodes, weights, ext, gathered_probes)
    return out.reshape(moments, layers, columns, width)


def front_kernel(row_count, layer_count, depth, block_ref, coef_ref, pieces_ref, across, total, regrouped,
                 left, right, gathered, send_sem, recv_sem, piece_send, piece_recv):
    me = lax.axis_index("layer")
    row = lax.axis_index("xs")
    peers = row_count - 1
    barrier = pltpu.get_barrier_semaphore()
    for step in range(1, row_count):
        pl.semaphore_signal(
            barrier, inc=1, device_id=(me, lax.rem(row + step, row_count)), device_id_type=MESH
        )

    def greet(step, carry):
        pl.semaphore_signal(
            barrier, inc=1, device_id=(lax.rem(me + step, layer_count), row), device_id_type=MESH
        )
        return carry

    lax.fori_loop(1, layer_count, greet, 0)
    pl.semaphore_wait(barrier, peers + layer_count - 1)

    def outgoing(step, carry):
        target = lax.rem(me + step, layer_count)
        pltpu.make_async_remote_copy(
            src_ref=pieces_ref.at[target],
            dst_ref=regrouped.at[me],
            send_sem=piece_send.at[step],
            recv_sem=piece_recv.at[step],
            device_id=(target, row),
            device_id_type=MESH,
        ).start()
        return carry

    copies = []
    targets = [
        (left, (me, lax.rem(row + 1, row_count))),
        (right, (me, lax.rem(row + row_count - 1, row_count))),
    ]
    for slot, (dst, device) in enumerate(targets):
        copies.append(
            pltpu.make_async_remote_copy(
                src_ref=block_ref, dst_ref=dst, send_sem=send_sem.at[slot], recv_sem=recv_sem.at[slot],
                device_id=device, device_id_type=MESH,
            )
        )
    for step in range(1, row_count):
        copies.append(
            pltpu.make_async_remote_copy(
                src_ref=coef_ref, dst_ref=gathered.at[step - 1], send_sem=send_sem.at[1 + step],
                recv_sem=recv_sem.at[1 + step], device_id=(me, lax.rem(row + step, row_count)),
                device_id_type=MESH,
            )
        )
    for copy in copies:
        copy.start()
    lax.fori_loop(1, layer_count, outgoing, 0)
    regrouped[me] = pieces_ref[me]
    for copy in copies[2:]:
        copy.wait()
    acc = coef_ref[...]
    for step in range(peers):
        acc = acc + gathered[step]
    total[...] = acc
    for copy in copies[:2]:
        copy.wait()
    before = left[...] * (row > 0).astype(jnp.float32)
    after = right[...] * (row < row_count - 1).astype(jnp.float32)
    mine = block_ref[...]
    first, second = slice(0, depth), slice(depth, 2 * depth)
    across[:, :, first] = (
        FAR * (before[:, :, first] + after[:, :, first])
        + NEAR * (before[:, :, second] + mine[:, :, second])
        + CENTER * mine[:, :, first]
    )
    across[:, :, second] = (
        FAR * (before[:, :, second] + after[:, :, second])
        + NEAR * (mine[:, :, first] + after[:, :, first])
        + CENTER * mine[:, :, second]
    )

    def arrived(step, carry):
        copy = pltpu.make_async_remote_copy(
            src_ref=pieces_ref.at[me],
            dst_ref=regrouped.at[lax.rem(me + layer_count - step, layer_count)],
            send_sem=piece_send.at[step],
            recv_sem=piece_recv.at[step],
            device_id=(lax.rem(me + step, layer_count), row),
            device_id_type=MESH,
        )
        copy.wait_send()
        copy.wait_recv()
        return carry

    lax.fori_loop(1, layer_count, arrived, 0)


def front_exchange(block, coef, depth):
    row_count = lax.axis_size("xs")
    layer_count = lax.axis_size("layer")
    layers, columns, width = block.shape
    pieces = jnp.transpose(block, (1, 0, 2)).reshape(columns, layers * width // 128, 128)
    spec = pl.BlockSpec(memory_space=pltpu.VMEM)
    return pl.pallas_call(
        functools.partial(front_kernel, row_count, layer_count, depth),
        out_shape=[jax.ShapeDtypeStruct(block.shape, jnp.float32)]
        + [jax.ShapeDtypeStruct(coef.shape, jnp.float32),
           jax.ShapeDtypeStruct((layer_count,) + pieces.shape[1:], jnp.float32)],
        in_specs=[spec, spec, spec],
        out_specs=[spec] * 3,
        scratch_shapes=[
            pltpu.VMEM(block.shape, jnp.float32),
            pltpu.VMEM(block.shape, jnp.float32),
            pltpu.VMEM((row_count - 1,) + coef.shape, jnp.float32),
            pltpu.SemaphoreType.DMA((1 + row_count,)),
            pltpu.SemaphoreType.DMA((1 + row_count,)),
            pltpu.SemaphoreType.DMA((layer_count,)),
            pltpu.SemaphoreType.DMA((layer_count,)),
        ],
        compiler_params=pltpu.CompilerParams(collective_id=1, has_side_effects=True),
    )(block, coef, pieces)


def shards(
    probes,
    potential,
    projector,
    intersection_ids,
    strength,
    decay_rates,
    contour_nodes,
    node_weights,
):
    layers, columns, rows, depth = probes.shape
    rounded = probes.astype(jnp.bfloat16).reshape(layers, columns, rows * depth)
    slot_coef = jnp.einsum("lsp,lcp->lsc", projector, rounded, preferred_element_type=jnp.float32)
    onehot = (intersection_ids[:, :, None] == jnp.arange(NPROJ, dtype=jnp.int32)).astype(
        jnp.float32
    )
    partial_coef = jnp.einsum("lsq,lsc->lcq", onehot, slot_coef, precision=lax.Precision.HIGHEST)
    if rows != 2:
        raise ValueError("rows")
    flat = probes.reshape(layers, columns, rows * depth)
    along_rows, coef, regrouped = front_exchange(flat, partial_coef, depth)
    laplace = along_rows + second_along_flat(flat, depth)
    coef = jnp.swapaxes(coef, 1, 2)
    scaled = (strength[:, :, None] * coef).astype(jnp.bfloat16)
    slot_back = jnp.einsum(
        "lsq,lqc->lsc", onehot.astype(jnp.bfloat16), scaled, preferred_element_type=jnp.float32
    ).astype(jnp.bfloat16)
    projected = jnp.einsum(
        "lsp,lsc->lcp", projector, slot_back, preferred_element_type=jnp.float32
    )
    partial = -0.5 * laplace + potential.reshape(layers, 1, rows * depth) * flat + projected
    swept = sweeps(
        partial, regrouped, decay_rates, contour_nodes,
        node_weights,
    )
    return swept.reshape(2, layers, columns, rows, depth)


def solution(mesh):
    in_specs = (
        P("layer", None, "xs", None),
        P("layer", "xs", None),
        P("layer", "xs", None),
        P("layer", "xs"),
        P("layer", None),
        P("layer", None),
        P(),
        P(),
    )
    out_specs = P(None, "layer", None, "xs", None)
    return jax.shard_map(shards, mesh=mesh, in_specs=in_specs, out_specs=out_specs, check_vma=False)
```

```python
import functools

import jax
import jax.numpy as jnp
from jax import lax
from jax.experimental import pallas as pl
from jax.experimental.pallas import tpu as pltpu
from jax.sharding import PartitionSpec as P

NPROJ = 256


FAR = -1.0 / 12.0
NEAR = 4.0 / 3.0
CENTER = -2.5


def with_halo(cells, sides, width):
    for axis, dim in sides:
        count = lax.axis_size(axis)
        ends = count - 1
        head = lax.slice_in_dim(cells, 0, width, axis=dim)
        tail = lax.slice_in_dim(cells, cells.shape[dim] - width, cells.shape[dim], axis=dim)
        cells = jnp.concatenate(
            [
                lax.ppermute(tail, axis, [(i, (i + 1) % count) for i in range(ends)]),
                cells,
                lax.ppermute(head, axis, [((i + 1) % count, i) for i in range(ends)]),
            ],
            axis=dim,
        )
    return cells


def second_along_flat(flat, depth):
    width = flat.shape[-1]
    padded = jnp.pad(flat, [(0, 0)] * (flat.ndim - 1) + [(2, 2)])
    spot = lax.broadcasted_iota(jnp.int32, (width,), 0) % depth

    def piece(offset):
        shifted = lax.slice_in_dim(padded, 2 + offset, 2 + offset + width, axis=flat.ndim - 1)
        if offset == 0:
            return shifted
        inside = (spot + offset >= 0) & (spot + offset < depth)
        return jnp.where(inside, shifted, 0.0)

    return FAR * (piece(-2) + piece(2)) + NEAR * (piece(-1) + piece(1)) + CENTER * piece(0)


def second_along(padded, axis, count):

    def piece(offset):
        return lax.slice_in_dim(padded, 2 + offset, 2 + offset + count, axis=axis)

    return FAR * (piece(-2) + piece(2)) + NEAR * (piece(-1) + piece(1)) + CENTER * piece(0)


MESH = pl.DeviceIdType.MESH


def spans_of(count):
    spans = []
    span = 1
    while 2 * span < count:
        spans.append(span)
        span *= 2
    return spans, span + 1


def sweep_kernel(count, f_ref, d_ref, o_ref, state, landed, send_sem, recv_sem):
    me = lax.axis_index("layer")
    row = lax.axis_index("xs")
    layers = f_ref.shape[1]
    width = f_ref.shape[3]
    spans, far = spans_of(count)
    hops = spans + [1, far]
    barrier = pltpu.get_barrier_semaphore()
    for hop in hops:
        for sign in (1, -1):
            pl.semaphore_signal(
                barrier, inc=1, device_id=(lax.rem(me + sign * hop + count, count), row),
                device_id_type=MESH,
            )
    pl.semaphore_wait(barrier, 2 * len(hops))

    rates = [d_ref[index] for index in range(layers)]
    through = rates[0]
    for index in range(1, layers):
        through = through * rates[index]

    def put(direction, slot, ends, keep):
        state[direction, slot, :, :, :width] = ends
        state[direction, slot, :, :, width:] = jnp.broadcast_to(keep[None], (2,) + keep.shape[:1] + (128,))

    def send(direction, slot, target_slot, hop, sign):
        copy = pltpu.make_async_remote_copy(
            src_ref=state.at[direction, slot],
            dst_ref=landed.at[direction, target_slot],
            send_sem=send_sem.at[direction, target_slot],
            recv_sem=recv_sem.at[direction, target_slot],
            device_id=(lax.rem(me + sign * hop + count, count), row),
            device_id_type=MESH,
        )
        copy.start()
        return copy

    def scan(direction, ends, sign):
        put(direction, 0, ends, through)
        for slot, hop in enumerate(spans):
            send(direction, slot, slot, hop, sign).wait()
            source = me - hop if sign == 1 else me + hop
            valid = ((source >= 0) & (source < count)).astype(jnp.float32)
            mine = state[direction, slot]
            got = landed[direction, slot]
            keep = mine[0, :, width:width + 1]
            put(
                direction, slot + 1,
                mine[:, :, :width] + (valid * keep)[None] * got[:, :, :width],
                keep * (valid * got[0, :, width:width + 1]),
            )
        last = len(spans)
        near = send(direction, last, last, 1, sign)
        distant = send(direction, last, last + 1, far, sign)
        near.wait()
        distant.wait()
        near_source = me - 1 if sign == 1 else me + 1
        far_source = me - far if sign == 1 else me + far
        near_valid = ((near_source >= 0) & (near_source < count)).astype(jnp.float32)
        far_valid = ((far_source >= 0) & (far_source < count)).astype(jnp.float32)
        got = landed[direction, last]
        result = got[:, :, :width]
        if far < count:
            result = result + (far_valid * got[0, :, width:width + 1])[None] * landed[direction, last + 1, :, :, :width]
        return near_valid * result

    state_now = None
    ahead = []
    for index in range(layers):
        source = f_ref[:, index]
        if state_now is None:
            state_now = (1.0 - rates[index])[None] * source
        else:
            state_now = rates[index][None] * state_now + (1.0 - rates[index])[None] * source
        ahead.append(state_now)
    entering = scan(0, state_now, 1)
    lower = rates[0]
    for index in range(layers):
        if index > 0:
            lower = lower * rates[index]
        ahead[index] = ahead[index] + lower[None] * entering
    state_now = None
    back = [None] * layers
    for index in reversed(range(layers)):
        if state_now is None:
            state_now = (1.0 - rates[index])[None] * ahead[index]
        else:
            state_now = rates[index][None] * state_now + (1.0 - rates[index])[None] * ahead[index]
        back[index] = state_now
    from_above = scan(1, state_now, -1)
    upper = rates[layers - 1]
    for index in reversed(range(layers)):
        if index < layers - 1:
            upper = upper * rates[index]
        o_ref[:, index] = back[index] + upper[None] * from_above


def exchange_kernel(count, layer_count, nodes_ref, weights_ref, ext_ref, probe_ref, out_ref, gathered, swept, send_sem, recv_sem, back_send, back_recv):
    me = lax.axis_index("layer")
    row = lax.axis_index("xs")
    layers = layer_count
    barrier = pltpu.get_barrier_semaphore()

    def greet(step, carry):
        pl.semaphore_signal(
            barrier, inc=1, device_id=(lax.rem(me + step, count), row), device_id_type=MESH
        )
        return carry

    lax.fori_loop(1, count, greet, 0)
    pl.semaphore_wait(barrier, count - 1)

    def outgoing(step, carry):
        target = lax.rem(me + step, count)
        pltpu.make_async_remote_copy(
            src_ref=ext_ref.at[target],
            dst_ref=gathered.at[me],
            send_sem=send_sem.at[step],
            recv_sem=recv_sem.at[step],
            device_id=(target, row),
            device_id_type=MESH,
        ).start()
        return carry

    lax.fori_loop(1, count, outgoing, 0)
    gathered[me] = ext_ref[me]

    def arrived(step, carry):
        copy = pltpu.make_async_remote_copy(
            src_ref=ext_ref.at[me],
            dst_ref=gathered.at[lax.rem(me + count - step, count)],
            send_sem=send_sem.at[step],
            recv_sem=recv_sem.at[step],
            device_id=(lax.rem(me + step, count), row),
            device_id_type=MESH,
        )
        copy.wait_send()
        copy.wait_recv()
        return carry

    lax.fori_loop(1, count, arrived, 0)

    half = out_ref.shape[3]
    rows_per_layer = 2 * half
    zero = jnp.zeros((half, out_ref.shape[4]), jnp.float32)
    data_rows = layers * half
    total = count * layers
    w0 = w1 = w2 = None
    for node in range(nodes_ref.shape[0]):
        weight = weights_ref[node]
        scaled = weight * nodes_ref[node]
        if w0 is None:
            w0, w1, w2 = weight, scaled, scaled * nodes_ref[node]
        else:
            w0, w1, w2 = w0 + weight, w1 + scaled, w2 + scaled * nodes_ref[node]

    def probe_at(place):
        inside = ((place >= 0) & (place < total)).astype(jnp.float32)
        place = jnp.clip(place, 0, total - 1)
        source = place // layers
        layer = place - source * layers
        return inside * probe_ref[source, pl.ds(layer * half, half), :]

    def prepare(source, carry):
        for layer in range(layers):
            place = source * layers + layer
            here = probe_ref[source, pl.ds(layer * half, half), :]
            partial = gathered[source, pl.ds(layer * half, half), :]
            second = (
                FAR * (probe_at(place - 2) + probe_at(place + 2))
                + NEAR * (probe_at(place - 1) + probe_at(place + 1))
                + CENTER * here
            )
            hamil = partial - 0.5 * second
            swept[source, 0, layer] = w0 * hamil - w1 * here
            swept[source, 1, layer] = w1 * hamil - w2 * here
        return carry

    lax.fori_loop(0, count, prepare, 0)

    def forward(source, state):
        for layer in range(layers):
            rate = probe_ref[source, pl.ds(data_rows + layer, 1), :]
            state = tuple(
                rate * state[m] + (1.0 - rate) * swept[source, m, layer] for m in range(2)
            )
            for m in range(2):
                swept[source, m, layer] = state[m]
        return state

    lax.fori_loop(0, count, forward, (zero, zero))

    def backward(step, state):
        source = count - 1 - step
        for layer in reversed(range(layers)):
            rate = probe_ref[source, pl.ds(data_rows + layer, 1), :]
            state = tuple(
                rate * state[m] + (1.0 - rate) * swept[source, m, layer] for m in range(2)
            )
            for m in range(2):
                swept[source, m, layer] = state[m]
        return state

    lax.fori_loop(0, count, backward, (zero, zero))

    def returning(step, carry):
        target = lax.rem(me + step, count)
        pltpu.make_async_remote_copy(
            src_ref=swept.at[target],
            dst_ref=out_ref.at[:, :, me],
            send_sem=back_send.at[step],
            recv_sem=back_recv.at[step],
            device_id=(target, row),
            device_id_type=MESH,
        ).start()
        return carry

    lax.fori_loop(1, count, returning, 0)
    out_ref[:, :, me] = swept[me]

    def returned(step, carry):
        copy = pltpu.make_async_remote_copy(
            src_ref=swept.at[me],
            dst_ref=out_ref.at[:, :, lax.rem(me + count - step, count)],
            send_sem=back_send.at[step],
            recv_sem=back_recv.at[step],
            device_id=(lax.rem(me + step, count), row),
            device_id_type=MESH,
        )
        copy.wait_send()
        copy.wait_recv()
        return carry

    lax.fori_loop(1, count, returned, 0)


def sweeps(partial, gathered_probes, decay_rates, nodes, weights):
    layers, columns, width = partial.shape
    moments = 2
    count = lax.axis_size("layer")
    if columns != count:
        raise ValueError("columns")
    tiles = width // 128
    data_rows = layers * tiles
    ext = jnp.transpose(partial, (1, 0, 2)).reshape(columns, data_rows, 128)
    vmem = pl.BlockSpec(memory_space=pltpu.VMEM)
    out = pl.pallas_call(
        functools.partial(exchange_kernel, count, layers),
        out_shape=jax.ShapeDtypeStruct((moments, layers, columns, tiles, 128), jnp.float32),
        in_specs=[pl.BlockSpec(memory_space=pltpu.SMEM)] * 2 + [vmem, vmem],
        out_specs=vmem,
        scratch_shapes=[
            pltpu.VMEM((count, data_rows, 128), jnp.float32),
            pltpu.VMEM((count, moments, layers, tiles, 128), jnp.float32),
            pltpu.SemaphoreType.DMA((count,)),
            pltpu.SemaphoreType.DMA((count,)),
            pltpu.SemaphoreType.DMA((count,)),
            pltpu.SemaphoreType.DMA((count,)),
        ],
        compiler_params=pltpu.CompilerParams(collective_id=0, has_side_effects=True),
    )(nodes, weights, ext, gathered_probes)
    return out.reshape(moments, layers, columns, width)


def front_kernel(row_count, layer_count, depth, block_ref, coef_ref, pieces_ref, across, total, regrouped,
                 left, right, gathered, send_sem, recv_sem, piece_send, piece_recv):
    me = lax.axis_index("layer")
    row = lax.axis_index("xs")
    peers = row_count - 1
    barrier = pltpu.get_barrier_semaphore()
    for step in range(1, row_count):
        pl.semaphore_signal(
            barrier, inc=1, device_id=(me, lax.rem(row + step, row_count)), device_id_type=MESH
        )

    def greet(step, carry):
        pl.semaphore_signal(
            barrier, inc=1, device_id=(lax.rem(me + step, layer_count), row), device_id_type=MESH
        )
        return carry

    lax.fori_loop(1, layer_count, greet, 0)
    pl.semaphore_wait(barrier, peers + layer_count - 1)

    def outgoing(step, carry):
        target = lax.rem(me + step, layer_count)
        pltpu.make_async_remote_copy(
            src_ref=pieces_ref.at[target],
            dst_ref=regrouped.at[me],
            send_sem=piece_send.at[step],
            recv_sem=piece_recv.at[step],
            device_id=(target, row),
            device_id_type=MESH,
        ).start()
        return carry

    copies = []
    targets = [
        (left, (me, lax.rem(row + 1, row_count))),
        (right, (me, lax.rem(row + row_count - 1, row_count))),
    ]
    for slot, (dst, device) in enumerate(targets):
        copies.append(
            pltpu.make_async_remote_copy(
                src_ref=block_ref, dst_ref=dst, send_sem=send_sem.at[slot], recv_sem=recv_sem.at[slot],
                device_id=device, device_id_type=MESH,
            )
        )
    for step in range(1, row_count):
        copies.append(
            pltpu.make_async_remote_copy(
                src_ref=coef_ref, dst_ref=gathered.at[step - 1], send_sem=send_sem.at[1 + step],
                recv_sem=recv_sem.at[1 + step], device_id=(me, lax.rem(row + step, row_count)),
                device_id_type=MESH,
            )
        )
    for copy in copies:
        copy.start()
    lax.fori_loop(1, layer_count, outgoing, 0)
    regrouped[me] = pieces_ref[me]
    for copy in copies[2:]:
        copy.wait()
    acc = coef_ref[...]
    for step in range(peers):
        acc = acc + gathered[step]
    total[...] = acc
    for copy in copies[:2]:
        copy.wait()
    before = left[...] * (row > 0).astype(jnp.float32)
    after = right[...] * (row < row_count - 1).astype(jnp.float32)
    mine = block_ref[...]
    first, second = slice(0, depth), slice(depth, 2 * depth)
    across[:, :, first] = (
        FAR * (before[:, :, first] + after[:, :, first])
        + NEAR * (before[:, :, second] + mine[:, :, second])
        + CENTER * mine[:, :, first]
    )
    across[:, :, second] = (
        FAR * (before[:, :, second] + after[:, :, second])
        + NEAR * (mine[:, :, first] + after[:, :, first])
        + CENTER * mine[:, :, second]
    )

    def arrived(step, carry):
        copy = pltpu.make_async_remote_copy(
            src_ref=pieces_ref.at[me],
            dst_ref=regrouped.at[lax.rem(me + layer_count - step, layer_count)],
            send_sem=piece_send.at[step],
            recv_sem=piece_recv.at[step],
            device_id=(lax.rem(me + step, layer_count), row),
            device_id_type=MESH,
        )
        copy.wait_send()
        copy.wait_recv()
        return carry

    lax.fori_loop(1, layer_count, arrived, 0)


def front_exchange(block, coef, depth, decay_rates):
    row_count = lax.axis_size("xs")
    layer_count = lax.axis_size("layer")
    layers, columns, width = block.shape
    data_rows = layers * width // 128
    padded_rows = -(-(data_rows + layers) // 8) * 8
    body = jnp.transpose(block, (1, 0, 2)).reshape(columns, data_rows, 128)
    lanes = jnp.broadcast_to(jnp.transpose(decay_rates)[:, :, None], (columns, layers, 128))
    spare = jnp.zeros((columns, padded_rows - data_rows - layers, 128), jnp.float32)
    pieces = jnp.concatenate([body, lanes, spare], axis=1)
    spec = pl.BlockSpec(memory_space=pltpu.VMEM)
    return pl.pallas_call(
        functools.partial(front_kernel, row_count, layer_count, depth),
        out_shape=[jax.ShapeDtypeStruct(block.shape, jnp.float32)]
        + [jax.ShapeDtypeStruct(coef.shape, jnp.float32),
           jax.ShapeDtypeStruct((layer_count,) + pieces.shape[1:], jnp.float32)],
        in_specs=[spec, spec, spec],
        out_specs=[spec] * 3,
        scratch_shapes=[
            pltpu.VMEM(block.shape, jnp.float32),
            pltpu.VMEM(block.shape, jnp.float32),
            pltpu.VMEM((row_count - 1,) + coef.shape, jnp.float32),
            pltpu.SemaphoreType.DMA((1 + row_count,)),
            pltpu.SemaphoreType.DMA((1 + row_count,)),
            pltpu.SemaphoreType.DMA((layer_count,)),
            pltpu.SemaphoreType.DMA((layer_count,)),
        ],
        compiler_params=pltpu.CompilerParams(collective_id=1, has_side_effects=True),
    )(block, coef, pieces)


def shards(
    probes,
    potential,
    projector,
    intersection_ids,
    strength,
    decay_rates,
    contour_nodes,
    node_weights,
):
    layers, columns, rows, depth = probes.shape
    flat = probes.reshape(layers, columns, rows * depth)
    rounded = flat.astype(jnp.bfloat16)
    slot_coef = jnp.einsum("lsp,lcp->lsc", projector, rounded, preferred_element_type=jnp.float32)
    onehot = (intersection_ids[:, :, None] == jnp.arange(NPROJ, dtype=jnp.int32)).astype(
        jnp.float32
    )
    partial_coef = jnp.einsum("lsq,lsc->lcq", onehot, slot_coef, precision=lax.Precision.HIGHEST)
    if rows != 2:
        raise ValueError("rows")
    along_rows, coef, regrouped = front_exchange(flat, partial_coef, depth, decay_rates)
    laplace = along_rows + second_along_flat(flat, depth)
    coef = jnp.swapaxes(coef, 1, 2)
    scaled = (strength[:, :, None] * coef).astype(jnp.bfloat16)
    slot_back = jnp.einsum(
        "lsq,lqc->lsc", onehot.astype(jnp.bfloat16), scaled, preferred_element_type=jnp.float32
    ).astype(jnp.bfloat16)
    projected = jnp.einsum(
        "lsp,lsc->lcp", projector, slot_back, preferred_element_type=jnp.float32
    )
    partial = -0.5 * laplace + potential.reshape(layers, 1, rows * depth) * flat + projected
    swept = sweeps(
        partial, regrouped, decay_rates, contour_nodes,
        node_weights,
    )
    return swept.reshape(2, layers, columns, rows, depth)


def solution(mesh):
    in_specs = (
        P("layer", None, "xs", None),
        P("layer", "xs", None),
        P("layer", "xs", None),
        P("layer", "xs"),
        P("layer", None),
        P("layer", None),
        P(),
        P(),
    )
    out_specs = P(None, "layer", None, "xs", None)
    return jax.shard_map(shards, mesh=mesh, in_specs=in_specs, out_specs=out_specs, check_vma=False)
```

```python
import functools

import jax
import jax.numpy as jnp
from jax import lax
from jax.experimental import pallas as pl
from jax.experimental.pallas import tpu as pltpu
from jax.sharding import PartitionSpec as P

NPROJ = 256


FAR = -1.0 / 12.0
NEAR = 4.0 / 3.0
CENTER = -2.5


def with_halo(cells, sides, width):
    for axis, dim in sides:
        count = lax.axis_size(axis)
        ends = count - 1
        head = lax.slice_in_dim(cells, 0, width, axis=dim)
        tail = lax.slice_in_dim(cells, cells.shape[dim] - width, cells.shape[dim], axis=dim)
        cells = jnp.concatenate(
            [
                lax.ppermute(tail, axis, [(i, (i + 1) % count) for i in range(ends)]),
                cells,
                lax.ppermute(head, axis, [((i + 1) % count, i) for i in range(ends)]),
            ],
            axis=dim,
        )
    return cells


def second_along_flat(flat, depth):
    width = flat.shape[-1]
    padded = jnp.pad(flat, [(0, 0)] * (flat.ndim - 1) + [(2, 2)])
    spot = lax.broadcasted_iota(jnp.int32, (width,), 0) % depth

    def piece(offset):
        shifted = lax.slice_in_dim(padded, 2 + offset, 2 + offset + width, axis=flat.ndim - 1)
        if offset == 0:
            return shifted
        inside = (spot + offset >= 0) & (spot + offset < depth)
        return jnp.where(inside, shifted, 0.0)

    return FAR * (piece(-2) + piece(2)) + NEAR * (piece(-1) + piece(1)) + CENTER * piece(0)


def second_along(padded, axis, count):

    def piece(offset):
        return lax.slice_in_dim(padded, 2 + offset, 2 + offset + count, axis=axis)

    return FAR * (piece(-2) + piece(2)) + NEAR * (piece(-1) + piece(1)) + CENTER * piece(0)


MESH = pl.DeviceIdType.MESH


def spans_of(count):
    spans = []
    span = 1
    while 2 * span < count:
        spans.append(span)
        span *= 2
    return spans, span + 1


def sweep_kernel(count, f_ref, d_ref, o_ref, state, landed, send_sem, recv_sem):
    me = lax.axis_index("layer")
    row = lax.axis_index("xs")
    layers = f_ref.shape[1]
    width = f_ref.shape[3]
    spans, far = spans_of(count)
    hops = spans + [1, far]
    barrier = pltpu.get_barrier_semaphore()
    for hop in hops:
        for sign in (1, -1):
            pl.semaphore_signal(
                barrier, inc=1, device_id=(lax.rem(me + sign * hop + count, count), row),
                device_id_type=MESH,
            )
    pl.semaphore_wait(barrier, 2 * len(hops))

    rates = [d_ref[index] for index in range(layers)]
    through = rates[0]
    for index in range(1, layers):
        through = through * rates[index]

    def put(direction, slot, ends, keep):
        state[direction, slot, :, :, :width] = ends
        state[direction, slot, :, :, width:] = jnp.broadcast_to(keep[None], (2,) + keep.shape[:1] + (128,))

    def send(direction, slot, target_slot, hop, sign):
        copy = pltpu.make_async_remote_copy(
            src_ref=state.at[direction, slot],
            dst_ref=landed.at[direction, target_slot],
            send_sem=send_sem.at[direction, target_slot],
            recv_sem=recv_sem.at[direction, target_slot],
            device_id=(lax.rem(me + sign * hop + count, count), row),
            device_id_type=MESH,
        )
        copy.start()
        return copy

    def scan(direction, ends, sign):
        put(direction, 0, ends, through)
        for slot, hop in enumerate(spans):
            send(direction, slot, slot, hop, sign).wait()
            source = me - hop if sign == 1 else me + hop
            valid = ((source >= 0) & (source < count)).astype(jnp.float32)
            mine = state[direction, slot]
            got = landed[direction, slot]
            keep = mine[0, :, width:width + 1]
            put(
                direction, slot + 1,
                mine[:, :, :width] + (valid * keep)[None] * got[:, :, :width],
                keep * (valid * got[0, :, width:width + 1]),
            )
        last = len(spans)
        near = send(direction, last, last, 1, sign)
        distant = send(direction, last, last + 1, far, sign)
        near.wait()
        distant.wait()
        near_source = me - 1 if sign == 1 else me + 1
        far_source = me - far if sign == 1 else me + far
        near_valid = ((near_source >= 0) & (near_source < count)).astype(jnp.float32)
        far_valid = ((far_source >= 0) & (far_source < count)).astype(jnp.float32)
        got = landed[direction, last]
        result = got[:, :, :width]
        if far < count:
            result = result + (far_valid * got[0, :, width:width + 1])[None] * landed[direction, last + 1, :, :, :width]
        return near_valid * result

    state_now = None
    ahead = []
    for index in range(layers):
        source = f_ref[:, index]
        if state_now is None:
            state_now = (1.0 - rates[index])[None] * source
        else:
            state_now = rates[index][None] * state_now + (1.0 - rates[index])[None] * source
        ahead.append(state_now)
    entering = scan(0, state_now, 1)
    lower = rates[0]
    for index in range(layers):
        if index > 0:
            lower = lower * rates[index]
        ahead[index] = ahead[index] + lower[None] * entering
    state_now = None
    back = [None] * layers
    for index in reversed(range(layers)):
        if state_now is None:
            state_now = (1.0 - rates[index])[None] * ahead[index]
        else:
            state_now = rates[index][None] * state_now + (1.0 - rates[index])[None] * ahead[index]
        back[index] = state_now
    from_above = scan(1, state_now, -1)
    upper = rates[layers - 1]
    for index in reversed(range(layers)):
        if index < layers - 1:
            upper = upper * rates[index]
        o_ref[:, index] = back[index] + upper[None] * from_above


def exchange_kernel(count, layer_count, nodes_ref, weights_ref, ext_ref, probe_ref, out_ref, gathered, swept, send_sem, recv_sem, back_send, back_recv):
    me = lax.axis_index("layer")
    row = lax.axis_index("xs")
    layers = layer_count
    barrier = pltpu.get_barrier_semaphore()

    def greet(step, carry):
        pl.semaphore_signal(
            barrier, inc=1, device_id=(lax.rem(me + step, count), row), device_id_type=MESH
        )
        return carry

    lax.fori_loop(1, count, greet, 0)
    pl.semaphore_wait(barrier, count - 1)

    def outgoing(step, carry):
        target = lax.rem(me + step, count)
        pltpu.make_async_remote_copy(
            src_ref=ext_ref.at[target],
            dst_ref=gathered.at[me],
            send_sem=send_sem.at[step],
            recv_sem=recv_sem.at[step],
            device_id=(target, row),
            device_id_type=MESH,
        ).start()
        return carry

    lax.fori_loop(1, count, outgoing, 0)
    gathered[me] = ext_ref[me]

    def arrived(step, carry):
        copy = pltpu.make_async_remote_copy(
            src_ref=ext_ref.at[me],
            dst_ref=gathered.at[lax.rem(me + count - step, count)],
            send_sem=send_sem.at[step],
            recv_sem=recv_sem.at[step],
            device_id=(lax.rem(me + step, count), row),
            device_id_type=MESH,
        )
        copy.wait_send()
        copy.wait_recv()
        return carry

    lax.fori_loop(1, count, arrived, 0)

    half = out_ref.shape[3]
    rows_per_layer = 2 * half
    zero = jnp.zeros((half, out_ref.shape[4]), jnp.float32)
    data_rows = layers * half
    total = count * layers
    w0 = w1 = w2 = None
    for node in range(nodes_ref.shape[0]):
        weight = weights_ref[node]
        scaled = weight * nodes_ref[node]
        if w0 is None:
            w0, w1, w2 = weight, scaled, scaled * nodes_ref[node]
        else:
            w0, w1, w2 = w0 + weight, w1 + scaled, w2 + scaled * nodes_ref[node]

    def probe_at(place):
        inside = ((place >= 0) & (place < total)).astype(jnp.float32)
        place = jnp.clip(place, 0, total - 1)
        source = place // layers
        layer = place - source * layers
        return inside * probe_ref[source, pl.ds(layer * half, half), :]

    def prepare(source, carry):
        for layer in range(layers):
            place = source * layers + layer
            here = probe_ref[source, pl.ds(layer * half, half), :]
            partial = gathered[source, pl.ds(layer * half, half), :]
            second = (
                FAR * (probe_at(place - 2) + probe_at(place + 2))
                + NEAR * (probe_at(place - 1) + probe_at(place + 1))
                + CENTER * here
            )
            hamil = partial - 0.5 * second
            swept[source, 0, layer] = w0 * hamil - w1 * here
            swept[source, 1, layer] = w1 * hamil - w2 * here
        return carry

    lax.fori_loop(0, count, prepare, 0)

    def forward(source, state):
        for layer in range(layers):
            rate = probe_ref[source, pl.ds(data_rows + layer, 1), :]
            state = tuple(
                rate * state[m] + (1.0 - rate) * swept[source, m, layer] for m in range(2)
            )
            for m in range(2):
                swept[source, m, layer] = state[m]
        return state

    lax.fori_loop(0, count, forward, (zero, zero))

    def backward(step, state):
        source = count - 1 - step
        for layer in reversed(range(layers)):
            rate = probe_ref[source, pl.ds(data_rows + layer, 1), :]
            state = tuple(
                rate * state[m] + (1.0 - rate) * swept[source, m, layer] for m in range(2)
            )
            for m in range(2):
                swept[source, m, layer] = state[m]
        return state

    lax.fori_loop(0, count, backward, (zero, zero))

    def returning(step, carry):
        target = lax.rem(me + step, count)
        pltpu.make_async_remote_copy(
            src_ref=swept.at[target],
            dst_ref=out_ref.at[:, :, me],
            send_sem=back_send.at[step],
            recv_sem=back_recv.at[step],
            device_id=(target, row),
            device_id_type=MESH,
        ).start()
        return carry

    lax.fori_loop(1, count, returning, 0)
    out_ref[:, :, me] = swept[me]

    def returned(step, carry):
        copy = pltpu.make_async_remote_copy(
            src_ref=swept.at[me],
            dst_ref=out_ref.at[:, :, lax.rem(me + count - step, count)],
            send_sem=back_send.at[step],
            recv_sem=back_recv.at[step],
            device_id=(lax.rem(me + step, count), row),
            device_id_type=MESH,
        )
        copy.wait_send()
        copy.wait_recv()
        return carry

    lax.fori_loop(1, count, returned, 0)


def sweeps(ext, gathered_probes, nodes, weights, width):
    columns, data_rows, _ = ext.shape
    tiles = width // 128
    layers = data_rows // tiles
    moments = 2
    count = lax.axis_size("layer")
    if columns != count:
        raise ValueError("columns")
    vmem = pl.BlockSpec(memory_space=pltpu.VMEM)
    out = pl.pallas_call(
        functools.partial(exchange_kernel, count, layers),
        out_shape=jax.ShapeDtypeStruct((moments, layers, columns, tiles, 128), jnp.float32),
        in_specs=[pl.BlockSpec(memory_space=pltpu.SMEM)] * 2 + [vmem, vmem],
        out_specs=vmem,
        scratch_shapes=[
            pltpu.VMEM((count, data_rows, 128), jnp.float32),
            pltpu.VMEM((count, moments, layers, tiles, 128), jnp.float32),
            pltpu.SemaphoreType.DMA((count,)),
            pltpu.SemaphoreType.DMA((count,)),
            pltpu.SemaphoreType.DMA((count,)),
            pltpu.SemaphoreType.DMA((count,)),
        ],
        compiler_params=pltpu.CompilerParams(collective_id=0, has_side_effects=True),
    )(nodes, weights, ext, gathered_probes)
    return out.reshape(moments, layers, columns, width)


def front_kernel(row_count, layer_count, depth, block_ref, coef_ref, pieces_ref, across, total, regrouped,
                 left, right, gathered, send_sem, recv_sem, piece_send, piece_recv):
    me = lax.axis_index("layer")
    row = lax.axis_index("xs")
    peers = row_count - 1
    barrier = pltpu.get_barrier_semaphore()
    for step in range(1, row_count):
        pl.semaphore_signal(
            barrier, inc=1, device_id=(me, lax.rem(row + step, row_count)), device_id_type=MESH
        )

    def greet(step, carry):
        pl.semaphore_signal(
            barrier, inc=1, device_id=(lax.rem(me + step, layer_count), row), device_id_type=MESH
        )
        return carry

    lax.fori_loop(1, layer_count, greet, 0)
    pl.semaphore_wait(barrier, peers + layer_count - 1)

    def outgoing(step, carry):
        target = lax.rem(me + step, layer_count)
        pltpu.make_async_remote_copy(
            src_ref=pieces_ref.at[target],
            dst_ref=regrouped.at[me],
            send_sem=piece_send.at[step],
            recv_sem=piece_recv.at[step],
            device_id=(target, row),
            device_id_type=MESH,
        ).start()
        return carry

    copies = []
    targets = [
        (left, (me, lax.rem(row + 1, row_count))),
        (right, (me, lax.rem(row + row_count - 1, row_count))),
    ]
    for slot, (dst, device) in enumerate(targets):
        copies.append(
            pltpu.make_async_remote_copy(
                src_ref=block_ref, dst_ref=dst, send_sem=send_sem.at[slot], recv_sem=recv_sem.at[slot],
                device_id=device, device_id_type=MESH,
            )
        )
    for step in range(1, row_count):
        copies.append(
            pltpu.make_async_remote_copy(
                src_ref=coef_ref, dst_ref=gathered.at[step - 1], send_sem=send_sem.at[1 + step],
                recv_sem=recv_sem.at[1 + step], device_id=(me, lax.rem(row + step, row_count)),
                device_id_type=MESH,
            )
        )
    for copy in copies:
        copy.start()
    lax.fori_loop(1, layer_count, outgoing, 0)
    regrouped[me] = pieces_ref[me]
    for copy in copies[2:]:
        copy.wait()
    acc = coef_ref[...]
    for step in range(peers):
        acc = acc + gathered[step]
    total[...] = acc
    for copy in copies[:2]:
        copy.wait()
    before = left[...] * (row > 0).astype(jnp.float32)
    after = right[...] * (row < row_count - 1).astype(jnp.float32)
    mine = block_ref[...]
    segment = depth // 128
    for layer in range(block_ref.shape[1] // (2 * segment)):
        first = slice(2 * layer * segment, (2 * layer + 1) * segment)
        second = slice((2 * layer + 1) * segment, (2 * layer + 2) * segment)
        across[:, first] = (
            FAR * (before[:, first] + after[:, first])
            + NEAR * (before[:, second] + mine[:, second])
            + CENTER * mine[:, first]
        )
        across[:, second] = (
            FAR * (before[:, second] + after[:, second])
            + NEAR * (mine[:, first] + after[:, first])
            + CENTER * mine[:, second]
        )

    def arrived(step, carry):
        copy = pltpu.make_async_remote_copy(
            src_ref=pieces_ref.at[me],
            dst_ref=regrouped.at[lax.rem(me + layer_count - step, layer_count)],
            send_sem=piece_send.at[step],
            recv_sem=piece_recv.at[step],
            device_id=(lax.rem(me + step, layer_count), row),
            device_id_type=MESH,
        )
        copy.wait_send()
        copy.wait_recv()
        return carry

    lax.fori_loop(1, layer_count, arrived, 0)


def front_exchange(body, coef, depth, decay_rates):
    row_count = lax.axis_size("xs")
    layer_count = lax.axis_size("layer")
    columns, data_rows, _ = body.shape
    layers = decay_rates.shape[0]
    padded_rows = -(-(data_rows + layers) // 8) * 8
    lanes = jnp.broadcast_to(jnp.transpose(decay_rates)[:, :, None], (columns, layers, 128))
    spare = jnp.zeros((columns, padded_rows - data_rows - layers, 128), jnp.float32)
    pieces = jnp.concatenate([body, lanes, spare], axis=1)
    block = body
    spec = pl.BlockSpec(memory_space=pltpu.VMEM)
    return pl.pallas_call(
        functools.partial(front_kernel, row_count, layer_count, depth),
        out_shape=[jax.ShapeDtypeStruct(block.shape, jnp.float32)]
        + [jax.ShapeDtypeStruct(coef.shape, jnp.float32),
           jax.ShapeDtypeStruct((layer_count,) + pieces.shape[1:], jnp.float32)],
        in_specs=[spec, spec, spec],
        out_specs=[spec] * 3,
        scratch_shapes=[
            pltpu.VMEM(block.shape, jnp.float32),
            pltpu.VMEM(block.shape, jnp.float32),
            pltpu.VMEM((row_count - 1,) + coef.shape, jnp.float32),
            pltpu.SemaphoreType.DMA((1 + row_count,)),
            pltpu.SemaphoreType.DMA((1 + row_count,)),
            pltpu.SemaphoreType.DMA((layer_count,)),
            pltpu.SemaphoreType.DMA((layer_count,)),
        ],
        compiler_params=pltpu.CompilerParams(collective_id=1, has_side_effects=True),
    )(block, coef, pieces)


def shards(
    probes,
    potential,
    projector,
    intersection_ids,
    strength,
    decay_rates,
    contour_nodes,
    node_weights,
):
    layers, columns, rows, depth = probes.shape
    width = rows * depth
    flat = jnp.transpose(probes, (1, 0, 2, 3)).reshape(columns, layers, width)
    rounded = flat.astype(jnp.bfloat16)
    slot_coef = jnp.einsum("lsp,clp->lsc", projector, rounded, preferred_element_type=jnp.float32)
    onehot = (intersection_ids[:, :, None] == jnp.arange(NPROJ, dtype=jnp.int32)).astype(
        jnp.float32
    )
    partial_coef = jnp.einsum("lsq,lsc->lcq", onehot, slot_coef, precision=lax.Precision.HIGHEST)
    if rows != 2:
        raise ValueError("rows")
    along_rows, coef, regrouped = front_exchange(
        flat.reshape(columns, layers * width // 128, 128), partial_coef, depth, decay_rates
    )
    laplace = along_rows.reshape(columns, layers, width) + second_along_flat(flat, depth)
    coef = jnp.swapaxes(coef, 1, 2)
    scaled = (strength[:, :, None] * coef).astype(jnp.bfloat16)
    slot_back = jnp.einsum(
        "lsq,lqc->lsc", onehot.astype(jnp.bfloat16), scaled, preferred_element_type=jnp.float32
    ).astype(jnp.bfloat16)
    projected = jnp.einsum(
        "lsp,lsc->clp", projector, slot_back, preferred_element_type=jnp.float32
    )
    partial = -0.5 * laplace + potential.reshape(1, layers, width) * flat + projected
    swept = sweeps(
        partial.reshape(columns, layers * width // 128, 128), regrouped, contour_nodes, node_weights,
        width,
    )
    return swept.reshape(2, layers, columns, rows, depth)


def solution(mesh):
    in_specs = (
        P("layer", None, "xs", None),
        P("layer", "xs", None),
        P("layer", "xs", None),
        P("layer", "xs"),
        P("layer", None),
        P("layer", None),
        P(),
        P(),
    )
    out_specs = P(None, "layer", None, "xs", None)
    return jax.shard_map(shards, mesh=mesh, in_specs=in_specs, out_specs=out_specs, check_vma=False)
```

```python
import functools

import jax
import jax.numpy as jnp
from jax import lax
from jax.experimental import pallas as pl
from jax.experimental.pallas import tpu as pltpu
from jax.sharding import PartitionSpec as P

NPROJ = 256


FAR = -1.0 / 12.0
NEAR = 4.0 / 3.0
CENTER = -2.5


def with_halo(cells, sides, width):
    for axis, dim in sides:
        count = lax.axis_size(axis)
        ends = count - 1
        head = lax.slice_in_dim(cells, 0, width, axis=dim)
        tail = lax.slice_in_dim(cells, cells.shape[dim] - width, cells.shape[dim], axis=dim)
        cells = jnp.concatenate(
            [
                lax.ppermute(tail, axis, [(i, (i + 1) % count) for i in range(ends)]),
                cells,
                lax.ppermute(head, axis, [((i + 1) % count, i) for i in range(ends)]),
            ],
            axis=dim,
        )
    return cells


def second_along_flat(flat, depth):
    width = flat.shape[-1]
    padded = jnp.pad(flat, [(0, 0)] * (flat.ndim - 1) + [(2, 2)])
    spot = lax.broadcasted_iota(jnp.int32, (width,), 0) % depth

    def piece(offset):
        shifted = lax.slice_in_dim(padded, 2 + offset, 2 + offset + width, axis=flat.ndim - 1)
        if offset == 0:
            return shifted
        inside = (spot + offset >= 0) & (spot + offset < depth)
        return jnp.where(inside, shifted, 0.0)

    return FAR * (piece(-2) + piece(2)) + NEAR * (piece(-1) + piece(1)) + CENTER * piece(0)


def second_along(padded, axis, count):

    def piece(offset):
        return lax.slice_in_dim(padded, 2 + offset, 2 + offset + count, axis=axis)

    return FAR * (piece(-2) + piece(2)) + NEAR * (piece(-1) + piece(1)) + CENTER * piece(0)


MESH = pl.DeviceIdType.MESH


def spans_of(count):
    spans = []
    span = 1
    while 2 * span < count:
        spans.append(span)
        span *= 2
    return spans, span + 1


def sweep_kernel(count, f_ref, d_ref, o_ref, state, landed, send_sem, recv_sem):
    me = lax.axis_index("layer")
    row = lax.axis_index("xs")
    layers = f_ref.shape[1]
    width = f_ref.shape[3]
    spans, far = spans_of(count)
    hops = spans + [1, far]
    barrier = pltpu.get_barrier_semaphore()
    for hop in hops:
        for sign in (1, -1):
            pl.semaphore_signal(
                barrier, inc=1, device_id=(lax.rem(me + sign * hop + count, count), row),
                device_id_type=MESH,
            )
    pl.semaphore_wait(barrier, 2 * len(hops))

    rates = [d_ref[index] for index in range(layers)]
    through = rates[0]
    for index in range(1, layers):
        through = through * rates[index]

    def put(direction, slot, ends, keep):
        state[direction, slot, :, :, :width] = ends
        state[direction, slot, :, :, width:] = jnp.broadcast_to(keep[None], (2,) + keep.shape[:1] + (128,))

    def send(direction, slot, target_slot, hop, sign):
        copy = pltpu.make_async_remote_copy(
            src_ref=state.at[direction, slot],
            dst_ref=landed.at[direction, target_slot],
            send_sem=send_sem.at[direction, target_slot],
            recv_sem=recv_sem.at[direction, target_slot],
            device_id=(lax.rem(me + sign * hop + count, count), row),
            device_id_type=MESH,
        )
        copy.start()
        return copy

    def scan(direction, ends, sign):
        put(direction, 0, ends, through)
        for slot, hop in enumerate(spans):
            send(direction, slot, slot, hop, sign).wait()
            source = me - hop if sign == 1 else me + hop
            valid = ((source >= 0) & (source < count)).astype(jnp.float32)
            mine = state[direction, slot]
            got = landed[direction, slot]
            keep = mine[0, :, width:width + 1]
            put(
                direction, slot + 1,
                mine[:, :, :width] + (valid * keep)[None] * got[:, :, :width],
                keep * (valid * got[0, :, width:width + 1]),
            )
        last = len(spans)
        near = send(direction, last, last, 1, sign)
        distant = send(direction, last, last + 1, far, sign)
        near.wait()
        distant.wait()
        near_source = me - 1 if sign == 1 else me + 1
        far_source = me - far if sign == 1 else me + far
        near_valid = ((near_source >= 0) & (near_source < count)).astype(jnp.float32)
        far_valid = ((far_source >= 0) & (far_source < count)).astype(jnp.float32)
        got = landed[direction, last]
        result = got[:, :, :width]
        if far < count:
            result = result + (far_valid * got[0, :, width:width + 1])[None] * landed[direction, last + 1, :, :, :width]
        return near_valid * result

    state_now = None
    ahead = []
    for index in range(layers):
        source = f_ref[:, index]
        if state_now is None:
            state_now = (1.0 - rates[index])[None] * source
        else:
            state_now = rates[index][None] * state_now + (1.0 - rates[index])[None] * source
        ahead.append(state_now)
    entering = scan(0, state_now, 1)
    lower = rates[0]
    for index in range(layers):
        if index > 0:
            lower = lower * rates[index]
        ahead[index] = ahead[index] + lower[None] * entering
    state_now = None
    back = [None] * layers
    for index in reversed(range(layers)):
        if state_now is None:
            state_now = (1.0 - rates[index])[None] * ahead[index]
        else:
            state_now = rates[index][None] * state_now + (1.0 - rates[index])[None] * ahead[index]
        back[index] = state_now
    from_above = scan(1, state_now, -1)
    upper = rates[layers - 1]
    for index in reversed(range(layers)):
        if index < layers - 1:
            upper = upper * rates[index]
        o_ref[:, index] = back[index] + upper[None] * from_above


def exchange_kernel(count, layer_count, nodes_ref, weights_ref, ext_ref, probe_ref, out_ref, gathered, swept, send_sem, recv_sem, back_send, back_recv):
    me = lax.axis_index("layer")
    row = lax.axis_index("xs")
    layers = layer_count
    barrier = pltpu.get_barrier_semaphore()

    def greet(step, carry):
        pl.semaphore_signal(
            barrier, inc=1, device_id=(lax.rem(me + step, count), row), device_id_type=MESH
        )
        return carry

    lax.fori_loop(1, count, greet, 0)
    pl.semaphore_wait(barrier, count - 1)

    def outgoing(step, carry):
        target = lax.rem(me + step, count)
        pltpu.make_async_remote_copy(
            src_ref=ext_ref.at[target],
            dst_ref=gathered.at[me],
            send_sem=send_sem.at[step],
            recv_sem=recv_sem.at[step],
            device_id=(target, row),
            device_id_type=MESH,
        ).start()
        return carry

    lax.fori_loop(1, count, outgoing, 0)
    gathered[me] = ext_ref[me]

    def arrived(step, carry):
        copy = pltpu.make_async_remote_copy(
            src_ref=ext_ref.at[me],
            dst_ref=gathered.at[lax.rem(me + count - step, count)],
            send_sem=send_sem.at[step],
            recv_sem=recv_sem.at[step],
            device_id=(lax.rem(me + step, count), row),
            device_id_type=MESH,
        )
        copy.wait_send()
        copy.wait_recv()
        return carry

    lax.fori_loop(1, count, arrived, 0)

    half = out_ref.shape[3]
    rows_per_layer = 2 * half
    zero = jnp.zeros((half, out_ref.shape[4]), jnp.float32)
    data_rows = layers * half
    total = count * layers
    w0 = w1 = w2 = None
    for node in range(nodes_ref.shape[0]):
        weight = weights_ref[node]
        scaled = weight * nodes_ref[node]
        if w0 is None:
            w0, w1, w2 = weight, scaled, scaled * nodes_ref[node]
        else:
            w0, w1, w2 = w0 + weight, w1 + scaled, w2 + scaled * nodes_ref[node]

    def probe_at(place):
        inside = ((place >= 0) & (place < total)).astype(jnp.float32)
        place = jnp.clip(place, 0, total - 1)
        source = place // layers
        layer = place - source * layers
        return inside * probe_ref[source, pl.ds(layer * half, half), :]

    def forward(source, state):
        for layer in range(layers):
            place = source * layers + layer
            here = probe_ref[source, pl.ds(layer * half, half), :]
            partial = gathered[source, pl.ds(layer * half, half), :]
            second = (
                FAR * (probe_at(place - 2) + probe_at(place + 2))
                + NEAR * (probe_at(place - 1) + probe_at(place + 1))
                + CENTER * here
            )
            hamil = partial - 0.5 * second
            forcing = (w0 * hamil - w1 * here, w1 * hamil - w2 * here)
            rate = probe_ref[source, pl.ds(data_rows + layer, 1), :]
            state = tuple(rate * state[m] + (1.0 - rate) * forcing[m] for m in range(2))
            for m in range(2):
                swept[source, m, layer] = state[m]
        return state

    lax.fori_loop(0, count, forward, (zero, zero))

    def backward(step, state):
        source = count - 1 - step
        for layer in reversed(range(layers)):
            rate = probe_ref[source, pl.ds(data_rows + layer, 1), :]
            state = tuple(
                rate * state[m] + (1.0 - rate) * swept[source, m, layer] for m in range(2)
            )
            for m in range(2):
                swept[source, m, layer] = state[m]
        return state

    lax.fori_loop(0, count, backward, (zero, zero))

    def returning(step, carry):
        target = lax.rem(me + step, count)
        pltpu.make_async_remote_copy(
            src_ref=swept.at[target],
            dst_ref=out_ref.at[:, :, me],
            send_sem=back_send.at[step],
            recv_sem=back_recv.at[step],
            device_id=(target, row),
            device_id_type=MESH,
        ).start()
        return carry

    lax.fori_loop(1, count, returning, 0)
    out_ref[:, :, me] = swept[me]

    def returned(step, carry):
        copy = pltpu.make_async_remote_copy(
            src_ref=swept.at[me],
            dst_ref=out_ref.at[:, :, lax.rem(me + count - step, count)],
            send_sem=back_send.at[step],
            recv_sem=back_recv.at[step],
            device_id=(lax.rem(me + step, count), row),
            device_id_type=MESH,
        )
        copy.wait_send()
        copy.wait_recv()
        return carry

    lax.fori_loop(1, count, returned, 0)


def sweeps(partial, gathered_probes, decay_rates, nodes, weights):
    layers, columns, width = partial.shape
    moments = 2
    count = lax.axis_size("layer")
    if columns != count:
        raise ValueError("columns")
    tiles = width // 128
    data_rows = layers * tiles
    ext = jnp.transpose(partial, (1, 0, 2)).reshape(columns, data_rows, 128)
    vmem = pl.BlockSpec(memory_space=pltpu.VMEM)
    out = pl.pallas_call(
        functools.partial(exchange_kernel, count, layers),
        out_shape=jax.ShapeDtypeStruct((moments, layers, columns, tiles, 128), jnp.float32),
        in_specs=[pl.BlockSpec(memory_space=pltpu.SMEM)] * 2 + [vmem, vmem],
        out_specs=vmem,
        scratch_shapes=[
            pltpu.VMEM((count, data_rows, 128), jnp.float32),
            pltpu.VMEM((count, moments, layers, tiles, 128), jnp.float32),
            pltpu.SemaphoreType.DMA((count,)),
            pltpu.SemaphoreType.DMA((count,)),
            pltpu.SemaphoreType.DMA((count,)),
            pltpu.SemaphoreType.DMA((count,)),
        ],
        compiler_params=pltpu.CompilerParams(collective_id=0, has_side_effects=True),
    )(nodes, weights, ext, gathered_probes)
    return out.reshape(moments, layers, columns, width)


def front_kernel(row_count, layer_count, depth, block_ref, coef_ref, pieces_ref, across, total, regrouped,
                 left, right, gathered, send_sem, recv_sem, piece_send, piece_recv):
    me = lax.axis_index("layer")
    row = lax.axis_index("xs")
    peers = row_count - 1
    barrier = pltpu.get_barrier_semaphore()
    for step in range(1, row_count):
        pl.semaphore_signal(
            barrier, inc=1, device_id=(me, lax.rem(row + step, row_count)), device_id_type=MESH
        )

    def greet(step, carry):
        pl.semaphore_signal(
            barrier, inc=1, device_id=(lax.rem(me + step, layer_count), row), device_id_type=MESH
        )
        return carry

    lax.fori_loop(1, layer_count, greet, 0)
    pl.semaphore_wait(barrier, peers + layer_count - 1)

    def outgoing(step, carry):
        target = lax.rem(me + step, layer_count)
        pltpu.make_async_remote_copy(
            src_ref=pieces_ref.at[target],
            dst_ref=regrouped.at[me],
            send_sem=piece_send.at[step],
            recv_sem=piece_recv.at[step],
            device_id=(target, row),
            device_id_type=MESH,
        ).start()
        return carry

    copies = []
    targets = [
        (left, (me, lax.rem(row + 1, row_count))),
        (right, (me, lax.rem(row + row_count - 1, row_count))),
    ]
    for slot, (dst, device) in enumerate(targets):
        copies.append(
            pltpu.make_async_remote_copy(
                src_ref=block_ref, dst_ref=dst, send_sem=send_sem.at[slot], recv_sem=recv_sem.at[slot],
                device_id=device, device_id_type=MESH,
            )
        )
    for step in range(1, row_count):
        copies.append(
            pltpu.make_async_remote_copy(
                src_ref=coef_ref, dst_ref=gathered.at[step - 1], send_sem=send_sem.at[1 + step],
                recv_sem=recv_sem.at[1 + step], device_id=(me, lax.rem(row + step, row_count)),
                device_id_type=MESH,
            )
        )
    for copy in copies:
        copy.start()
    lax.fori_loop(1, layer_count, outgoing, 0)
    regrouped[me] = pieces_ref[me]
    for copy in copies[2:]:
        copy.wait()
    acc = coef_ref[...]
    for step in range(peers):
        acc = acc + gathered[step]
    total[...] = acc
    for copy in copies[:2]:
        copy.wait()
    before = left[...] * (row > 0).astype(jnp.float32)
    after = right[...] * (row < row_count - 1).astype(jnp.float32)
    mine = block_ref[...]
    first, second = slice(0, depth), slice(depth, 2 * depth)
    across[:, :, first] = (
        FAR * (before[:, :, first] + after[:, :, first])
        + NEAR * (before[:, :, second] + mine[:, :, second])
        + CENTER * mine[:, :, first]
    )
    across[:, :, second] = (
        FAR * (before[:, :, second] + after[:, :, second])
        + NEAR * (mine[:, :, first] + after[:, :, first])
        + CENTER * mine[:, :, second]
    )

    def arrived(step, carry):
        copy = pltpu.make_async_remote_copy(
            src_ref=pieces_ref.at[me],
            dst_ref=regrouped.at[lax.rem(me + layer_count - step, layer_count)],
            send_sem=piece_send.at[step],
            recv_sem=piece_recv.at[step],
            device_id=(lax.rem(me + step, layer_count), row),
            device_id_type=MESH,
        )
        copy.wait_send()
        copy.wait_recv()
        return carry

    lax.fori_loop(1, layer_count, arrived, 0)


def front_exchange(block, coef, depth, decay_rates):
    row_count = lax.axis_size("xs")
    layer_count = lax.axis_size("layer")
    layers, columns, width = block.shape
    data_rows = layers * width // 128
    padded_rows = -(-(data_rows + layers) // 8) * 8
    body = jnp.transpose(block, (1, 0, 2)).reshape(columns, data_rows, 128)
    lanes = jnp.broadcast_to(jnp.transpose(decay_rates)[:, :, None], (columns, layers, 128))
    spare = jnp.zeros((columns, padded_rows - data_rows - layers, 128), jnp.float32)
    pieces = jnp.concatenate([body, lanes, spare], axis=1)
    spec = pl.BlockSpec(memory_space=pltpu.VMEM)
    return pl.pallas_call(
        functools.partial(front_kernel, row_count, layer_count, depth),
        out_shape=[jax.ShapeDtypeStruct(block.shape, jnp.float32)]
        + [jax.ShapeDtypeStruct(coef.shape, jnp.float32),
           jax.ShapeDtypeStruct((layer_count,) + pieces.shape[1:], jnp.float32)],
        in_specs=[spec, spec, spec],
        out_specs=[spec] * 3,
        scratch_shapes=[
            pltpu.VMEM(block.shape, jnp.float32),
            pltpu.VMEM(block.shape, jnp.float32),
            pltpu.VMEM((row_count - 1,) + coef.shape, jnp.float32),
            pltpu.SemaphoreType.DMA((1 + row_count,)),
            pltpu.SemaphoreType.DMA((1 + row_count,)),
            pltpu.SemaphoreType.DMA((layer_count,)),
            pltpu.SemaphoreType.DMA((layer_count,)),
        ],
        compiler_params=pltpu.CompilerParams(collective_id=1, has_side_effects=True),
    )(block, coef, pieces)


def shards(
    probes,
    potential,
    projector,
    intersection_ids,
    strength,
    decay_rates,
    contour_nodes,
    node_weights,
):
    layers, columns, rows, depth = probes.shape
    flat = probes.reshape(layers, columns, rows * depth)
    rounded = flat.astype(jnp.bfloat16)
    slot_coef = jnp.einsum("lsp,lcp->lsc", projector, rounded, preferred_element_type=jnp.float32)
    onehot = (intersection_ids[:, :, None] == jnp.arange(NPROJ, dtype=jnp.int32)).astype(
        jnp.float32
    )
    partial_coef = jnp.einsum("lsq,lsc->lcq", onehot, slot_coef, precision=lax.Precision.HIGHEST)
    if rows != 2:
        raise ValueError("rows")
    along_rows, coef, regrouped = front_exchange(flat, partial_coef, depth, decay_rates)
    laplace = along_rows + second_along_flat(flat, depth)
    coef = jnp.swapaxes(coef, 1, 2)
    scaled = (strength[:, :, None] * coef).astype(jnp.bfloat16)
    slot_back = jnp.einsum(
        "lsq,lqc->lsc", onehot.astype(jnp.bfloat16), scaled, preferred_element_type=jnp.float32
    ).astype(jnp.bfloat16)
    projected = jnp.einsum(
        "lsp,lsc->lcp", projector, slot_back, preferred_element_type=jnp.float32
    )
    partial = -0.5 * laplace + potential.reshape(layers, 1, rows * depth) * flat + projected
    swept = sweeps(
        partial, regrouped, decay_rates, contour_nodes,
        node_weights,
    )
    return swept.reshape(2, layers, columns, rows, depth)


def solution(mesh):
    in_specs = (
        P("layer", None, "xs", None),
        P("layer", "xs", None),
        P("layer", "xs", None),
        P("layer", "xs"),
        P("layer", None),
        P("layer", None),
        P(),
        P(),
    )
    out_specs = P(None, "layer", None, "xs", None)
    return jax.shard_map(shards, mesh=mesh, in_specs=in_specs, out_specs=out_specs, check_vma=False)
```

```python
import functools

import jax
import jax.numpy as jnp
from jax import lax
from jax.experimental import pallas as pl
from jax.experimental.pallas import tpu as pltpu
from jax.sharding import PartitionSpec as P

NPROJ = 256


FAR = -1.0 / 12.0
NEAR = 4.0 / 3.0
CENTER = -2.5


def with_halo(cells, sides, width):
    for axis, dim in sides:
        count = lax.axis_size(axis)
        ends = count - 1
        head = lax.slice_in_dim(cells, 0, width, axis=dim)
        tail = lax.slice_in_dim(cells, cells.shape[dim] - width, cells.shape[dim], axis=dim)
        cells = jnp.concatenate(
            [
                lax.ppermute(tail, axis, [(i, (i + 1) % count) for i in range(ends)]),
                cells,
                lax.ppermute(head, axis, [((i + 1) % count, i) for i in range(ends)]),
            ],
            axis=dim,
        )
    return cells


def second_along_flat(flat, depth):
    width = flat.shape[-1]
    padded = jnp.pad(flat, [(0, 0)] * (flat.ndim - 1) + [(2, 2)])
    spot = lax.broadcasted_iota(jnp.int32, (width,), 0) % depth

    def piece(offset):
        shifted = lax.slice_in_dim(padded, 2 + offset, 2 + offset + width, axis=flat.ndim - 1)
        if offset == 0:
            return shifted
        inside = (spot + offset >= 0) & (spot + offset < depth)
        return jnp.where(inside, shifted, 0.0)

    return FAR * (piece(-2) + piece(2)) + NEAR * (piece(-1) + piece(1)) + CENTER * piece(0)


def second_along(padded, axis, count):

    def piece(offset):
        return lax.slice_in_dim(padded, 2 + offset, 2 + offset + count, axis=axis)

    return FAR * (piece(-2) + piece(2)) + NEAR * (piece(-1) + piece(1)) + CENTER * piece(0)


MESH = pl.DeviceIdType.MESH


def spans_of(count):
    spans = []
    span = 1
    while 2 * span < count:
        spans.append(span)
        span *= 2
    return spans, span + 1


def sweep_kernel(count, f_ref, d_ref, o_ref, state, landed, send_sem, recv_sem):
    me = lax.axis_index("layer")
    row = lax.axis_index("xs")
    layers = f_ref.shape[1]
    width = f_ref.shape[3]
    spans, far = spans_of(count)
    hops = spans + [1, far]
    barrier = pltpu.get_barrier_semaphore()
    for hop in hops:
        for sign in (1, -1):
            pl.semaphore_signal(
                barrier, inc=1, device_id=(lax.rem(me + sign * hop + count, count), row),
                device_id_type=MESH,
            )
    pl.semaphore_wait(barrier, 2 * len(hops))

    rates = [d_ref[index] for index in range(layers)]
    through = rates[0]
    for index in range(1, layers):
        through = through * rates[index]

    def put(direction, slot, ends, keep):
        state[direction, slot, :, :, :width] = ends
        state[direction, slot, :, :, width:] = jnp.broadcast_to(keep[None], (2,) + keep.shape[:1] + (128,))

    def send(direction, slot, target_slot, hop, sign):
        copy = pltpu.make_async_remote_copy(
            src_ref=state.at[direction, slot],
            dst_ref=landed.at[direction, target_slot],
            send_sem=send_sem.at[direction, target_slot],
            recv_sem=recv_sem.at[direction, target_slot],
            device_id=(lax.rem(me + sign * hop + count, count), row),
            device_id_type=MESH,
        )
        copy.start()
        return copy

    def scan(direction, ends, sign):
        put(direction, 0, ends, through)
        for slot, hop in enumerate(spans):
            send(direction, slot, slot, hop, sign).wait()
            source = me - hop if sign == 1 else me + hop
            valid = ((source >= 0) & (source < count)).astype(jnp.float32)
            mine = state[direction, slot]
            got = landed[direction, slot]
            keep = mine[0, :, width:width + 1]
            put(
                direction, slot + 1,
                mine[:, :, :width] + (valid * keep)[None] * got[:, :, :width],
                keep * (valid * got[0, :, width:width + 1]),
            )
        last = len(spans)
        near = send(direction, last, last, 1, sign)
        distant = send(direction, last, last + 1, far, sign)
        near.wait()
        distant.wait()
        near_source = me - 1 if sign == 1 else me + 1
        far_source = me - far if sign == 1 else me + far
        near_valid = ((near_source >= 0) & (near_source < count)).astype(jnp.float32)
        far_valid = ((far_source >= 0) & (far_source < count)).astype(jnp.float32)
        got = landed[direction, last]
        result = got[:, :, :width]
        if far < count:
            result = result + (far_valid * got[0, :, width:width + 1])[None] * landed[direction, last + 1, :, :, :width]
        return near_valid * result

    state_now = None
    ahead = []
    for index in range(layers):
        source = f_ref[:, index]
        if state_now is None:
            state_now = (1.0 - rates[index])[None] * source
        else:
            state_now = rates[index][None] * state_now + (1.0 - rates[index])[None] * source
        ahead.append(state_now)
    entering = scan(0, state_now, 1)
    lower = rates[0]
    for index in range(layers):
        if index > 0:
            lower = lower * rates[index]
        ahead[index] = ahead[index] + lower[None] * entering
    state_now = None
    back = [None] * layers
    for index in reversed(range(layers)):
        if state_now is None:
            state_now = (1.0 - rates[index])[None] * ahead[index]
        else:
            state_now = rates[index][None] * state_now + (1.0 - rates[index])[None] * ahead[index]
        back[index] = state_now
    from_above = scan(1, state_now, -1)
    upper = rates[layers - 1]
    for index in reversed(range(layers)):
        if index < layers - 1:
            upper = upper * rates[index]
        o_ref[:, index] = back[index] + upper[None] * from_above


def exchange_kernel(count, layer_count, nodes_ref, weights_ref, ext_ref, probe_ref, out_ref, gathered, swept, send_sem, recv_sem, back_send, back_recv):
    me = lax.axis_index("layer")
    row = lax.axis_index("xs")
    layers = layer_count
    barrier = pltpu.get_barrier_semaphore()

    def greet(step, carry):
        pl.semaphore_signal(
            barrier, inc=1, device_id=(lax.rem(me + step, count), row), device_id_type=MESH
        )
        return carry

    lax.fori_loop(1, count, greet, 0)
    pl.semaphore_wait(barrier, count - 1)

    def outgoing(step, carry):
        target = lax.rem(me + step, count)
        pltpu.make_async_remote_copy(
            src_ref=ext_ref.at[target],
            dst_ref=gathered.at[me],
            send_sem=send_sem.at[step],
            recv_sem=recv_sem.at[step],
            device_id=(target, row),
            device_id_type=MESH,
        ).start()
        return carry

    lax.fori_loop(1, count, outgoing, 0)
    gathered[me] = ext_ref[me]

    def arrived(step, carry):
        copy = pltpu.make_async_remote_copy(
            src_ref=ext_ref.at[me],
            dst_ref=gathered.at[lax.rem(me + count - step, count)],
            send_sem=send_sem.at[step],
            recv_sem=recv_sem.at[step],
            device_id=(lax.rem(me + step, count), row),
            device_id_type=MESH,
        )
        copy.wait_send()
        copy.wait_recv()
        return carry

    lax.fori_loop(1, count, arrived, 0)

    half = out_ref.shape[3]
    rows_per_layer = 2 * half
    zero = jnp.zeros((half, out_ref.shape[4]), jnp.float32)
    data_rows = layers * half
    total = count * layers
    w0 = w1 = w2 = None
    for node in range(nodes_ref.shape[0]):
        weight = weights_ref[node]
        scaled = weight * nodes_ref[node]
        if w0 is None:
            w0, w1, w2 = weight, scaled, scaled * nodes_ref[node]
        else:
            w0, w1, w2 = w0 + weight, w1 + scaled, w2 + scaled * nodes_ref[node]

    def probe_at(place):
        inside = ((place >= 0) & (place < total)).astype(jnp.float32)
        place = jnp.clip(place, 0, total - 1)
        source = place // layers
        layer = place - source * layers
        return inside * probe_ref[source, pl.ds(layer * half, half), :]

    def forward(source, state):
        for layer in range(layers):
            place = source * layers + layer
            here = probe_ref[source, pl.ds(layer * half, half), :]
            partial = gathered[source, pl.ds(layer * half, half), :]
            def near(offset):
                if 0 <= layer + offset < layers:
                    return probe_ref[source, pl.ds((layer + offset) * half, half), :]
                return probe_at(place + offset)

            second = (
                FAR * (near(-2) + near(2))
                + NEAR * (near(-1) + near(1))
                + CENTER * here
            )
            hamil = partial - 0.5 * second
            forcing = (w0 * hamil - w1 * here, w1 * hamil - w2 * here)
            rate = probe_ref[source, pl.ds(data_rows + layer, 1), :]
            state = tuple(rate * state[m] + (1.0 - rate) * forcing[m] for m in range(2))
            for m in range(2):
                swept[source, m, layer] = state[m]
        return state

    lax.fori_loop(0, count, forward, (zero, zero))

    def backward(step, state):
        source = count - 1 - step
        for layer in reversed(range(layers)):
            rate = probe_ref[source, pl.ds(data_rows + layer, 1), :]
            state = tuple(
                rate * state[m] + (1.0 - rate) * swept[source, m, layer] for m in range(2)
            )
            for m in range(2):
                swept[source, m, layer] = state[m]
        return state

    lax.fori_loop(0, count, backward, (zero, zero))

    def returning(step, carry):
        target = lax.rem(me + step, count)
        pltpu.make_async_remote_copy(
            src_ref=swept.at[target],
            dst_ref=out_ref.at[:, :, me],
            send_sem=back_send.at[step],
            recv_sem=back_recv.at[step],
            device_id=(target, row),
            device_id_type=MESH,
        ).start()
        return carry

    lax.fori_loop(1, count, returning, 0)
    out_ref[:, :, me] = swept[me]

    def returned(step, carry):
        copy = pltpu.make_async_remote_copy(
            src_ref=swept.at[me],
            dst_ref=out_ref.at[:, :, lax.rem(me + count - step, count)],
            send_sem=back_send.at[step],
            recv_sem=back_recv.at[step],
            device_id=(lax.rem(me + step, count), row),
            device_id_type=MESH,
        )
        copy.wait_send()
        copy.wait_recv()
        return carry

    lax.fori_loop(1, count, returned, 0)


def sweeps(partial, gathered_probes, decay_rates, nodes, weights):
    layers, columns, width = partial.shape
    moments = 2
    count = lax.axis_size("layer")
    if columns != count:
        raise ValueError("columns")
    tiles = width // 128
    data_rows = layers * tiles
    ext = jnp.transpose(partial, (1, 0, 2)).reshape(columns, data_rows, 128)
    vmem = pl.BlockSpec(memory_space=pltpu.VMEM)
    out = pl.pallas_call(
        functools.partial(exchange_kernel, count, layers),
        out_shape=jax.ShapeDtypeStruct((moments, layers, columns, tiles, 128), jnp.float32),
        in_specs=[pl.BlockSpec(memory_space=pltpu.SMEM)] * 2 + [vmem, vmem],
        out_specs=vmem,
        scratch_shapes=[
            pltpu.VMEM((count, data_rows, 128), jnp.float32),
            pltpu.VMEM((count, moments, layers, tiles, 128), jnp.float32),
            pltpu.SemaphoreType.DMA((count,)),
            pltpu.SemaphoreType.DMA((count,)),
            pltpu.SemaphoreType.DMA((count,)),
            pltpu.SemaphoreType.DMA((count,)),
        ],
        compiler_params=pltpu.CompilerParams(collective_id=0, has_side_effects=True),
    )(nodes, weights, ext, gathered_probes)
    return out.reshape(moments, layers, columns, width)


def front_kernel(row_count, layer_count, depth, block_ref, coef_ref, pieces_ref, across, total, regrouped,
                 left, right, gathered, send_sem, recv_sem, piece_send, piece_recv):
    me = lax.axis_index("layer")
    row = lax.axis_index("xs")
    peers = row_count - 1
    barrier = pltpu.get_barrier_semaphore()
    for step in range(1, row_count):
        pl.semaphore_signal(
            barrier, inc=1, device_id=(me, lax.rem(row + step, row_count)), device_id_type=MESH
        )

    def greet(step, carry):
        pl.semaphore_signal(
            barrier, inc=1, device_id=(lax.rem(me + step, layer_count), row), device_id_type=MESH
        )
        return carry

    lax.fori_loop(1, layer_count, greet, 0)
    pl.semaphore_wait(barrier, peers + layer_count - 1)

    def outgoing(step, carry):
        target = lax.rem(me + step, layer_count)
        pltpu.make_async_remote_copy(
            src_ref=pieces_ref.at[target],
            dst_ref=regrouped.at[me],
            send_sem=piece_send.at[step],
            recv_sem=piece_recv.at[step],
            device_id=(target, row),
            device_id_type=MESH,
        ).start()
        return carry

    copies = []
    targets = [
        (left, (me, lax.rem(row + 1, row_count))),
        (right, (me, lax.rem(row + row_count - 1, row_count))),
    ]
    for slot, (dst, device) in enumerate(targets):
        copies.append(
            pltpu.make_async_remote_copy(
                src_ref=block_ref, dst_ref=dst, send_sem=send_sem.at[slot], recv_sem=recv_sem.at[slot],
                device_id=device, device_id_type=MESH,
            )
        )
    for step in range(1, row_count):
        copies.append(
            pltpu.make_async_remote_copy(
                src_ref=coef_ref, dst_ref=gathered.at[step - 1], send_sem=send_sem.at[1 + step],
                recv_sem=recv_sem.at[1 + step], device_id=(me, lax.rem(row + step, row_count)),
                device_id_type=MESH,
            )
        )
    for copy in copies:
        copy.start()
    lax.fori_loop(1, layer_count, outgoing, 0)
    regrouped[me] = pieces_ref[me]
    for copy in copies[2:]:
        copy.wait()
    acc = coef_ref[...]
    for step in range(peers):
        acc = acc + gathered[step]
    total[...] = acc
    for copy in copies[:2]:
        copy.wait()
    before = left[...] * (row > 0).astype(jnp.float32)
    after = right[...] * (row < row_count - 1).astype(jnp.float32)
    mine = block_ref[...]
    first, second = slice(0, depth), slice(depth, 2 * depth)
    across[:, :, first] = (
        FAR * (before[:, :, first] + after[:, :, first])
        + NEAR * (before[:, :, second] + mine[:, :, second])
        + CENTER * mine[:, :, first]
    )
    across[:, :, second] = (
        FAR * (before[:, :, second] + after[:, :, second])
        + NEAR * (mine[:, :, first] + after[:, :, first])
        + CENTER * mine[:, :, second]
    )

    def arrived(step, carry):
        copy = pltpu.make_async_remote_copy(
            src_ref=pieces_ref.at[me],
            dst_ref=regrouped.at[lax.rem(me + layer_count - step, layer_count)],
            send_sem=piece_send.at[step],
            recv_sem=piece_recv.at[step],
            device_id=(lax.rem(me + step, layer_count), row),
            device_id_type=MESH,
        )
        copy.wait_send()
        copy.wait_recv()
        return carry

    lax.fori_loop(1, layer_count, arrived, 0)


def front_exchange(block, coef, depth, decay_rates):
    row_count = lax.axis_size("xs")
    layer_count = lax.axis_size("layer")
    layers, columns, width = block.shape
    data_rows = layers * width // 128
    padded_rows = -(-(data_rows + layers) // 8) * 8
    body = jnp.transpose(block, (1, 0, 2)).reshape(columns, data_rows, 128)
    lanes = jnp.broadcast_to(jnp.transpose(decay_rates)[:, :, None], (columns, layers, 128))
    spare = jnp.zeros((columns, padded_rows - data_rows - layers, 128), jnp.float32)
    pieces = jnp.concatenate([body, lanes, spare], axis=1)
    spec = pl.BlockSpec(memory_space=pltpu.VMEM)
    return pl.pallas_call(
        functools.partial(front_kernel, row_count, layer_count, depth),
        out_shape=[jax.ShapeDtypeStruct(block.shape, jnp.float32)]
        + [jax.ShapeDtypeStruct(coef.shape, jnp.float32),
           jax.ShapeDtypeStruct((layer_count,) + pieces.shape[1:], jnp.float32)],
        in_specs=[spec, spec, spec],
        out_specs=[spec] * 3,
        scratch_shapes=[
            pltpu.VMEM(block.shape, jnp.float32),
            pltpu.VMEM(block.shape, jnp.float32),
            pltpu.VMEM((row_count - 1,) + coef.shape, jnp.float32),
            pltpu.SemaphoreType.DMA((1 + row_count,)),
            pltpu.SemaphoreType.DMA((1 + row_count,)),
            pltpu.SemaphoreType.DMA((layer_count,)),
            pltpu.SemaphoreType.DMA((layer_count,)),
        ],
        compiler_params=pltpu.CompilerParams(collective_id=1, has_side_effects=True),
    )(block, coef, pieces)


def shards(
    probes,
    potential,
    projector,
    intersection_ids,
    strength,
    decay_rates,
    contour_nodes,
    node_weights,
):
    layers, columns, rows, depth = probes.shape
    flat = probes.reshape(layers, columns, rows * depth)
    rounded = flat.astype(jnp.bfloat16)
    slot_coef = jnp.einsum("lsp,lcp->lsc", projector, rounded, preferred_element_type=jnp.float32)
    onehot = (intersection_ids[:, :, None] == jnp.arange(NPROJ, dtype=jnp.int32)).astype(
        jnp.float32
    )
    partial_coef = jnp.einsum("lsq,lsc->lcq", onehot, slot_coef, precision=lax.Precision.HIGHEST)
    if rows != 2:
        raise ValueError("rows")
    along_rows, coef, regrouped = front_exchange(flat, partial_coef, depth, decay_rates)
    laplace = along_rows + second_along_flat(flat, depth)
    coef = jnp.swapaxes(coef, 1, 2)
    scaled = (strength[:, :, None] * coef).astype(jnp.bfloat16)
    slot_back = jnp.einsum(
        "lsq,lqc->lsc", onehot.astype(jnp.bfloat16), scaled, preferred_element_type=jnp.float32
    ).astype(jnp.bfloat16)
    projected = jnp.einsum(
        "lsp,lsc->lcp", projector, slot_back, preferred_element_type=jnp.float32
    )
    partial = -0.5 * laplace + potential.reshape(layers, 1, rows * depth) * flat + projected
    swept = sweeps(
        partial, regrouped, decay_rates, contour_nodes,
        node_weights,
    )
    return swept.reshape(2, layers, columns, rows, depth)


def solution(mesh):
    in_specs = (
        P("layer", None, "xs", None),
        P("layer", "xs", None),
        P("layer", "xs", None),
        P("layer", "xs"),
        P("layer", None),
        P("layer", None),
        P(),
        P(),
    )
    out_specs = P(None, "layer", None, "xs", None)
    return jax.shard_map(shards, mesh=mesh, in_specs=in_specs, out_specs=out_specs, check_vma=False)
```

```python
import functools

import jax
import jax.numpy as jnp
from jax import lax
from jax.experimental import pallas as pl
from jax.experimental.pallas import tpu as pltpu
from jax.sharding import PartitionSpec as P

NPROJ = 256


FAR = -1.0 / 12.0
NEAR = 4.0 / 3.0
CENTER = -2.5


def with_halo(cells, sides, width):
    for axis, dim in sides:
        count = lax.axis_size(axis)
        ends = count - 1
        head = lax.slice_in_dim(cells, 0, width, axis=dim)
        tail = lax.slice_in_dim(cells, cells.shape[dim] - width, cells.shape[dim], axis=dim)
        cells = jnp.concatenate(
            [
                lax.ppermute(tail, axis, [(i, (i + 1) % count) for i in range(ends)]),
                cells,
                lax.ppermute(head, axis, [((i + 1) % count, i) for i in range(ends)]),
            ],
            axis=dim,
        )
    return cells


def second_along_flat(flat, depth):
    width = flat.shape[-1]
    padded = jnp.pad(flat, [(0, 0)] * (flat.ndim - 1) + [(2, 2)])
    spot = lax.broadcasted_iota(jnp.int32, (width,), 0) % depth

    def piece(offset):
        shifted = lax.slice_in_dim(padded, 2 + offset, 2 + offset + width, axis=flat.ndim - 1)
        if offset == 0:
            return shifted
        inside = (spot + offset >= 0) & (spot + offset < depth)
        return jnp.where(inside, shifted, 0.0)

    return FAR * (piece(-2) + piece(2)) + NEAR * (piece(-1) + piece(1)) + CENTER * piece(0)


def second_along(padded, axis, count):

    def piece(offset):
        return lax.slice_in_dim(padded, 2 + offset, 2 + offset + count, axis=axis)

    return FAR * (piece(-2) + piece(2)) + NEAR * (piece(-1) + piece(1)) + CENTER * piece(0)


MESH = pl.DeviceIdType.MESH


def spans_of(count):
    spans = []
    span = 1
    while 2 * span < count:
        spans.append(span)
        span *= 2
    return spans, span + 1


def sweep_kernel(count, f_ref, d_ref, o_ref, state, landed, send_sem, recv_sem):
    me = lax.axis_index("layer")
    row = lax.axis_index("xs")
    layers = f_ref.shape[1]
    width = f_ref.shape[3]
    spans, far = spans_of(count)
    hops = spans + [1, far]
    barrier = pltpu.get_barrier_semaphore()
    for hop in hops:
        for sign in (1, -1):
            pl.semaphore_signal(
                barrier, inc=1, device_id=(lax.rem(me + sign * hop + count, count), row),
                device_id_type=MESH,
            )
    pl.semaphore_wait(barrier, 2 * len(hops))

    rates = [d_ref[index] for index in range(layers)]
    through = rates[0]
    for index in range(1, layers):
        through = through * rates[index]

    def put(direction, slot, ends, keep):
        state[direction, slot, :, :, :width] = ends
        state[direction, slot, :, :, width:] = jnp.broadcast_to(keep[None], (2,) + keep.shape[:1] + (128,))

    def send(direction, slot, target_slot, hop, sign):
        copy = pltpu.make_async_remote_copy(
            src_ref=state.at[direction, slot],
            dst_ref=landed.at[direction, target_slot],
            send_sem=send_sem.at[direction, target_slot],
            recv_sem=recv_sem.at[direction, target_slot],
            device_id=(lax.rem(me + sign * hop + count, count), row),
            device_id_type=MESH,
        )
        copy.start()
        return copy

    def scan(direction, ends, sign):
        put(direction, 0, ends, through)
        for slot, hop in enumerate(spans):
            send(direction, slot, slot, hop, sign).wait()
            source = me - hop if sign == 1 else me + hop
            valid = ((source >= 0) & (source < count)).astype(jnp.float32)
            mine = state[direction, slot]
            got = landed[direction, slot]
            keep = mine[0, :, width:width + 1]
            put(
                direction, slot + 1,
                mine[:, :, :width] + (valid * keep)[None] * got[:, :, :width],
                keep * (valid * got[0, :, width:width + 1]),
            )
        last = len(spans)
        near = send(direction, last, last, 1, sign)
        distant = send(direction, last, last + 1, far, sign)
        near.wait()
        distant.wait()
        near_source = me - 1 if sign == 1 else me + 1
        far_source = me - far if sign == 1 else me + far
        near_valid = ((near_source >= 0) & (near_source < count)).astype(jnp.float32)
        far_valid = ((far_source >= 0) & (far_source < count)).astype(jnp.float32)
        got = landed[direction, last]
        result = got[:, :, :width]
        if far < count:
            result = result + (far_valid * got[0, :, width:width + 1])[None] * landed[direction, last + 1, :, :, :width]
        return near_valid * result

    state_now = None
    ahead = []
    for index in range(layers):
        source = f_ref[:, index]
        if state_now is None:
            state_now = (1.0 - rates[index])[None] * source
        else:
            state_now = rates[index][None] * state_now + (1.0 - rates[index])[None] * source
        ahead.append(state_now)
    entering = scan(0, state_now, 1)
    lower = rates[0]
    for index in range(layers):
        if index > 0:
            lower = lower * rates[index]
        ahead[index] = ahead[index] + lower[None] * entering
    state_now = None
    back = [None] * layers
    for index in reversed(range(layers)):
        if state_now is None:
            state_now = (1.0 - rates[index])[None] * ahead[index]
        else:
            state_now = rates[index][None] * state_now + (1.0 - rates[index])[None] * ahead[index]
        back[index] = state_now
    from_above = scan(1, state_now, -1)
    upper = rates[layers - 1]
    for index in reversed(range(layers)):
        if index < layers - 1:
            upper = upper * rates[index]
        o_ref[:, index] = back[index] + upper[None] * from_above


def exchange_kernel(count, layer_count, nodes_ref, weights_ref, ext_ref, probe_ref, out_ref, gathered, swept, send_sem, recv_sem, back_send, back_recv):
    me = lax.axis_index("layer")
    row = lax.axis_index("xs")
    layers = layer_count
    barrier = pltpu.get_barrier_semaphore()

    def greet(step, carry):
        pl.semaphore_signal(
            barrier, inc=1, device_id=(lax.rem(me + step, count), row), device_id_type=MESH
        )
        return carry

    lax.fori_loop(1, count, greet, 0)
    pl.semaphore_wait(barrier, count - 1)

    def outgoing(step, carry):
        target = lax.rem(me + step, count)
        pltpu.make_async_remote_copy(
            src_ref=ext_ref.at[target],
            dst_ref=gathered.at[me],
            send_sem=send_sem.at[step],
            recv_sem=recv_sem.at[step],
            device_id=(target, row),
            device_id_type=MESH,
        ).start()
        return carry

    lax.fori_loop(1, count, outgoing, 0)
    gathered[me] = ext_ref[me]

    def arrived(step, carry):
        copy = pltpu.make_async_remote_copy(
            src_ref=ext_ref.at[me],
            dst_ref=gathered.at[lax.rem(me + count - step, count)],
            send_sem=send_sem.at[step],
            recv_sem=recv_sem.at[step],
            device_id=(lax.rem(me + step, count), row),
            device_id_type=MESH,
        )
        copy.wait_send()
        copy.wait_recv()
        return carry

    lax.fori_loop(1, count, arrived, 0)

    half = out_ref.shape[3]
    rows_per_layer = 2 * half
    zero = jnp.zeros((half, out_ref.shape[4]), jnp.float32)
    data_rows = layers * half
    total = count * layers
    w0 = w1 = w2 = None
    for node in range(nodes_ref.shape[0]):
        weight = weights_ref[node]
        scaled = weight * nodes_ref[node]
        if w0 is None:
            w0, w1, w2 = weight, scaled, scaled * nodes_ref[node]
        else:
            w0, w1, w2 = w0 + weight, w1 + scaled, w2 + scaled * nodes_ref[node]

    def probe_at(place):
        inside = ((place >= 0) & (place < total)).astype(jnp.float32)
        place = jnp.clip(place, 0, total - 1)
        source = place // layers
        layer = place - source * layers
        return inside * probe_ref[source, pl.ds(layer * half, half), :]

    def forward(source, state):
        for layer in range(layers):
            place = source * layers + layer
            here = probe_ref[source, pl.ds(layer * half, half), :]
            partial = gathered[source, pl.ds(layer * half, half), :]
            def near(offset):
                if 0 <= layer + offset < layers:
                    return probe_ref[source, pl.ds((layer + offset) * half, half), :]
                return probe_at(place + offset)

            second = (
                FAR * (near(-2) + near(2))
                + NEAR * (near(-1) + near(1))
                + CENTER * here
            )
            hamil = partial - 0.5 * second
            forcing = (w0 * hamil - w1 * here, w1 * hamil - w2 * here)
            rate = probe_ref[source, pl.ds(data_rows + layer, 1), :]
            state = tuple(rate * state[m] + (1.0 - rate) * forcing[m] for m in range(2))
            for m in range(2):
                swept[source, m, layer] = state[m]
        return state

    lax.fori_loop(0, count, forward, (zero, zero))

    def backward(step, state):
        source = count - 1 - step
        for layer in reversed(range(layers)):
            rate = probe_ref[source, pl.ds(data_rows + layer, 1), :]
            state = tuple(
                rate * state[m] + (1.0 - rate) * swept[source, m, layer] for m in range(2)
            )
            for m in range(2):
                swept[source, m, layer] = state[m]

        @pl.when(source != me)
        def _():
            pltpu.make_async_remote_copy(
                src_ref=swept.at[source],
                dst_ref=out_ref.at[:, :, me],
                send_sem=back_send.at[lax.rem(source - me + count, count)],
                recv_sem=back_recv.at[lax.rem(source - me + count, count)],
                device_id=(source, row),
                device_id_type=MESH,
            ).start()

        return state

    lax.fori_loop(0, count, backward, (zero, zero))
    out_ref[:, :, me] = swept[me]

    def returned(step, carry):
        copy = pltpu.make_async_remote_copy(
            src_ref=swept.at[me],
            dst_ref=out_ref.at[:, :, lax.rem(me + count - step, count)],
            send_sem=back_send.at[step],
            recv_sem=back_recv.at[step],
            device_id=(lax.rem(me + step, count), row),
            device_id_type=MESH,
        )
        copy.wait_send()
        copy.wait_recv()
        return carry

    lax.fori_loop(1, count, returned, 0)


def sweeps(partial, gathered_probes, decay_rates, nodes, weights):
    layers, columns, width = partial.shape
    moments = 2
    count = lax.axis_size("layer")
    if columns != count:
        raise ValueError("columns")
    tiles = width // 128
    data_rows = layers * tiles
    ext = jnp.transpose(partial, (1, 0, 2)).reshape(columns, data_rows, 128)
    vmem = pl.BlockSpec(memory_space=pltpu.VMEM)
    out = pl.pallas_call(
        functools.partial(exchange_kernel, count, layers),
        out_shape=jax.ShapeDtypeStruct((moments, layers, columns, tiles, 128), jnp.float32),
        in_specs=[pl.BlockSpec(memory_space=pltpu.SMEM)] * 2 + [vmem, vmem],
        out_specs=vmem,
        scratch_shapes=[
            pltpu.VMEM((count, data_rows, 128), jnp.float32),
            pltpu.VMEM((count, moments, layers, tiles, 128), jnp.float32),
            pltpu.SemaphoreType.DMA((count,)),
            pltpu.SemaphoreType.DMA((count,)),
            pltpu.SemaphoreType.DMA((count,)),
            pltpu.SemaphoreType.DMA((count,)),
        ],
        compiler_params=pltpu.CompilerParams(collective_id=0, has_side_effects=True),
    )(nodes, weights, ext, gathered_probes)
    return out.reshape(moments, layers, columns, width)


def front_kernel(row_count, layer_count, depth, block_ref, coef_ref, pieces_ref, across, total, regrouped,
                 left, right, gathered, send_sem, recv_sem, piece_send, piece_recv):
    me = lax.axis_index("layer")
    row = lax.axis_index("xs")
    peers = row_count - 1
    barrier = pltpu.get_barrier_semaphore()
    for step in range(1, row_count):
        pl.semaphore_signal(
            barrier, inc=1, device_id=(me, lax.rem(row + step, row_count)), device_id_type=MESH
        )

    def greet(step, carry):
        pl.semaphore_signal(
            barrier, inc=1, device_id=(lax.rem(me + step, layer_count), row), device_id_type=MESH
        )
        return carry

    lax.fori_loop(1, layer_count, greet, 0)
    pl.semaphore_wait(barrier, peers + layer_count - 1)

    def outgoing(step, carry):
        target = lax.rem(me + step, layer_count)
        pltpu.make_async_remote_copy(
            src_ref=pieces_ref.at[target],
            dst_ref=regrouped.at[me],
            send_sem=piece_send.at[step],
            recv_sem=piece_recv.at[step],
            device_id=(target, row),
            device_id_type=MESH,
        ).start()
        return carry

    copies = []
    targets = [
        (left, (me, lax.rem(row + 1, row_count))),
        (right, (me, lax.rem(row + row_count - 1, row_count))),
    ]
    for slot, (dst, device) in enumerate(targets):
        copies.append(
            pltpu.make_async_remote_copy(
                src_ref=block_ref, dst_ref=dst, send_sem=send_sem.at[slot], recv_sem=recv_sem.at[slot],
                device_id=device, device_id_type=MESH,
            )
        )
    for step in range(1, row_count):
        copies.append(
            pltpu.make_async_remote_copy(
                src_ref=coef_ref, dst_ref=gathered.at[step - 1], send_sem=send_sem.at[1 + step],
                recv_sem=recv_sem.at[1 + step], device_id=(me, lax.rem(row + step, row_count)),
                device_id_type=MESH,
            )
        )
    for copy in copies:
        copy.start()
    lax.fori_loop(1, layer_count, outgoing, 0)
    regrouped[me] = pieces_ref[me]
    for copy in copies[2:]:
        copy.wait()
    acc = coef_ref[...]
    for step in range(peers):
        acc = acc + gathered[step]
    total[...] = acc
    for copy in copies[:2]:
        copy.wait()
    before = left[...] * (row > 0).astype(jnp.float32)
    after = right[...] * (row < row_count - 1).astype(jnp.float32)
    mine = block_ref[...]
    first, second = slice(0, depth), slice(depth, 2 * depth)
    across[:, :, first] = (
        FAR * (before[:, :, first] + after[:, :, first])
        + NEAR * (before[:, :, second] + mine[:, :, second])
        + CENTER * mine[:, :, first]
    )
    across[:, :, second] = (
        FAR * (before[:, :, second] + after[:, :, second])
        + NEAR * (mine[:, :, first] + after[:, :, first])
        + CENTER * mine[:, :, second]
    )

    def arrived(step, carry):
        copy = pltpu.make_async_remote_copy(
            src_ref=pieces_ref.at[me],
            dst_ref=regrouped.at[lax.rem(me + layer_count - step, layer_count)],
            send_sem=piece_send.at[step],
            recv_sem=piece_recv.at[step],
            device_id=(lax.rem(me + step, layer_count), row),
            device_id_type=MESH,
        )
        copy.wait_send()
        copy.wait_recv()
        return carry

    lax.fori_loop(1, layer_count, arrived, 0)


def front_exchange(block, coef, depth, decay_rates):
    row_count = lax.axis_size("xs")
    layer_count = lax.axis_size("layer")
    layers, columns, width = block.shape
    data_rows = layers * width // 128
    padded_rows = -(-(data_rows + layers) // 8) * 8
    body = jnp.transpose(block, (1, 0, 2)).reshape(columns, data_rows, 128)
    lanes = jnp.broadcast_to(jnp.transpose(decay_rates)[:, :, None], (columns, layers, 128))
    spare = jnp.zeros((columns, padded_rows - data_rows - layers, 128), jnp.float32)
    pieces = jnp.concatenate([body, lanes, spare], axis=1)
    spec = pl.BlockSpec(memory_space=pltpu.VMEM)
    return pl.pallas_call(
        functools.partial(front_kernel, row_count, layer_count, depth),
        out_shape=[jax.ShapeDtypeStruct(block.shape, jnp.float32)]
        + [jax.ShapeDtypeStruct(coef.shape, jnp.float32),
           jax.ShapeDtypeStruct((layer_count,) + pieces.shape[1:], jnp.float32)],
        in_specs=[spec, spec, spec],
        out_specs=[spec] * 3,
        scratch_shapes=[
            pltpu.VMEM(block.shape, jnp.float32),
            pltpu.VMEM(block.shape, jnp.float32),
            pltpu.VMEM((row_count - 1,) + coef.shape, jnp.float32),
            pltpu.SemaphoreType.DMA((1 + row_count,)),
            pltpu.SemaphoreType.DMA((1 + row_count,)),
            pltpu.SemaphoreType.DMA((layer_count,)),
            pltpu.SemaphoreType.DMA((layer_count,)),
        ],
        compiler_params=pltpu.CompilerParams(collective_id=1, has_side_effects=True),
    )(block, coef, pieces)


def shards(
    probes,
    potential,
    projector,
    intersection_ids,
    strength,
    decay_rates,
    contour_nodes,
    node_weights,
):
    layers, columns, rows, depth = probes.shape
    flat = probes.reshape(layers, columns, rows * depth)
    rounded = flat.astype(jnp.bfloat16)
    slot_coef = jnp.einsum("lsp,lcp->lsc", projector, rounded, preferred_element_type=jnp.float32)
    onehot = (intersection_ids[:, :, None] == jnp.arange(NPROJ, dtype=jnp.int32)).astype(
        jnp.float32
    )
    partial_coef = jnp.einsum("lsq,lsc->lcq", onehot, slot_coef, precision=lax.Precision.HIGHEST)
    if rows != 2:
        raise ValueError("rows")
    along_rows, coef, regrouped = front_exchange(flat, partial_coef, depth, decay_rates)
    laplace = along_rows + second_along_flat(flat, depth)
    coef = jnp.swapaxes(coef, 1, 2)
    scaled = (strength[:, :, None] * coef).astype(jnp.bfloat16)
    slot_back = jnp.einsum(
        "lsq,lqc->lsc", onehot.astype(jnp.bfloat16), scaled, preferred_element_type=jnp.float32
    ).astype(jnp.bfloat16)
    projected = jnp.einsum(
        "lsp,lsc->lcp", projector, slot_back, preferred_element_type=jnp.float32
    )
    partial = -0.5 * laplace + potential.reshape(layers, 1, rows * depth) * flat + projected
    swept = sweeps(
        partial, regrouped, decay_rates, contour_nodes,
        node_weights,
    )
    return swept.reshape(2, layers, columns, rows, depth)


def solution(mesh):
    in_specs = (
        P("layer", None, "xs", None),
        P("layer", "xs", None),
        P("layer", "xs", None),
        P("layer", "xs"),
        P("layer", None),
        P("layer", None),
        P(),
        P(),
    )
    out_specs = P(None, "layer", None, "xs", None)
    return jax.shard_map(shards, mesh=mesh, in_specs=in_specs, out_specs=out_specs, check_vma=False)
```

```python
import functools

import jax
import jax.numpy as jnp
from jax import lax
from jax.experimental import pallas as pl
from jax.experimental.pallas import tpu as pltpu
from jax.sharding import PartitionSpec as P

NPROJ = 256


FAR = -1.0 / 12.0
NEAR = 4.0 / 3.0
CENTER = -2.5


def with_halo(cells, sides, width):
    for axis, dim in sides:
        count = lax.axis_size(axis)
        ends = count - 1
        head = lax.slice_in_dim(cells, 0, width, axis=dim)
        tail = lax.slice_in_dim(cells, cells.shape[dim] - width, cells.shape[dim], axis=dim)
        cells = jnp.concatenate(
            [
                lax.ppermute(tail, axis, [(i, (i + 1) % count) for i in range(ends)]),
                cells,
                lax.ppermute(head, axis, [((i + 1) % count, i) for i in range(ends)]),
            ],
            axis=dim,
        )
    return cells


def second_along_flat(flat, depth):
    width = flat.shape[-1]
    padded = jnp.pad(flat, [(0, 0)] * (flat.ndim - 1) + [(2, 2)])
    spot = lax.broadcasted_iota(jnp.int32, (width,), 0) % depth

    def piece(offset):
        shifted = lax.slice_in_dim(padded, 2 + offset, 2 + offset + width, axis=flat.ndim - 1)
        if offset == 0:
            return shifted
        inside = (spot + offset >= 0) & (spot + offset < depth)
        return jnp.where(inside, shifted, 0.0)

    return FAR * (piece(-2) + piece(2)) + NEAR * (piece(-1) + piece(1)) + CENTER * piece(0)


def second_along(padded, axis, count):

    def piece(offset):
        return lax.slice_in_dim(padded, 2 + offset, 2 + offset + count, axis=axis)

    return FAR * (piece(-2) + piece(2)) + NEAR * (piece(-1) + piece(1)) + CENTER * piece(0)


MESH = pl.DeviceIdType.MESH


def spans_of(count):
    spans = []
    span = 1
    while 2 * span < count:
        spans.append(span)
        span *= 2
    return spans, span + 1


def sweep_kernel(count, f_ref, d_ref, o_ref, state, landed, send_sem, recv_sem):
    me = lax.axis_index("layer")
    row = lax.axis_index("xs")
    layers = f_ref.shape[1]
    width = f_ref.shape[3]
    spans, far = spans_of(count)
    hops = spans + [1, far]
    barrier = pltpu.get_barrier_semaphore()
    for hop in hops:
        for sign in (1, -1):
            pl.semaphore_signal(
                barrier, inc=1, device_id=(lax.rem(me + sign * hop + count, count), row),
                device_id_type=MESH,
            )
    pl.semaphore_wait(barrier, 2 * len(hops))

    rates = [d_ref[index] for index in range(layers)]
    through = rates[0]
    for index in range(1, layers):
        through = through * rates[index]

    def put(direction, slot, ends, keep):
        state[direction, slot, :, :, :width] = ends
        state[direction, slot, :, :, width:] = jnp.broadcast_to(keep[None], (2,) + keep.shape[:1] + (128,))

    def send(direction, slot, target_slot, hop, sign):
        copy = pltpu.make_async_remote_copy(
            src_ref=state.at[direction, slot],
            dst_ref=landed.at[direction, target_slot],
            send_sem=send_sem.at[direction, target_slot],
            recv_sem=recv_sem.at[direction, target_slot],
            device_id=(lax.rem(me + sign * hop + count, count), row),
            device_id_type=MESH,
        )
        copy.start()
        return copy

    def scan(direction, ends, sign):
        put(direction, 0, ends, through)
        for slot, hop in enumerate(spans):
            send(direction, slot, slot, hop, sign).wait()
            source = me - hop if sign == 1 else me + hop
            valid = ((source >= 0) & (source < count)).astype(jnp.float32)
            mine = state[direction, slot]
            got = landed[direction, slot]
            keep = mine[0, :, width:width + 1]
            put(
                direction, slot + 1,
                mine[:, :, :width] + (valid * keep)[None] * got[:, :, :width],
                keep * (valid * got[0, :, width:width + 1]),
            )
        last = len(spans)
        near = send(direction, last, last, 1, sign)
        distant = send(direction, last, last + 1, far, sign)
        near.wait()
        distant.wait()
        near_source = me - 1 if sign == 1 else me + 1
        far_source = me - far if sign == 1 else me + far
        near_valid = ((near_source >= 0) & (near_source < count)).astype(jnp.float32)
        far_valid = ((far_source >= 0) & (far_source < count)).astype(jnp.float32)
        got = landed[direction, last]
        result = got[:, :, :width]
        if far < count:
            result = result + (far_valid * got[0, :, width:width + 1])[None] * landed[direction, last + 1, :, :, :width]
        return near_valid * result

    state_now = None
    ahead = []
    for index in range(layers):
        source = f_ref[:, index]
        if state_now is None:
            state_now = (1.0 - rates[index])[None] * source
        else:
            state_now = rates[index][None] * state_now + (1.0 - rates[index])[None] * source
        ahead.append(state_now)
    entering = scan(0, state_now, 1)
    lower = rates[0]
    for index in range(layers):
        if index > 0:
            lower = lower * rates[index]
        ahead[index] = ahead[index] + lower[None] * entering
    state_now = None
    back = [None] * layers
    for index in reversed(range(layers)):
        if state_now is None:
            state_now = (1.0 - rates[index])[None] * ahead[index]
        else:
            state_now = rates[index][None] * state_now + (1.0 - rates[index])[None] * ahead[index]
        back[index] = state_now
    from_above = scan(1, state_now, -1)
    upper = rates[layers - 1]
    for index in reversed(range(layers)):
        if index < layers - 1:
            upper = upper * rates[index]
        o_ref[:, index] = back[index] + upper[None] * from_above


def exchange_kernel(count, layer_count, nodes_ref, weights_ref, ext_ref, probe_ref, out_ref, gathered, swept, send_sem, recv_sem, back_send, back_recv):
    me = lax.axis_index("layer")
    row = lax.axis_index("xs")
    layers = layer_count
    def offset(step):
        return ((step + 1) // 2) * (1 - 2 * ((step + 1) % 2))

    barrier = pltpu.get_barrier_semaphore()

    def greet(step, carry):
        pl.semaphore_signal(
            barrier, inc=1, device_id=(lax.rem(me + offset(step) + count, count), row), device_id_type=MESH
        )
        return carry

    lax.fori_loop(1, count, greet, 0)
    pl.semaphore_wait(barrier, count - 1)

    def outgoing(step, carry):
        target = lax.rem(me + offset(step) + count, count)
        pltpu.make_async_remote_copy(
            src_ref=ext_ref.at[target],
            dst_ref=gathered.at[me],
            send_sem=send_sem.at[step],
            recv_sem=recv_sem.at[step],
            device_id=(target, row),
            device_id_type=MESH,
        ).start()
        return carry

    lax.fori_loop(1, count, outgoing, 0)
    gathered[me] = ext_ref[me]

    def arrived(step, carry):
        copy = pltpu.make_async_remote_copy(
            src_ref=ext_ref.at[me],
            dst_ref=gathered.at[lax.rem(me + count - offset(step), count)],
            send_sem=send_sem.at[step],
            recv_sem=recv_sem.at[step],
            device_id=(lax.rem(me + offset(step) + count, count), row),
            device_id_type=MESH,
        )
        copy.wait_send()
        copy.wait_recv()
        return carry

    lax.fori_loop(1, count, arrived, 0)

    half = out_ref.shape[3]
    rows_per_layer = 2 * half
    zero = jnp.zeros((half, out_ref.shape[4]), jnp.float32)
    data_rows = layers * half
    total = count * layers
    w0 = w1 = w2 = None
    for node in range(nodes_ref.shape[0]):
        weight = weights_ref[node]
        scaled = weight * nodes_ref[node]
        if w0 is None:
            w0, w1, w2 = weight, scaled, scaled * nodes_ref[node]
        else:
            w0, w1, w2 = w0 + weight, w1 + scaled, w2 + scaled * nodes_ref[node]

    def probe_at(place):
        inside = ((place >= 0) & (place < total)).astype(jnp.float32)
        place = jnp.clip(place, 0, total - 1)
        source = place // layers
        layer = place - source * layers
        return inside * probe_ref[source, pl.ds(layer * half, half), :]

    def forward(source, state):
        for layer in range(layers):
            place = source * layers + layer
            here = probe_ref[source, pl.ds(layer * half, half), :]
            partial = gathered[source, pl.ds(layer * half, half), :]
            def near(offset):
                if 0 <= layer + offset < layers:
                    return probe_ref[source, pl.ds((layer + offset) * half, half), :]
                return probe_at(place + offset)

            second = (
                FAR * (near(-2) + near(2))
                + NEAR * (near(-1) + near(1))
                + CENTER * here
            )
            hamil = partial - 0.5 * second
            forcing = (w0 * hamil - w1 * here, w1 * hamil - w2 * here)
            rate = probe_ref[source, pl.ds(data_rows + layer, 1), :]
            state = tuple(rate * state[m] + (1.0 - rate) * forcing[m] for m in range(2))
            for m in range(2):
                swept[source, m, layer] = state[m]
        return state

    lax.fori_loop(0, count, forward, (zero, zero))

    def backward(step, state):
        source = count - 1 - step
        for layer in reversed(range(layers)):
            rate = probe_ref[source, pl.ds(data_rows + layer, 1), :]
            state = tuple(
                rate * state[m] + (1.0 - rate) * swept[source, m, layer] for m in range(2)
            )
            for m in range(2):
                swept[source, m, layer] = state[m]
        return state

    lax.fori_loop(0, count, backward, (zero, zero))

    def returning(step, carry):
        target = lax.rem(me + offset(step) + count, count)
        pltpu.make_async_remote_copy(
            src_ref=swept.at[target],
            dst_ref=out_ref.at[:, :, me],
            send_sem=back_send.at[step],
            recv_sem=back_recv.at[step],
            device_id=(target, row),
            device_id_type=MESH,
        ).start()
        return carry

    lax.fori_loop(1, count, returning, 0)
    out_ref[:, :, me] = swept[me]

    def returned(step, carry):
        copy = pltpu.make_async_remote_copy(
            src_ref=swept.at[me],
            dst_ref=out_ref.at[:, :, lax.rem(me + count - offset(step), count)],
            send_sem=back_send.at[step],
            recv_sem=back_recv.at[step],
            device_id=(lax.rem(me + offset(step) + count, count), row),
            device_id_type=MESH,
        )
        copy.wait_send()
        copy.wait_recv()
        return carry

    lax.fori_loop(1, count, returned, 0)


def sweeps(partial, gathered_probes, decay_rates, nodes, weights):
    layers, columns, width = partial.shape
    moments = 2
    count = lax.axis_size("layer")
    if columns != count:
        raise ValueError("columns")
    tiles = width // 128
    data_rows = layers * tiles
    ext = jnp.transpose(partial, (1, 0, 2)).reshape(columns, data_rows, 128)
    vmem = pl.BlockSpec(memory_space=pltpu.VMEM)
    out = pl.pallas_call(
        functools.partial(exchange_kernel, count, layers),
        out_shape=jax.ShapeDtypeStruct((moments, layers, columns, tiles, 128), jnp.float32),
        in_specs=[pl.BlockSpec(memory_space=pltpu.SMEM)] * 2 + [vmem, vmem],
        out_specs=vmem,
        scratch_shapes=[
            pltpu.VMEM((count, data_rows, 128), jnp.float32),
            pltpu.VMEM((count, moments, layers, tiles, 128), jnp.float32),
            pltpu.SemaphoreType.DMA((count,)),
            pltpu.SemaphoreType.DMA((count,)),
            pltpu.SemaphoreType.DMA((count,)),
            pltpu.SemaphoreType.DMA((count,)),
        ],
        compiler_params=pltpu.CompilerParams(collective_id=0, has_side_effects=True),
    )(nodes, weights, ext, gathered_probes)
    return out.reshape(moments, layers, columns, width)


def front_kernel(row_count, layer_count, depth, block_ref, coef_ref, pieces_ref, across, total, regrouped,
                 left, right, gathered, send_sem, recv_sem, piece_send, piece_recv):
    me = lax.axis_index("layer")
    row = lax.axis_index("xs")
    peers = row_count - 1
    barrier = pltpu.get_barrier_semaphore()
    for step in range(1, row_count):
        pl.semaphore_signal(
            barrier, inc=1, device_id=(me, lax.rem(row + step, row_count)), device_id_type=MESH
        )

    def greet(step, carry):
        pl.semaphore_signal(
            barrier, inc=1, device_id=(lax.rem(me + step, layer_count), row), device_id_type=MESH
        )
        return carry

    lax.fori_loop(1, layer_count, greet, 0)
    pl.semaphore_wait(barrier, peers + layer_count - 1)

    def outgoing(step, carry):
        target = lax.rem(me + step, layer_count)
        pltpu.make_async_remote_copy(
            src_ref=pieces_ref.at[target],
            dst_ref=regrouped.at[me],
            send_sem=piece_send.at[step],
            recv_sem=piece_recv.at[step],
            device_id=(target, row),
            device_id_type=MESH,
        ).start()
        return carry

    copies = []
    targets = [
        (left, (me, lax.rem(row + 1, row_count))),
        (right, (me, lax.rem(row + row_count - 1, row_count))),
    ]
    for slot, (dst, device) in enumerate(targets):
        copies.append(
            pltpu.make_async_remote_copy(
                src_ref=block_ref, dst_ref=dst, send_sem=send_sem.at[slot], recv_sem=recv_sem.at[slot],
                device_id=device, device_id_type=MESH,
            )
        )
    for step in range(1, row_count):
        copies.append(
            pltpu.make_async_remote_copy(
                src_ref=coef_ref, dst_ref=gathered.at[step - 1], send_sem=send_sem.at[1 + step],
                recv_sem=recv_sem.at[1 + step], device_id=(me, lax.rem(row + step, row_count)),
                device_id_type=MESH,
            )
        )
    for copy in copies:
        copy.start()
    lax.fori_loop(1, layer_count, outgoing, 0)
    regrouped[me] = pieces_ref[me]
    for copy in copies[2:]:
        copy.wait()
    acc = coef_ref[...]
    for step in range(peers):
        acc = acc + gathered[step]
    total[...] = acc
    for copy in copies[:2]:
        copy.wait()
    before = left[...] * (row > 0).astype(jnp.float32)
    after = right[...] * (row < row_count - 1).astype(jnp.float32)
    mine = block_ref[...]
    first, second = slice(0, depth), slice(depth, 2 * depth)
    across[:, :, first] = (
        FAR * (before[:, :, first] + after[:, :, first])
        + NEAR * (before[:, :, second] + mine[:, :, second])
        + CENTER * mine[:, :, first]
    )
    across[:, :, second] = (
        FAR * (before[:, :, second] + after[:, :, second])
        + NEAR * (mine[:, :, first] + after[:, :, first])
        + CENTER * mine[:, :, second]
    )

    def arrived(step, carry):
        copy = pltpu.make_async_remote_copy(
            src_ref=pieces_ref.at[me],
            dst_ref=regrouped.at[lax.rem(me + layer_count - step, layer_count)],
            send_sem=piece_send.at[step],
            recv_sem=piece_recv.at[step],
            device_id=(lax.rem(me + step, layer_count), row),
            device_id_type=MESH,
        )
        copy.wait_send()
        copy.wait_recv()
        return carry

    lax.fori_loop(1, layer_count, arrived, 0)


def front_exchange(block, coef, depth, decay_rates):
    row_count = lax.axis_size("xs")
    layer_count = lax.axis_size("layer")
    layers, columns, width = block.shape
    data_rows = layers * width // 128
    padded_rows = -(-(data_rows + layers) // 8) * 8
    body = jnp.transpose(block, (1, 0, 2)).reshape(columns, data_rows, 128)
    lanes = jnp.broadcast_to(jnp.transpose(decay_rates)[:, :, None], (columns, layers, 128))
    spare = jnp.zeros((columns, padded_rows - data_rows - layers, 128), jnp.float32)
    pieces = jnp.concatenate([body, lanes, spare], axis=1)
    spec = pl.BlockSpec(memory_space=pltpu.VMEM)
    return pl.pallas_call(
        functools.partial(front_kernel, row_count, layer_count, depth),
        out_shape=[jax.ShapeDtypeStruct(block.shape, jnp.float32)]
        + [jax.ShapeDtypeStruct(coef.shape, jnp.float32),
           jax.ShapeDtypeStruct((layer_count,) + pieces.shape[1:], jnp.float32)],
        in_specs=[spec, spec, spec],
        out_specs=[spec] * 3,
        scratch_shapes=[
            pltpu.VMEM(block.shape, jnp.float32),
            pltpu.VMEM(block.shape, jnp.float32),
            pltpu.VMEM((row_count - 1,) + coef.shape, jnp.float32),
            pltpu.SemaphoreType.DMA((1 + row_count,)),
            pltpu.SemaphoreType.DMA((1 + row_count,)),
            pltpu.SemaphoreType.DMA((layer_count,)),
            pltpu.SemaphoreType.DMA((layer_count,)),
        ],
        compiler_params=pltpu.CompilerParams(collective_id=1, has_side_effects=True),
    )(block, coef, pieces)


def shards(
    probes,
    potential,
    projector,
    intersection_ids,
    strength,
    decay_rates,
    contour_nodes,
    node_weights,
):
    layers, columns, rows, depth = probes.shape
    flat = probes.reshape(layers, columns, rows * depth)
    rounded = flat.astype(jnp.bfloat16)
    slot_coef = jnp.einsum("lsp,lcp->lsc", projector, rounded, preferred_element_type=jnp.float32)
    onehot = (intersection_ids[:, :, None] == jnp.arange(NPROJ, dtype=jnp.int32)).astype(
        jnp.float32
    )
    partial_coef = jnp.einsum("lsq,lsc->lcq", onehot, slot_coef, precision=lax.Precision.HIGHEST)
    if rows != 2:
        raise ValueError("rows")
    along_rows, coef, regrouped = front_exchange(flat, partial_coef, depth, decay_rates)
    laplace = along_rows + second_along_flat(flat, depth)
    coef = jnp.swapaxes(coef, 1, 2)
    scaled = (strength[:, :, None] * coef).astype(jnp.bfloat16)
    slot_back = jnp.einsum(
        "lsq,lqc->lsc", onehot.astype(jnp.bfloat16), scaled, preferred_element_type=jnp.float32
    ).astype(jnp.bfloat16)
    projected = jnp.einsum(
        "lsp,lsc->lcp", projector, slot_back, preferred_element_type=jnp.float32
    )
    partial = -0.5 * laplace + potential.reshape(layers, 1, rows * depth) * flat + projected
    swept = sweeps(
        partial, regrouped, decay_rates, contour_nodes,
        node_weights,
    )
    return swept.reshape(2, layers, columns, rows, depth)


def solution(mesh):
    in_specs = (
        P("layer", None, "xs", None),
        P("layer", "xs", None),
        P("layer", "xs", None),
        P("layer", "xs"),
        P("layer", None),
        P("layer", None),
        P(),
        P(),
    )
    out_specs = P(None, "layer", None, "xs", None)
    return jax.shard_map(shards, mesh=mesh, in_specs=in_specs, out_specs=out_specs, check_vma=False)
```
